128 devices in a mesh: dom: 32 (over z, x, core), sub: 4 (over y).
Axes of the slice: x: 4, y: 4, z: 4, core: 2. Of those that a mesh axis runs over, the one named last changes fastest.
Arguments:
- position: float32 [3, 524288], P(None, ('dom', 'sub')), may hold values from -3 to 3
- smoothing: float32 [524288], P(('dom', 'sub')), may hold values from 0.7 to 1.4
- mass: float32 [524288], P(('dom', 'sub')), may hold values from 0.001 to 0.004
- energy: float32 [524288], P(('dom', 'sub')), may hold values from 0.5 to 2
- species: float32 [12, 524288], P(None, ('dom', 'sub')), may hold values from 0 to 1
- neighbours: int32 [4096, 4], P(('dom', 'sub')), may hold values from 0 to 31
- exports: int32 [1024, 2], P(('dom', 'sub')), may hold values from 0 to 31
- imports: int32 [2048, 2], P(('dom', 'sub')), may hold values from 0 to 31
- jac_inverse: float32 [12, 12], replicated
- rates: float32 [12, 12], replicated, may hold values from -1.75 to 1.75
- chem_steps: int32 [524288], P(('dom', 'sub')), may hold values from 1 to 32, as said below
- dense_slot: int32 [524288], P(('dom', 'sub')), may hold values from -1 to 2559, as said below
Outputs:
- density: float32 [524288], P(('dom', 'sub'))
- accel: float32 [3, 524288], P(None, ('dom', 'sub'))
- abundances: float32 [12, 524288], P(None, ('dom', 'sub'))
The draws below stay inside these ranges and needn't reach their ends.
Inputs may be any that keep to these rules, and one draw needn't show every extreme that they name: chem_steps is above 4 exactly on particles with dense_slot >= 0, at most 4 elsewhere. `dense_slot`: A value s below 1280 names slot s of this device's dense-clump buffer; 1280 + s names slot s of the buffer of the next device along dom (the last wraps to the first, same sub index). No two particles name the same slot of the same buffer.
All inputs are finite; a program needn't handle non-finite values.
Results may differ from the reference program's by a relative error of at most 0.0003.
Values sent between devices are 32-bit elements; how exact they have to be, the bound alone decides.
A program may use at most 64 MiB of HBM per device.

```python
import math
import jax
import jax.numpy as jnp
from jax import lax

NB_DEV = 32
BLOCK = 128
NBR_K = 4
EXP_SLOTS = 2
IMP_K = 2
SPECIES = 12
S_LO = 4
SMAX = 32
QUOTA = 256
RCAP = 1280
NP = 524288
N_DOM = 32
N_SUB = 4


def chem_layout(key):
    base = jax.random.fold_in(key, 4242)
    rows = NB_DEV * BLOCK
    devices = N_DOM * N_SUB

    def single(device):
        domain = device // N_SUB
        column = device % N_SUB
        offset = jax.random.randint(jax.random.fold_in(base, 900000 + column), (), 0, 4)
        phase = (domain + offset) % 4
        heavy = phase == 0
        after = phase == 1
        follower = (domain + 1) % N_DOM * N_SUB + column
        own_key = jax.random.fold_in(base, device)
        next_key = jax.random.fold_in(base, follower)
        own_perm = jax.random.permutation(jax.random.fold_in(own_key, 1), RCAP).astype(jnp.int32)
        next_perm = jax.random.permutation(jax.random.fold_in(next_key, 1), RCAP).astype(jnp.int32)
        row_perm = jax.random.permutation(jax.random.fold_in(own_key, 2), rows).astype(jnp.int32)
        ranking = jnp.argsort(row_perm, stable=True).astype(jnp.int32)
        light = jax.random.randint(jax.random.fold_in(own_key, 3), (), QUOTA // 2, QUOTA + 1)
        count = jnp.where(heavy, 8 * QUOTA, jnp.where(after, QUOTA, light))
        dense = ranking < count
        own_pos = jnp.where(after, 4 * QUOTA + ranking, ranking)
        own_code = own_perm[jnp.clip(own_pos, 0, RCAP - 1)]
        moved = RCAP + next_perm[jnp.clip(ranking - 4 * QUOTA, 0, RCAP - 1)]
        code = jnp.where(heavy & (ranking >= 4 * QUOTA), moved, own_code)
        slot = jnp.where(dense, code, -1)
        high = jax.random.randint(jax.random.fold_in(own_key, 4), (rows,), S_LO + 1, SMAX + 1)
        low = jax.random.randint(jax.random.fold_in(own_key, 5), (rows,), 1, S_LO + 1)
        steps = jnp.where(dense, high, low)
        steps = jnp.where(ranking == 0, SMAX, steps)
        return (steps.astype(jnp.int32), slot.astype(jnp.int32))
    steps, slots = jax.vmap(single)(jnp.arange(devices, dtype=jnp.int32))
    return (steps.reshape(-1), slots.reshape(-1))


def draw_chem_steps(key, part):
    return chem_layout(key)[0]


def draw_dense_slot(key, part):
    return chem_layout(key)[1]


def draw_jac_inverse(key, part):
    noise = jax.random.normal(jax.random.fold_in(key, 11), (SPECIES, SPECIES), jnp.float32)
    return 0.7 * jnp.eye(SPECIES, dtype=jnp.float32) + 0.25 * noise / jnp.sqrt(float(SPECIES))


def set_ends(drawn, key, smallest, largest):
    index_at = [jax.random.randint(jax.random.fold_in(key, axis), (), 0, length) for axis, length in enumerate(drawn.shape)]
    main_axis = drawn.shape.index(max(drawn.shape))
    beside = index_at[:main_axis] + [(index_at[main_axis] + 1) % drawn.shape[main_axis]] + index_at[main_axis + 1:]
    return drawn.at[tuple(index_at)].set(smallest).at[tuple(beside)].set(largest)


def level_of(key, dims, cuts, least, largest):
    factor_of = 1.0
    for dim, parts in cuts:
        steps = jax.random.uniform(jax.random.fold_in(jax.random.fold_in(key, 6), dim), (parts,), jnp.float32, least / len(cuts), largest / len(cuts))
        factor_of = factor_of * jnp.repeat(jnp.exp(steps), dims[dim] // parts).reshape((-1,) + (1,) * (len(dims) - 1 - dim))
    return factor_of


def gaussian(key, dims, width, most, cuts=(), held_as=jnp.bfloat16):
    factor_of = level_of(key, dims, cuts, -0.22, 0.18) if cuts else 1.0
    values = jax.random.normal(key, dims, jnp.float32) * width * factor_of
    return jnp.minimum(jnp.maximum(values, -most), most).astype(held_as)


def setup_inputs(seed: int = 0) -> dict:
    arg_keys = jax.random.split(jax.random.key(seed), 13)
    return {
        "position": gaussian(arg_keys[0], (3, NP), 0.5, 3.0, ((1, 128),), jnp.float32),
        "smoothing": jnp.clip(jnp.exp(math.log(1.4) - 0.6931472 * jax.random.uniform(arg_keys[1], (NP,), jnp.float32) ** level_of(arg_keys[1], (NP,), ((0, 128),), -0.2, 0.2)), 0.7, 1.4),
        "mass": jnp.clip(jnp.exp(math.log(0.004) - 1.3862944 * jax.random.uniform(arg_keys[2], (NP,), jnp.float32) ** level_of(arg_keys[2], (NP,), ((0, 128),), -0.2, 0.2)), 0.001, 0.004),
        "energy": jnp.clip(jnp.exp(math.log(2.0) - 1.3862944 * jax.random.uniform(arg_keys[3], (NP,), jnp.float32) ** level_of(arg_keys[3], (NP,), ((0, 128),), -0.2, 0.2)), 0.5, 2.0),
        "species": jnp.clip(1.0 * jax.random.uniform(arg_keys[4], (SPECIES, NP), jnp.float32) ** level_of(arg_keys[4], (SPECIES, NP), ((1, 128),), -0.2, 0.2), 0.0, 1.0),
        "neighbours": set_ends(jax.random.randint(arg_keys[5], (NB_DEV * N_DOM * N_SUB, NBR_K), 0, NB_DEV), jax.random.fold_in(arg_keys[5], 1), 0, NB_DEV - 1).astype(jnp.int32),
        "exports": set_ends(jax.random.randint(arg_keys[6], (N_DOM * N_SUB * 2 * N_SUB, EXP_SLOTS), 0, NB_DEV), jax.random.fold_in(arg_keys[6], 1), 0, NB_DEV - 1).astype(jnp.int32),
        "imports": set_ends(jax.random.randint(arg_keys[7], (N_DOM * N_SUB * 2 * N_SUB * EXP_SLOTS, IMP_K), 0, NB_DEV), jax.random.fold_in(arg_keys[7], 1), 0, NB_DEV - 1).astype(jnp.int32),
        "jac_inverse": draw_jac_inverse(jax.random.fold_in(arg_keys[12], 71), 0),
        "rates": gaussian(arg_keys[9], (SPECIES, SPECIES), SPECIES ** -0.5, 1.75, (), jnp.float32),
        "chem_steps": draw_chem_steps(jax.random.fold_in(arg_keys[12], 71), 0),
        "dense_slot": draw_dense_slot(jax.random.fold_in(arg_keys[12], 71), 0),
    }


gamma_gas = 5.0 / 3.0
chem_tau = 0.5
map_batch = 16


def pair_kernel(tgt_pos, tgt_width, src_pos, src_mass, src_factor, with_density, with_first, with_second):
    offset = tgt_pos[:, :, None] - src_pos[:, None, :]
    squared = jnp.sum(offset * offset, axis=0)
    inv_sq = 1.0 / (tgt_width * tgt_width)
    base = 1.0 / (1.0 + squared * inv_sq[:, None])
    pieces = []
    if with_density:
        dens = jnp.sum(base * base * src_mass[None, :], axis=1) / (tgt_width * tgt_width * tgt_width)
        pieces.append(dens[None, :])
    if with_first or with_second:
        slope = (-4.0 * inv_sq * inv_sq / tgt_width)[:, None] * base * base * base
        weighted = slope * src_mass[None, :]
        if with_first:
            pieces.append(jnp.sum(offset * weighted[None], axis=2))
        if with_second:
            pieces.append(jnp.sum(offset * (weighted * src_factor[None, :])[None], axis=2))
    return jnp.concatenate(pieces, axis=0)


def group_terms(tgt_fields, tgt_rows, src_fields, src_rows, flags):
    def single(record):
        target, sources = record
        picked = src_fields[:, sources]
        flat = picked.reshape(picked.shape[0], -1)
        return pair_kernel(tgt_fields[:3, target], tgt_fields[3, target], flat[:3], flat[3], flat[4],
                           flags[0], flags[1], flags[2])
    return lax.map(single, (tgt_rows, src_rows), batch_size=map_batch)


def chem_update(abund, drive_gain, jac_inverse, rates):
    drive = jnp.tanh(jnp.dot(rates, abund, precision=lax.Precision.HIGHEST, preferred_element_type=jnp.float32)) + 1.0
    return jnp.dot(jac_inverse, abund + chem_tau * drive_gain[None, :] * drive,
                   precision=lax.Precision.HIGHEST, preferred_element_type=jnp.float32)


def reference(position, smoothing, mass, energy, species, neighbours, exports, imports, jac_inverse, rates, chem_steps, dense_slot):
    devices = N_DOM * N_SUB
    blocks = devices * NB_DEV
    tgt_fields = jnp.concatenate([position, smoothing[None]], 0).reshape(4, blocks, BLOCK)
    all_rows = jnp.arange(blocks, dtype=jnp.int32)
    owner = (all_rows // NB_DEV) * NB_DEV
    local_src = (owner[:, None] + neighbours).astype(jnp.int32)
    device_ids = jnp.arange(devices, dtype=jnp.int32)
    dom_of = device_ids // N_SUB
    sub_of = device_ids % N_SUB
    shifts = jnp.array([-1, 1], dtype=jnp.int32)
    sub_ids = jnp.arange(N_SUB, dtype=jnp.int32)
    receiver = (((dom_of[:, None, None] + shifts[None, :, None]) % N_DOM) * N_SUB + sub_ids[None, None, :]).astype(jnp.int32)
    export_grid = exports.reshape(devices, 2, N_SUB, EXP_SLOTS)
    import_grid = imports.reshape(devices, 2, N_SUB, EXP_SLOTS, IMP_K)
    flipped = (1 - jnp.arange(2, dtype=jnp.int32))[None, :, None]
    sender_sub = sub_of[:, None, None]
    picked = import_grid[receiver, flipped, sender_sub]
    remote_src = (receiver[:, :, :, None, None] * NB_DEV + picked).reshape(-1, IMP_K).astype(jnp.int32)
    remote_tgt = (device_ids[:, None, None, None] * NB_DEV + export_grid).reshape(-1).astype(jnp.int32)
    zero_field = jnp.zeros_like(mass)
    src_first = jnp.concatenate([position, mass[None], zero_field[None]], 0).reshape(5, blocks, BLOCK)
    local_dens = group_terms(tgt_fields, all_rows, src_first, local_src, (True, False, False))
    remote_dens = group_terms(tgt_fields, remote_tgt, src_first, remote_src, (True, False, False))
    dens_total = local_dens + jax.ops.segment_sum(remote_dens, remote_tgt, num_segments=blocks)
    density = dens_total.reshape(-1)
    factor = (gamma_gas - 1.0) * energy / density
    src_second = jnp.concatenate([position, mass[None], factor[None]], 0).reshape(5, blocks, BLOCK)
    local_grad = group_terms(tgt_fields, all_rows, src_second, local_src, (False, True, True))
    remote_grad = group_terms(tgt_fields, remote_tgt, src_second, remote_src, (False, True, True))
    grads = local_grad + jax.ops.segment_sum(remote_grad, remote_tgt, num_segments=blocks)
    first = jnp.transpose(grads[:, 0:3], (1, 0, 2)).reshape(3, -1)
    second = jnp.transpose(grads[:, 3:6], (1, 0, 2)).reshape(3, -1)
    accel = -(factor[None, :] * first + second)
    drive_gain = density / (density + 1.0)
    limit = jnp.where(dense_slot >= 0, chem_steps, jnp.minimum(chem_steps, S_LO))

    def advance(cycle_no, abund):
        update = chem_update(abund, drive_gain, jac_inverse, rates)
        return jnp.where((cycle_no < limit)[None, :], update, abund)

    abund = lax.fori_loop(0, SMAX, advance, species)
    return density, accel, abund
```

```python
import functools

import jax
import jax.numpy as jnp
from jax import lax
from jax.experimental import pallas as pl
from jax.experimental.pallas import tpu as pltpu
from jax.sharding import PartitionSpec as P

BLOCK = 128
BLOCKS = 32
NBR = 4
SLOTS = 16
SPECIES = 12
S_LO = 4
SMAX = 32
HALF = BLOCKS * BLOCK // 2
FEAT = 48
GROUPS = 4
MESH = pl.DeviceIdType.MESH
F32 = jnp.float32
BF16 = jnp.bfloat16
HIGH = lax.Precision.HIGHEST

gamma_gas = 5.0 / 3.0
chem_tau = 0.5


def pieces(value):
    high = value.astype(BF16).astype(F32)
    rest = value - high
    middle = rest.astype(BF16).astype(F32)
    return high, middle, rest - middle


def halves(value):
    high = value.astype(BF16)
    return high, (value - high.astype(F32)).astype(BF16)


def mm(a, b):
    return jnp.dot(a, b, preferred_element_type=F32)


def source_features(fields):
    high, middle, low = pieces(fields)
    return jnp.concatenate([high, high, high, middle, middle, low], 0).T.astype(BF16)


def gradient_rows(fields, factor):
    row = lax.broadcasted_iota(jnp.int32, fields.shape, 0)
    both = jnp.where(row < 4, fields, pltpu.roll(fields, 4, 0))
    high, low = halves(both * jnp.where(row < 4, 1.0, factor))
    return jnp.concatenate([high, low], 0)


def pair_terms(features, target, high_ref, low_ref):
    base = 1.0 / mm(features, target)
    squared = base * base
    high, low = halves(squared * base)
    high_ref[...] = high
    low_ref[...] = low
    return jnp.sum(squared, axis=0, keepdims=True)


def spread(matrix):
    wide = 2 * SPECIES
    pick = (
        lax.broadcasted_iota(jnp.int32, (wide, SPECIES), 0) % SPECIES
        == lax.broadcasted_iota(jnp.int32, (wide, SPECIES), 1)
    ).astype(F32)
    tall = jnp.dot(pick, matrix, precision=HIGH, preferred_element_type=F32)
    full = lax.dot_general(
        tall, pick, (((1,), (1,)), ((), ())), precision=HIGH, preferred_element_type=F32
    )
    same = (
        lax.broadcasted_iota(jnp.int32, (wide, wide), 0) // SPECIES
        == lax.broadcasted_iota(jnp.int32, (wide, wide), 1) // SPECIES
    )
    return jnp.where(same, full, 0.0)


def left_side(matrix):
    high, low = halves(matrix)
    return jnp.concatenate([high.astype(F32), high.astype(F32), low.astype(F32)], 1).astype(BF16)


def right_side(state):
    high, low = halves(state)
    return jnp.concatenate([high, low, high], 0)


def kernel(
    pos,
    width,
    mass,
    energy,
    species,
    neigh,
    exports,
    imports,
    jac,
    rates,
    steps,
    slot,
    dens_out,
    accel_out,
    abund_out,
    fields,
    targets,
    feats,
    far_feats,
    stage,
    far_fields,
    factor,
    stage_factor,
    far_factor,
    rows,
    far_rows,
    near_high,
    near_low,
    far_high,
    far_low,
    near_dens,
    far_dens,
    near_acc,
    far_acc,
    root_mass,
    gain,
    limit,
    state,
    rate_in,
    send_one,
    recv_one,
    send_two,
    recv_two,
):
    dom = lax.axis_index("dom")
    sub = lax.axis_index("sub")
    doms = lax.axis_size("dom")
    subs = lax.axis_size("sub")
    sides = [lax.rem(dom + doms - 1, doms), lax.rem(dom + 1, doms)]
    barrier = pltpu.get_barrier_semaphore()
    for side in sides:
        for q in range(subs):
            pl.semaphore_signal(barrier, inc=1, device_id=(side, q), device_id_type=MESH)

    def exchange(sent, landed, send_sem, recv_sem):
        copies = []
        for e in range(2):
            for q in range(subs):
                copies.append(
                    pltpu.make_async_remote_copy(
                        src_ref=sent.at[e * subs + q],
                        dst_ref=landed.at[(1 - e) * subs + sub],
                        send_sem=send_sem.at[e * subs + q],
                        recv_sem=recv_sem.at[(1 - e) * subs + sub],
                        device_id=(sides[e], q),
                        device_id_type=MESH,
                    )
                )
        return copies

    def arrive(sent, landed, send_sem, recv_sem):
        for e in range(2):
            for q in range(subs):
                pltpu.make_async_remote_copy(
                    src_ref=sent.at[e * subs + q],
                    dst_ref=landed.at[e * subs + q],
                    send_sem=send_sem.at[e * subs + q],
                    recv_sem=recv_sem.at[e * subs + q],
                    device_id=(sides[e], q),
                    device_id_type=MESH,
                ).wait_recv()

    root_mass[...] = 1.0 / jnp.sqrt(mass[...])

    def prepare(b, _):
        place = pos[:, pl.ds(pl.multiple_of(b * BLOCK, BLOCK), BLOCK)]
        weight = root_mass[pl.ds(b, 1)]
        norm = jnp.sum(place * place, axis=0, keepdims=True)
        fields[b, 0:3] = place * weight
        fields[b, 3:4] = weight
        fields[b, 4:5] = norm * weight
        fields[b, 5:8] = jnp.zeros((3, BLOCK), F32)
        span = width[pl.ds(b, 1)]
        target = jnp.concatenate(
            [place * -2.0, span * span + norm, jnp.ones_like(norm), jnp.zeros((3, BLOCK), F32)], 0
        )
        high, middle, low = pieces(target)
        targets[b] = jnp.concatenate([high, middle, low, high, middle, high], 0).astype(BF16)
        return 0

    lax.fori_loop(0, BLOCKS, prepare, 0, unroll=4)
    for r in range(SLOTS):
        for k in range(2):
            stage[r // 2, (r % 2) * 2 + k] = fields[imports[k, r]]
    jac_full = spread(jac[...])
    rate_full = spread(rates[...])
    both = jnp.dot(rate_full, jac_full, precision=HIGH, preferred_element_type=F32)
    left = left_side(jnp.concatenate([jac_full, both], 0))
    left_first = left_side(rate_full)
    pl.semaphore_wait(barrier, 2 * subs)
    first = exchange(stage, far_fields, send_one, recv_one)
    for copy in first:
        copy.start()

    def transposed(b, _):
        feats[b] = source_features(fields[b])
        return 0

    lax.fori_loop(0, BLOCKS, transposed, 0, unroll=4)

    def near_first(b, _):
        lhs = jnp.concatenate([feats[neigh[k, b]] for k in range(NBR)], 0)
        near_dens[pl.ds(b, 1)] = pair_terms(lhs, targets[b], near_high.at[b], near_low.at[b])
        return 0

    lax.fori_loop(0, BLOCKS, near_first, 0, unroll=4)
    arrive(stage, far_fields, send_one, recv_one)

    def far_transposed(j, _):
        for k in range(4):
            far_feats[j * 4 + k] = source_features(far_fields[j, k])
        return 0

    lax.fori_loop(0, SLOTS // 2, far_transposed, 0)

    def far_first(r, _):
        lhs = jnp.concatenate([far_feats[r * 2 + k] for k in range(2)], 0)
        target = targets[exports[lax.rem(r, 2), r // 2]]
        far_dens[pl.ds(r, 1)] = pair_terms(lhs, target, far_high.at[r], far_low.at[r])
        return 0

    lax.fori_loop(0, SLOTS, far_first, 0, unroll=4)

    owner = lax.broadcasted_iota(jnp.int32, (BLOCKS, BLOCK), 0)
    total = near_dens[...]
    for r in range(SLOTS):
        total += jnp.where(owner == exports[r % 2, r // 2], far_dens[r : r + 1], 0.0)
    density = total * width[...]
    dens_out[...] = density
    factor[...] = (gamma_gas - 1.0) * energy[...] / density
    for r in range(SLOTS):
        for k in range(2):
            stage_factor[r // 2, pl.ds((r % 2) * 2 + k, 1)] = factor[pl.ds(imports[k, r], 1)]
    gain_all = chem_tau * (density / (density + 1.0))
    most = jnp.where(slot[...] >= 0, steps[...], jnp.minimum(steps[...], S_LO)).astype(F32)
    second = exchange(stage_factor, far_factor, send_two, recv_two)
    for copy in second:
        copy.start()

    def rows_near(b, _):
        rows[b] = gradient_rows(fields[b], factor[pl.ds(b, 1)])
        return 0

    lax.fori_loop(0, BLOCKS, rows_near, 0, unroll=4)

    def near_second(b, _):
        lhs = jnp.concatenate([rows[neigh[k, b]] for k in range(NBR)], 1)
        out = mm(lhs, near_high[b]) + mm(lhs, near_low[b])
        near_acc[b] = out[0:8] + out[8:16]
        return 0

    lax.fori_loop(0, BLOCKS, near_second, 0, unroll=4)

    for b in range(BLOCKS // 2):
        for h in range(2):
            block = b + h * (BLOCKS // 2)
            at = pl.ds(b * BLOCK, BLOCK)
            span = pl.ds(h * SPECIES, SPECIES)
            gain[span, at] = jnp.broadcast_to(gain_all[block : block + 1], (SPECIES, BLOCK))
            limit[span, at] = jnp.broadcast_to(most[block : block + 1], (SPECIES, BLOCK))
    state[0:SPECIES] = species[:, 0:HALF]
    state[SPECIES : 2 * SPECIES] = species[:, HALF : 2 * HALF]
    part = HALF // GROUPS
    for g in range(GROUPS):
        at = pl.ds(g * part, part)
        rate_in[:, at] = mm(left_first, right_side(state[:, at]))

    def cycle(c, _):
        for g in range(GROUPS):
            at = pl.ds(g * part, part)
            abund = state[:, at]
            lift = gain[:, at]
            moved = (abund + lift) + lift * jnp.tanh(rate_in[:, at])
            out = mm(left, right_side(moved))
            rate_in[:, at] = out[2 * SPECIES :]
            state[:, at] = jnp.where(c.astype(F32) < limit[:, at], out[: 2 * SPECIES], abund)
        return 0

    lax.fori_loop(0, SMAX, cycle, 0, unroll=4)
    abund_out[:, 0:HALF] = state[0:SPECIES]
    abund_out[:, HALF : 2 * HALF] = state[SPECIES : 2 * SPECIES]

    arrive(stage_factor, far_factor, send_two, recv_two)

    def rows_far(j, _):
        for k in range(4):
            far_rows[j * 4 + k] = gradient_rows(far_fields[j, k], far_factor[j, pl.ds(k, 1)])
        return 0

    lax.fori_loop(0, SLOTS // 2, rows_far, 0)

    def far_second(r, _):
        lhs = jnp.concatenate([far_rows[r * 2 + k] for k in range(2)], 1)
        out = mm(lhs, far_high[r]) + mm(lhs, far_low[r])
        far_acc[r] = out[0:8] + out[8:16]
        return 0

    lax.fori_loop(0, SLOTS, far_second, 0, unroll=4)

    row = lax.broadcasted_iota(jnp.int32, (8, BLOCK), 0)

    def finish(b, _):
        acc = near_acc[b]
        for r in range(SLOTS):
            acc += far_acc[r] * (exports[r % 2, r // 2] == b).astype(F32)
        acc = acc * jnp.where(row < 4, factor[pl.ds(b, 1)], 1.0)
        acc = acc + pltpu.roll(acc, 4, 0)
        at = pl.ds(pl.multiple_of(b * BLOCK, BLOCK), BLOCK)
        accel_out[:, at] = (4.0 * width[pl.ds(b, 1)]) * (pos[:, at] * acc[3:4] - acc[0:3])
        return 0

    lax.fori_loop(0, BLOCKS, finish, 0, unroll=2)
    for copy in first + second:
        copy.wait_send()


def on_device(
    position,
    smoothing,
    mass,
    energy,
    species,
    neighbours,
    exports,
    imports,
    jac_inverse,
    rates,
    chem_steps,
    dense_slot,
):
    tile = (BLOCKS, BLOCK)
    vmem = pl.BlockSpec(memory_space=pltpu.VMEM)
    smem = pl.BlockSpec(memory_space=pltpu.SMEM)
    far = 2 * SLOTS
    density, accel, abund = pl.pallas_call(
        kernel,
        out_shape=(
            jax.ShapeDtypeStruct(tile, F32),
            jax.ShapeDtypeStruct(position.shape, F32),
            jax.ShapeDtypeStruct(species.shape, F32),
        ),
        in_specs=[vmem] * 5 + [smem] * 3 + [vmem] * 4,
        out_specs=(vmem, vmem, vmem),
        scratch_shapes=[
            pltpu.VMEM((BLOCKS, 8, BLOCK), F32),
            pltpu.VMEM((BLOCKS, FEAT, BLOCK), BF16),
            pltpu.VMEM((BLOCKS, BLOCK, FEAT), BF16),
            pltpu.VMEM((far, BLOCK, FEAT), BF16),
            pltpu.VMEM((SLOTS // 2, 4, 8, BLOCK), F32),
            pltpu.VMEM((SLOTS // 2, 4, 8, BLOCK), F32),
            pltpu.VMEM(tile, F32),
            pltpu.VMEM((SLOTS // 2, 4, BLOCK), F32),
            pltpu.VMEM((SLOTS // 2, 4, BLOCK), F32),
            pltpu.VMEM((BLOCKS, 16, BLOCK), BF16),
            pltpu.VMEM((far, 16, BLOCK), BF16),
            pltpu.VMEM((BLOCKS, NBR * BLOCK, BLOCK), BF16),
            pltpu.VMEM((BLOCKS, NBR * BLOCK, BLOCK), BF16),
            pltpu.VMEM((SLOTS, 2 * BLOCK, BLOCK), BF16),
            pltpu.VMEM((SLOTS, 2 * BLOCK, BLOCK), BF16),
            pltpu.VMEM(tile, F32),
            pltpu.VMEM((SLOTS, BLOCK), F32),
            pltpu.VMEM((BLOCKS, 8, BLOCK), F32),
            pltpu.VMEM((SLOTS, 8, BLOCK), F32),
            pltpu.VMEM(tile, F32),
            pltpu.VMEM((2 * SPECIES, HALF), F32),
            pltpu.VMEM((2 * SPECIES, HALF), F32),
            pltpu.VMEM((2 * SPECIES, HALF), F32),
            pltpu.VMEM((2 * SPECIES, HALF), F32),
            pltpu.SemaphoreType.DMA((SLOTS // 2,)),
            pltpu.SemaphoreType.DMA((SLOTS // 2,)),
            pltpu.SemaphoreType.DMA((SLOTS // 2,)),
            pltpu.SemaphoreType.DMA((SLOTS // 2,)),
        ],
        compiler_params=pltpu.CompilerParams(
            collective_id=0, has_side_effects=True, vmem_limit_bytes=67043328
        ),
        name="particle_step",
    )(
        position,
        smoothing.reshape(tile),
        mass.reshape(tile),
        energy.reshape(tile),
        species,
        neighbours.T,
        exports.T,
        imports.T,
        jac_inverse,
        rates,
        chem_steps.reshape(tile),
        dense_slot.reshape(tile),
    )
    return density.reshape(-1), accel, abund


def solution(mesh):
    flat = P(("dom", "sub"))
    wide = P(None, ("dom", "sub"))
    tall = P(("dom", "sub"), None)
    return jax.shard_map(
        on_device,
        mesh=mesh,
        in_specs=(wide, flat, flat, flat, wide, tall, tall, tall, P(), P(), flat, flat),
        out_specs=(flat, wide, wide),
        check_vma=False,
    )
```

```python
import functools

import jax
import jax.numpy as jnp
from jax import lax
from jax.experimental import pallas as pl
from jax.experimental.pallas import tpu as pltpu
from jax.sharding import PartitionSpec as P

BLOCK = 128
BLOCKS = 32
NBR = 4
SLOTS = 16
SPECIES = 12
S_LO = 4
SMAX = 32
HALF = BLOCKS * BLOCK // 2
FEAT = 48
GROUPS = 4
FIRST = 8
MESH = pl.DeviceIdType.MESH
F32 = jnp.float32
BF16 = jnp.bfloat16
HIGH = lax.Precision.HIGHEST

gamma_gas = 5.0 / 3.0
chem_tau = 0.5


def pieces(value):
    high = value.astype(BF16).astype(F32)
    rest = value - high
    middle = rest.astype(BF16).astype(F32)
    return high, middle, rest - middle


def halves(value):
    high = value.astype(BF16)
    return high, (value - high.astype(F32)).astype(BF16)


def mm(a, b):
    return jnp.dot(a, b, preferred_element_type=F32)


def source_features(fields):
    high, middle, low = pieces(fields)
    return jnp.concatenate([high, high, high, middle, middle, low], 0).T.astype(BF16)


def gradient_rows(fields, factor):
    row = lax.broadcasted_iota(jnp.int32, fields.shape, 0)
    both = jnp.where(row < 4, fields, pltpu.roll(fields, 4, 0))
    high, low = halves(both * jnp.where(row < 4, 1.0, factor))
    return jnp.concatenate([high, low], 0)


def pair_terms(features, target, cubes, dens, row):
    total = None
    for k, feature in enumerate(features):
        base = 1.0 / mm(feature, target)
        squared = base * base
        cubes[k * BLOCK : (k + 1) * BLOCK] = squared * base
        part = jnp.sum(squared.reshape(BLOCK // 8, 8, BLOCK), axis=0)
        total = part if total is None else total + part
    dens[pl.ds(row, 1)] = jnp.sum(total, axis=0, keepdims=True)


def pair_sums(rows, cubes):
    high, low = halves(cubes[...])
    lhs = jnp.concatenate(rows, 1)
    out = mm(lhs, high) + mm(lhs, low)
    return out[0:8] + out[8:16]


def spread(matrix):
    wide = 2 * SPECIES
    pick = (
        lax.broadcasted_iota(jnp.int32, (wide, SPECIES), 0) % SPECIES
        == lax.broadcasted_iota(jnp.int32, (wide, SPECIES), 1)
    ).astype(F32)
    tall = jnp.dot(pick, matrix, precision=HIGH, preferred_element_type=F32)
    full = lax.dot_general(
        tall, pick, (((1,), (1,)), ((), ())), precision=HIGH, preferred_element_type=F32
    )
    same = (
        lax.broadcasted_iota(jnp.int32, (wide, wide), 0) // SPECIES
        == lax.broadcasted_iota(jnp.int32, (wide, wide), 1) // SPECIES
    )
    return jnp.where(same, full, 0.0)


def left_side(matrix):
    high, low = halves(matrix)
    return jnp.concatenate([high.astype(F32), high.astype(F32), low.astype(F32)], 1).astype(BF16)


def right_side(state):
    high, low = halves(state)
    return jnp.concatenate([high, low, high], 0)


def kernel(
    pos_in,
    width_in,
    mass_in,
    energy_in,
    species_in,
    neigh_in,
    exports_in,
    imports_in,
    jac_in,
    rates_in,
    steps_in,
    slot_in,
    density,
    accel,
    abund_all,
    pos,
    width,
    mass,
    energy,
    species,
    neigh,
    exports,
    imports,
    jac,
    rates,
    steps,
    slot,
    fields,
    targets,
    feats,
    stage,
    far_fields,
    factor,
    stage_factor,
    far_factor,
    rows,
    far_rows,
    near_cubes,
    far_cubes,
    near_dens,
    far_dens,
    near_acc,
    far_acc,
    root_mass,
    gain,
    limit,
    state,
    rate_in,
    load_sem,
    send_one,
    recv_one,
    send_two,
    recv_two,
):
    dom = lax.axis_index("dom")
    sub = lax.axis_index("sub")
    doms = lax.axis_size("dom")
    subs = lax.axis_size("sub")
    sides = [lax.rem(dom + doms - 1, doms), lax.rem(dom + 1, doms)]
    barrier = pltpu.get_barrier_semaphore()
    for side in sides:
        for q in range(subs):
            pl.semaphore_signal(barrier, inc=1, device_id=(side, q), device_id_type=MESH)

    pairs = {
        "pos": (pos_in, pos),
        "mass": (mass_in, mass),
        "imports": (imports_in, imports),
        "width": (width_in, width),
        "neigh": (neigh_in, neigh),
        "exports": (exports_in, exports),
        "jac": (jac_in, jac),
        "rates": (rates_in, rates),
        "energy": (energy_in, energy),
        "steps": (steps_in, steps),
        "slot": (slot_in, slot),
        "species": (species_in, species),
    }
    loads = {}
    for i, (name, (source, target)) in enumerate(pairs.items()):
        loads[name] = pltpu.make_async_copy(source, target, load_sem.at[i])
        loads[name].start()

    def exchange(sent, landed, send_sem, recv_sem):
        copies = []
        for e in range(2):
            for q in range(subs):
                copies.append(
                    pltpu.make_async_remote_copy(
                        src_ref=sent.at[e * subs + q],
                        dst_ref=landed.at[(1 - e) * subs + sub],
                        send_sem=send_sem.at[e * subs + q],
                        recv_sem=recv_sem.at[(1 - e) * subs + sub],
                        device_id=(sides[e], q),
                        device_id_type=MESH,
                    )
                )
        return copies

    def arrive(place, sent, landed, send_sem, recv_sem):
        pltpu.make_async_remote_copy(
            src_ref=sent.at[place],
            dst_ref=landed.at[place],
            send_sem=send_sem.at[place],
            recv_sem=recv_sem.at[place],
            device_id=(sides[0], 0),
            device_id_type=MESH,
        ).wait_recv()

    loads["pos"].wait()
    loads["mass"].wait()
    root_mass[...] = 1.0 / jnp.sqrt(mass[...])

    def prepare(b, _):
        place = pos[:, pl.ds(pl.multiple_of(b * BLOCK, BLOCK), BLOCK)]
        weight = root_mass[pl.ds(b, 1)]
        fields[b, 0:3] = place * weight
        fields[b, 3:4] = weight
        fields[b, 4:5] = jnp.sum(place * place, axis=0, keepdims=True) * weight
        fields[b, 5:8] = jnp.zeros((3, BLOCK), F32)
        return 0

    lax.fori_loop(0, BLOCKS, prepare, 0, unroll=8)
    loads["imports"].wait()
    for r in range(SLOTS):
        for k in range(2):
            stage[r // 2, (r % 2) * 2 + k] = fields[imports[k, r]]
    loads["width"].wait()
    loads["neigh"].wait()
    loads["exports"].wait()
    loads["jac"].wait()
    loads["rates"].wait()
    pl.semaphore_wait(barrier, 2 * subs)
    first = exchange(stage, far_fields, send_one, recv_one)
    for copy in first:
        copy.start()

    def shape_block(b):
        place = pos[:, pl.ds(pl.multiple_of(b * BLOCK, BLOCK), BLOCK)]
        norm = jnp.sum(place * place, axis=0, keepdims=True)
        span = width[pl.ds(b, 1)]
        target = jnp.concatenate(
            [place * -2.0, span * span + norm, jnp.ones_like(norm), jnp.zeros((3, BLOCK), F32)], 0
        )
        high, middle, low = pieces(target)
        targets[b] = jnp.concatenate([high, middle, low, high, middle, high], 0).astype(BF16)
        feats[b] = source_features(fields[b])

    for b in range(FIRST):
        shape_block(b)
    jac_full = spread(jac[...])
    rate_full = spread(rates[...])
    both = jnp.dot(rate_full, jac_full, precision=HIGH, preferred_element_type=F32)
    left = left_side(jnp.concatenate([jac_full, both], 0))
    left_first = left_side(rate_full)

    def shape_more(b, _):
        shape_block(b)
        return 0

    lax.fori_loop(FIRST, BLOCKS, shape_more, 0, unroll=4)

    def near_first(b, _):
        parts = [feats[neigh[k, b]] for k in range(NBR)]
        pair_terms(parts, targets[b], near_cubes.at[b], near_dens, b)
        return 0

    lax.fori_loop(0, BLOCKS, near_first, 0, unroll=4)
    for name in ("energy", "steps", "slot", "species"):
        loads[name].wait()

    def far_first(i, _):
        q = lax.rem(sub + i + (i // 2) * (1 - 2 * lax.rem(i, 2)), subs)
        for e in range(2):
            arrive(e * subs + q, stage, far_fields, send_one, recv_one)
        for e in range(2):
            place = e * subs + q
            parts = [source_features(far_fields[place, k]) for k in range(4)]
            for x in range(2):
                slot_at = place * 2 + x
                target = targets[exports[x, place]]
                pair_terms(
                    parts[2 * x : 2 * x + 2], target, far_cubes.at[slot_at], far_dens, slot_at
                )
        return 0

    lax.fori_loop(0, subs, far_first, 0)

    owner = lax.broadcasted_iota(jnp.int32, (BLOCKS, BLOCK), 0)
    total = near_dens[...]
    for r in range(SLOTS):
        total += jnp.where(owner == exports[r % 2, r // 2], far_dens[r : r + 1], 0.0)
    dens = total * width[...]
    density[...] = dens
    factor[...] = (gamma_gas - 1.0) * energy[...] / dens
    for r in range(SLOTS):
        for k in range(2):
            stage_factor[r // 2, pl.ds((r % 2) * 2 + k, 1)] = factor[pl.ds(imports[k, r], 1)]
    gain_all = chem_tau * (dens / (dens + 1.0))
    most = jnp.where(slot[...] >= 0, steps[...], jnp.minimum(steps[...], S_LO)).astype(F32)
    for b in range(BLOCKS // 2):
        for h in range(2):
            block = b + h * (BLOCKS // 2)
            at = pl.ds(b * BLOCK, BLOCK)
            span = pl.ds(h * SPECIES, SPECIES)
            gain[span, at] = jnp.broadcast_to(gain_all[block : block + 1], (SPECIES, BLOCK))
            limit[span, at] = jnp.broadcast_to(most[block : block + 1], (SPECIES, BLOCK))
    state[0:SPECIES] = species[:, 0:HALF]
    state[SPECIES : 2 * SPECIES] = species[:, HALF : 2 * HALF]
    second = exchange(stage_factor, far_factor, send_two, recv_two)
    for copy in second:
        copy.start()
    part = HALF // GROUPS
    for g in range(GROUPS):
        at = pl.ds(g * part, part)
        rate_in[:, at] = mm(left_first, right_side(state[:, at]))

    def rows_near(b, _):
        rows[b] = gradient_rows(fields[b], factor[pl.ds(b, 1)])
        return 0

    lax.fori_loop(0, BLOCKS, rows_near, 0, unroll=8)

    def chem_step(c):
        for g in range(GROUPS):
            at = pl.ds(g * part, part)
            abund = state[:, at]
            lift = gain[:, at]
            moved = (abund + lift) + lift * jnp.tanh(rate_in[:, at])
            out = mm(left, right_side(moved))
            rate_in[:, at] = out[2 * SPECIES :]
            state[:, at] = jnp.where(c.astype(F32) < limit[:, at], out[: 2 * SPECIES], abund)

    def with_near(i, _):
        for s in range(4):
            chem_step(i * 4 + s)
            for n in range(2):
                b = i * 8 + s * 2 + n
                near_acc[b] = pair_sums([rows[neigh[k, b]] for k in range(NBR)], near_cubes.at[b])
        return 0

    lax.fori_loop(0, 4, with_near, 0)
    for place in range(2 * subs):
        arrive(place, stage_factor, far_factor, send_two, recv_two)
    for j in range(2 * subs):
        for k in range(4):
            far_rows[j * 4 + k] = gradient_rows(far_fields[j, k], far_factor[j, k : k + 1])

    def with_far(i, _):
        for s in range(4):
            chem_step(16 + i * 4 + s)
            for n in range(2):
                r = i * 8 + s * 2 + n
                far_acc[r] = pair_sums([far_rows[r * 2 + k] for k in range(2)], far_cubes.at[r])
        return 0

    lax.fori_loop(0, 2, with_far, 0)
    row = lax.broadcasted_iota(jnp.int32, (8, BLOCK), 0)

    def with_finish(i, _):
        for s in range(4):
            chem_step(24 + i * 4 + s)
            for n in range(4):
                b = i * 16 + s * 4 + n
                acc = near_acc[b]
                for r in range(SLOTS):
                    acc += far_acc[r] * (exports[r % 2, r // 2] == b).astype(F32)
                acc = acc * jnp.where(row < 4, factor[pl.ds(b, 1)], 1.0)
                acc = acc + pltpu.roll(acc, 4, 0)
                at = pl.ds(pl.multiple_of(b * BLOCK, BLOCK), BLOCK)
                accel[:, at] = (4.0 * width[pl.ds(b, 1)]) * (pos[:, at] * acc[3:4] - acc[0:3])
        return 0

    lax.fori_loop(0, 2, with_finish, 0)
    abund_all[:, 0:HALF] = state[0:SPECIES]
    abund_all[:, HALF : 2 * HALF] = state[SPECIES : 2 * SPECIES]
    for copy in first + second:
        copy.wait_send()


def deliver(density, accel, abund, dens_out, accel_out, abund_out, sems):
    pairs = ((abund, abund_out), (accel, accel_out), (density, dens_out))
    copies = [pltpu.make_async_copy(a, b, sems.at[i]) for i, (a, b) in enumerate(pairs)]
    for copy in copies:
        copy.start()
    for copy in copies:
        copy.wait()


def on_device(
    position,
    smoothing,
    mass,
    energy,
    species,
    neighbours,
    exports,
    imports,
    jac_inverse,
    rates,
    chem_steps,
    dense_slot,
):
    tile = (BLOCKS, BLOCK)
    vmem = pl.BlockSpec(memory_space=pltpu.VMEM)
    hbm = pl.BlockSpec(memory_space=pltpu.HBM)
    far = 2 * SLOTS
    sides = SLOTS // 2
    chem = (2 * SPECIES, HALF)
    given = (
        position,
        smoothing.reshape(tile),
        mass.reshape(tile),
        energy.reshape(tile),
        species,
        neighbours.T,
        exports.T,
        imports.T,
        jac_inverse,
        rates,
        chem_steps.reshape(tile),
        dense_slot.reshape(tile),
    )
    spaces = [pltpu.VMEM] * 5 + [pltpu.SMEM] * 3 + [pltpu.VMEM] * 4
    density, accel, abund = pl.pallas_call(
        kernel,
        out_shape=(
            pltpu.VMEM(tile, F32),
            pltpu.VMEM(position.shape, F32),
            pltpu.VMEM(species.shape, F32),
        ),
        in_specs=[hbm] * len(given),
        out_specs=(vmem, vmem, vmem),
        scratch_shapes=[space(x.shape, x.dtype) for space, x in zip(spaces, given)]
        + [
            pltpu.VMEM((BLOCKS, 8, BLOCK), F32),
            pltpu.VMEM((BLOCKS, FEAT, BLOCK), BF16),
            pltpu.VMEM((BLOCKS, BLOCK, FEAT), BF16),
            pltpu.VMEM((sides, 4, 8, BLOCK), F32),
            pltpu.VMEM((sides, 4, 8, BLOCK), F32),
            pltpu.VMEM(tile, F32),
            pltpu.VMEM((sides, 4, BLOCK), F32),
            pltpu.VMEM((sides, 4, BLOCK), F32),
            pltpu.VMEM((BLOCKS, 16, BLOCK), BF16),
            pltpu.VMEM((far, 16, BLOCK), BF16),
            pltpu.VMEM((BLOCKS, NBR * BLOCK, BLOCK), F32),
            pltpu.VMEM((SLOTS, 2 * BLOCK, BLOCK), F32),
            pltpu.VMEM(tile, F32),
            pltpu.VMEM((SLOTS, BLOCK), F32),
            pltpu.VMEM((BLOCKS, 8, BLOCK), F32),
            pltpu.VMEM((SLOTS, 8, BLOCK), F32),
            pltpu.VMEM(tile, F32),
            pltpu.VMEM(chem, F32),
            pltpu.VMEM(chem, F32),
            pltpu.VMEM(chem, F32),
            pltpu.VMEM(chem, F32),
            pltpu.SemaphoreType.DMA((len(given),)),
        ]
        + [pltpu.SemaphoreType.DMA((sides,))] * 4,
        compiler_params=pltpu.CompilerParams(
            collective_id=0, has_side_effects=True, vmem_limit_bytes=24 << 20
        ),
        name="particle_step",
    )(*(pltpu.with_memory_space_constraint(x, pltpu.HBM) for x in given))
    density, accel, abund = pl.pallas_call(
        deliver,
        out_shape=(
            jax.ShapeDtypeStruct(tile, F32),
            jax.ShapeDtypeStruct(position.shape, F32),
            jax.ShapeDtypeStruct(species.shape, F32),
        ),
        in_specs=[vmem] * 3,
        out_specs=(hbm,) * 3,
        scratch_shapes=[pltpu.SemaphoreType.DMA((3,))],
        compiler_params=pltpu.CompilerParams(vmem_limit_bytes=1 << 20),
        name="deliver",
    )(density, accel, abund)
    return density.reshape(-1), accel, abund


def solution(mesh):
    flat = P(("dom", "sub"))
    wide = P(None, ("dom", "sub"))
    tall = P(("dom", "sub"), None)
    return jax.shard_map(
        on_device,
        mesh=mesh,
        in_specs=(wide, flat, flat, flat, wide, tall, tall, tall, P(), P(), flat, flat),
        out_specs=(flat, wide, wide),
        check_vma=False,
    )
```

```python
import functools

import jax
import jax.numpy as jnp
from jax import lax
from jax.experimental import pallas as pl
from jax.experimental.pallas import tpu as pltpu
from jax.sharding import PartitionSpec as P

BLOCK = 128
BLOCKS = 32
NBR = 4
SLOTS = 16
SPECIES = 12
S_LO = 4
SMAX = 32
HALF = BLOCKS * BLOCK // 2
FEAT = 48
GROUPS = 4
FIRST = 8
MESH = pl.DeviceIdType.MESH
F32 = jnp.float32
BF16 = jnp.bfloat16
HIGH = lax.Precision.HIGHEST

gamma_gas = 5.0 / 3.0
chem_tau = 0.5


def pieces(value):
    high = value.astype(BF16).astype(F32)
    rest = value - high
    middle = rest.astype(BF16).astype(F32)
    return high, middle, rest - middle


def halves(value):
    high = value.astype(BF16)
    return high, (value - high.astype(F32)).astype(BF16)


def mm(a, b):
    return jnp.dot(a, b, preferred_element_type=F32)


def source_features(fields):
    high, middle, low = pieces(fields)
    return jnp.concatenate([high, high, high, middle, middle, low], 0).T.astype(BF16)


def gradient_rows(fields, factor):
    row = lax.broadcasted_iota(jnp.int32, fields.shape, 0)
    both = jnp.where(row < 4, fields, pltpu.roll(fields, 4, 0))
    high, low = halves(both * jnp.where(row < 4, 1.0, factor))
    return jnp.concatenate([high, low], 0)


def distances(features, target, place):
    for k in range(0, len(features), 2):
        place[k // 2] = mm(jnp.concatenate(features[k : k + 2], 1), target)


def pair_terms(place, count, cubes, dens, row):
    total = None
    for k in range(count):
        for half in range(2):
            base = 1.0 / place[k, :, half * BLOCK : (half + 1) * BLOCK]
            squared = base * base
            at = (2 * k + half) * BLOCK
            cubes[at : at + BLOCK] = squared * base
            part = jnp.sum(squared.reshape(BLOCK // 8, 8, BLOCK), axis=0)
            total = part if total is None else total + part
    dens[pl.ds(row, 1)] = jnp.sum(total, axis=0, keepdims=True)


def pair_sums(rows, cubes):
    high, low = halves(cubes[...])
    lhs = jnp.concatenate(rows, 1)
    out = mm(lhs, high) + mm(lhs, low)
    return out[0:8] + out[8:16]


def spread(matrix):
    wide = 2 * SPECIES
    tall = jnp.concatenate([matrix, matrix], 0)
    full = jnp.concatenate([tall, tall], 1)
    same = (
        lax.broadcasted_iota(jnp.int32, (wide, wide), 0) // SPECIES
        == lax.broadcasted_iota(jnp.int32, (wide, wide), 1) // SPECIES
    )
    return jnp.where(same, full, 0.0)


def left_side(matrix):
    high, low = halves(matrix)
    blank = jnp.zeros((matrix.shape[0], 8), F32)
    high, low = high.astype(F32), low.astype(F32)
    return jnp.concatenate([high, blank, high, blank, low, blank], 1).astype(BF16)


def right_side(state):
    high, low = halves(jnp.concatenate([state, jnp.zeros((8, state.shape[1]), F32)], 0))
    return jnp.concatenate([high, low, high], 0)


def kernel(
    pos_in,
    width_in,
    mass_in,
    energy_in,
    species_in,
    neigh_in,
    exports_in,
    imports_in,
    jac_in,
    rates_in,
    steps_in,
    slot_in,
    density,
    accel,
    abund_all,
    pos,
    width,
    mass,
    energy,
    species,
    neigh,
    exports,
    imports,
    jac,
    rates,
    steps,
    slot,
    fields,
    targets,
    feats,
    far_feats,
    even,
    odd,
    stage,
    far_fields,
    factor,
    stage_factor,
    far_factor,
    rows,
    far_rows,
    near_cubes,
    far_cubes,
    near_dens,
    far_dens,
    near_acc,
    far_acc,
    root_mass,
    gain,
    limit,
    state,
    rate_in,
    load_sem,
    send_one,
    recv_one,
    send_two,
    recv_two,
):
    dom = lax.axis_index("dom")
    sub = lax.axis_index("sub")
    doms = lax.axis_size("dom")
    subs = lax.axis_size("sub")
    sides = [lax.rem(dom + doms - 1, doms), lax.rem(dom + 1, doms)]
    barrier = pltpu.get_barrier_semaphore()
    for side in sides:
        for q in range(subs):
            pl.semaphore_signal(barrier, inc=1, device_id=(side, q), device_id_type=MESH)

    pairs = {
        "pos": (pos_in, pos),
        "mass": (mass_in, mass),
        "imports": (imports_in, imports),
        "width": (width_in, width),
        "neigh": (neigh_in, neigh),
        "exports": (exports_in, exports),
        "jac": (jac_in, jac),
        "rates": (rates_in, rates),
        "energy": (energy_in, energy),
        "steps": (steps_in, steps),
        "slot": (slot_in, slot),
        "species": (species_in, species),
    }
    loads = {}
    for i, (name, (source, target)) in enumerate(pairs.items()):
        loads[name] = pltpu.make_async_copy(source, target, load_sem.at[i])
        loads[name].start()

    def exchange(sent, landed, send_sem, recv_sem):
        copies = []
        for e in range(2):
            for q in range(subs):
                copies.append(
                    pltpu.make_async_remote_copy(
                        src_ref=sent.at[e * subs + q],
                        dst_ref=landed.at[(1 - e) * subs + sub],
                        send_sem=send_sem.at[e * subs + q],
                        recv_sem=recv_sem.at[(1 - e) * subs + sub],
                        device_id=(sides[e], q),
                        device_id_type=MESH,
                    )
                )
        return copies

    def arrive(place, sent, landed, send_sem, recv_sem):
        pltpu.make_async_remote_copy(
            src_ref=sent.at[place],
            dst_ref=landed.at[place],
            send_sem=send_sem.at[place],
            recv_sem=recv_sem.at[place],
            device_id=(sides[0], 0),
            device_id_type=MESH,
        ).wait_recv()

    feats[...] = jnp.zeros_like(feats)
    targets[...] = jnp.zeros_like(targets)
    far_feats[...] = jnp.zeros_like(far_feats)
    loads["pos"].wait()
    loads["mass"].wait()
    root_mass[...] = 1.0 / jnp.sqrt(mass[...])

    def prepare(b, _):
        place = pos[:, pl.ds(pl.multiple_of(b * BLOCK, BLOCK), BLOCK)]
        weight = root_mass[pl.ds(b, 1)]
        fields[b, 0:3] = place * weight
        fields[b, 3:4] = weight
        fields[b, 4:5] = jnp.sum(place * place, axis=0, keepdims=True) * weight
        fields[b, 5:8] = jnp.zeros((3, BLOCK), F32)
        return 0

    lax.fori_loop(0, BLOCKS, prepare, 0, unroll=8)
    loads["imports"].wait()
    for r in range(SLOTS):
        for k in range(2):
            stage[r // 2, (r % 2) * 2 + k] = fields[imports[k, r]]
    loads["width"].wait()
    loads["neigh"].wait()
    loads["exports"].wait()
    loads["jac"].wait()
    loads["rates"].wait()
    pl.semaphore_wait(barrier, 2 * subs)
    first = exchange(stage, far_fields, send_one, recv_one)
    for copy in first:
        copy.start()

    def shape_block(b):
        place = pos[:, pl.ds(pl.multiple_of(b * BLOCK, BLOCK), BLOCK)]
        norm = jnp.sum(place * place, axis=0, keepdims=True)
        span = width[pl.ds(b, 1)]
        target = jnp.concatenate(
            [place * -2.0, span * span + norm, jnp.ones_like(norm), jnp.zeros((3, BLOCK), F32)], 0
        )
        high, middle, low = pieces(target)
        split = jnp.concatenate([high, middle, low, high, middle, high], 0).astype(BF16)
        targets[b, 0:FEAT, 0:BLOCK] = split
        targets[b, BLOCK : BLOCK + FEAT, BLOCK : 2 * BLOCK] = split
        feats[b, :, 0:FEAT] = source_features(fields[b])

    for b in range(FIRST):
        shape_block(b)
    jac_full = spread(jac[...])
    rate_full = spread(rates[...])
    both = jnp.dot(rates[...], jac[...], precision=HIGH, preferred_element_type=F32)
    left = left_side(jnp.concatenate([spread(both), jac_full], 0))
    left_first = left_side(rate_full)

    def shape_more(b, _):
        shape_block(b)
        return 0

    lax.fori_loop(FIRST, BLOCKS, shape_more, 0, unroll=4)

    def fill(b, place):
        distances([feats[neigh[k, b]] for k in range(NBR)], targets[b], place)

    def drain(b, place):
        pair_terms(place, NBR // 2, near_cubes.at[b], near_dens, b)

    fill(0, even.at[0])
    fill(1, even.at[1])

    def near_first(i, _):
        b = i * 4
        for n in range(2):
            fill(b + 2 + n, odd.at[n])
            drain(b + n, even.at[n])
        for n in range(2):
            fill(lax.rem(b + 4 + n, BLOCKS), even.at[n])
            drain(b + 2 + n, odd.at[n])
        return 0

    lax.fori_loop(0, BLOCKS // 4, near_first, 0)
    for name in ("energy", "steps", "slot", "species"):
        loads[name].wait()

    def far_fill(i, place):
        q = lax.rem(sub + (0, 1, 3, 2)[i], subs)
        for e in range(2):
            arrive(e * subs + q, stage, far_fields, send_one, recv_one)
        for e in range(2):
            for k in range(4):
                far_feats[i % 2, e * 4 + k, :, 0:FEAT] = source_features(
                    far_fields[e * subs + q, k]
                )
            for x in range(2):
                parts = [far_feats[i % 2, e * 4 + 2 * x + k] for k in range(2)]
                target = targets[exports[x, e * subs + q]]
                distances(parts, target, place.at[e, pl.ds(x, 1)])

    def far_drain(i, place):
        q = lax.rem(sub + (0, 1, 3, 2)[i], subs)
        for e in range(2):
            for x in range(2):
                at = (e * subs + q) * 2 + x
                pair_terms(place.at[e, pl.ds(x, 1)], 1, far_cubes.at[at], far_dens, at)

    places = (odd, even)
    far_fill(0, places[0])
    for i in range(1, 4):
        far_fill(i, places[i % 2])
        far_drain(i - 1, places[(i - 1) % 2])
    far_drain(3, places[1])

    owner = lax.broadcasted_iota(jnp.int32, (BLOCKS, BLOCK), 0)
    total = near_dens[...]
    for r in range(SLOTS):
        total += jnp.where(owner == exports[r % 2, r // 2], far_dens[r : r + 1], 0.0)
    dens = total * width[...]
    density[...] = dens
    factor[...] = (gamma_gas - 1.0) * energy[...] / dens
    for r in range(SLOTS):
        for k in range(2):
            stage_factor[r // 2, pl.ds((r % 2) * 2 + k, 1)] = factor[pl.ds(imports[k, r], 1)]
    second = exchange(stage_factor, far_factor, send_two, recv_two)
    for copy in second:
        copy.start()
    gain_all = chem_tau * (dens / (dens + 1.0))
    most = jnp.where(slot[...] >= 0, steps[...], jnp.minimum(steps[...], S_LO)).astype(F32)
    for b in range(BLOCKS // 2):
        for h in range(2):
            block = b + h * (BLOCKS // 2)
            at = pl.ds(b * BLOCK, BLOCK)
            span = pl.ds(h * SPECIES, SPECIES)
            gain[span, at] = jnp.broadcast_to(gain_all[block : block + 1], (SPECIES, BLOCK))
            limit[span, at] = jnp.broadcast_to(most[block : block + 1], (SPECIES, BLOCK))
    state[0:SPECIES] = species[:, 0:HALF]
    state[SPECIES : 2 * SPECIES] = species[:, HALF : 2 * HALF]
    part = HALF // GROUPS
    for g in range(GROUPS):
        at = pl.ds(g * part, part)
        rate_in[:, at] = mm(left_first, right_side(state[:, at]))

    def rows_near(b, _):
        rows[b] = gradient_rows(fields[b], factor[pl.ds(b, 1)])
        return 0

    lax.fori_loop(0, BLOCKS, rows_near, 0, unroll=8)

    def chem_step(c):
        for g in range(GROUPS):
            at = pl.ds(g * part, part)
            abund = state[:, at]
            lift = gain[:, at]
            moved = (abund + lift) + lift * jnp.tanh(rate_in[:, at])
            out = mm(left, right_side(moved))
            rate_in[:, at] = out[: 2 * SPECIES]
            state[:, at] = jnp.where(c.astype(F32) < limit[:, at], out[2 * SPECIES :], abund)

    def with_near(i, _):
        for s in range(4):
            chem_step(i * 4 + s)
            for n in range(2):
                b = i * 8 + s * 2 + n
                near_acc[b] = pair_sums([rows[neigh[k, b]] for k in range(NBR)], near_cubes.at[b])
        return 0

    lax.fori_loop(0, 4, with_near, 0)
    def alone(i, _):
        for s in range(4):
            chem_step(16 + i * 4 + s)
        return 0

    lax.fori_loop(0, 2, alone, 0)
    for place in range(2 * subs):
        arrive(place, stage_factor, far_factor, send_two, recv_two)
    for j in range(2 * subs):
        for k in range(4):
            far_rows[j * 4 + k] = gradient_rows(far_fields[j, k], far_factor[j, k : k + 1])
    row = lax.broadcasted_iota(jnp.int32, (8, BLOCK), 0)
    lane = lax.broadcasted_iota(jnp.int32, (8, BLOCK), 1)
    named = jnp.zeros((8, BLOCK), jnp.int32)
    for r in range(SLOTS):
        named = jnp.where(lane // 8 == r, exports[r % 2, r // 2], named)
    named = jnp.where(lane % 8 == row, named, -1)
    for s in range(4):
        chem_step(jnp.int32(24 + s))
        for n in range(4):
            r = s * 4 + n
            far_acc[r] = pair_sums([far_rows[r * 2 + k] for k in range(2)], far_cubes.at[r])
    pick = jnp.concatenate(
        [jnp.where(named == b, 1.0, 0.0) for b in range(BLOCKS)], 0
    ).astype(BF16)
    high, low = halves(far_acc[...].reshape(SLOTS * 8, BLOCK))
    far_all = mm(jnp.concatenate([pick, pick], 1), jnp.concatenate([high, low], 0))
    for s in range(4):
        chem_step(jnp.int32(28 + s))
        for n in range(8):
            b = s * 8 + n
            acc = near_acc[b] + far_all[b * 8 : b * 8 + 8]
            acc = acc * jnp.where(row < 4, factor[b : b + 1], 1.0)
            acc = acc + pltpu.roll(acc, 4, 0)
            at = pl.ds(b * BLOCK, BLOCK)
            accel[:, at] = (4.0 * width[b : b + 1]) * (pos[:, at] * acc[3:4] - acc[0:3])
    abund_all[:, 0:HALF] = state[0:SPECIES]
    abund_all[:, HALF : 2 * HALF] = state[SPECIES : 2 * SPECIES]
    for copy in first + second:
        copy.wait_send()


def deliver(density, accel, abund, dens_out, accel_out, abund_out, sems):
    pairs = ((abund, abund_out), (accel, accel_out), (density, dens_out))
    copies = [pltpu.make_async_copy(a, b, sems.at[i]) for i, (a, b) in enumerate(pairs)]
    for copy in copies:
        copy.start()
    for copy in copies:
        copy.wait()


def on_device(
    position,
    smoothing,
    mass,
    energy,
    species,
    neighbours,
    exports,
    imports,
    jac_inverse,
    rates,
    chem_steps,
    dense_slot,
):
    tile = (BLOCKS, BLOCK)
    vmem = pl.BlockSpec(memory_space=pltpu.VMEM)
    hbm = pl.BlockSpec(memory_space=pltpu.HBM)
    far = 2 * SLOTS
    sides = SLOTS // 2
    chem = (2 * SPECIES, HALF)
    given = (
        position,
        smoothing.reshape(tile),
        mass.reshape(tile),
        energy.reshape(tile),
        species,
        neighbours.T,
        exports.T,
        imports.T,
        jac_inverse,
        rates,
        chem_steps.reshape(tile),
        dense_slot.reshape(tile),
    )
    spaces = [pltpu.VMEM] * 5 + [pltpu.SMEM] * 3 + [pltpu.VMEM] * 4
    density, accel, abund = pl.pallas_call(
        kernel,
        out_shape=(
            pltpu.VMEM(tile, F32),
            pltpu.VMEM(position.shape, F32),
            pltpu.VMEM(species.shape, F32),
        ),
        in_specs=[hbm] * len(given),
        out_specs=(vmem, vmem, vmem),
        scratch_shapes=[space(x.shape, x.dtype) for space, x in zip(spaces, given)]
        + [
            pltpu.VMEM((BLOCKS, 8, BLOCK), F32),
            pltpu.VMEM((BLOCKS, 2 * BLOCK, 2 * BLOCK), BF16),
            pltpu.VMEM((BLOCKS, BLOCK, BLOCK), BF16),
            pltpu.VMEM((2, 8, BLOCK, BLOCK), BF16),
            pltpu.VMEM((2, NBR // 2, BLOCK, 2 * BLOCK), F32),
            pltpu.VMEM((2, NBR // 2, BLOCK, 2 * BLOCK), F32),
            pltpu.VMEM((sides, 4, 8, BLOCK), F32),
            pltpu.VMEM((sides, 4, 8, BLOCK), F32),
            pltpu.VMEM(tile, F32),
            pltpu.VMEM((sides, 4, BLOCK), F32),
            pltpu.VMEM((sides, 4, BLOCK), F32),
            pltpu.VMEM((BLOCKS, 16, BLOCK), BF16),
            pltpu.VMEM((far, 16, BLOCK), BF16),
            pltpu.VMEM((BLOCKS, NBR * BLOCK, BLOCK), F32),
            pltpu.VMEM((SLOTS, 2 * BLOCK, BLOCK), F32),
            pltpu.VMEM(tile, F32),
            pltpu.VMEM((SLOTS, BLOCK), F32),
            pltpu.VMEM((BLOCKS, 8, BLOCK), F32),
            pltpu.VMEM((SLOTS, 8, BLOCK), F32),
            pltpu.VMEM(tile, F32),
            pltpu.VMEM(chem, F32),
            pltpu.VMEM(chem, F32),
            pltpu.VMEM(chem, F32),
            pltpu.VMEM(chem, F32),
            pltpu.SemaphoreType.DMA((len(given),)),
        ]
        + [pltpu.SemaphoreType.DMA((sides,))] * 4,
        compiler_params=pltpu.CompilerParams(
            collective_id=0, has_side_effects=True, vmem_limit_bytes=24 << 20
        ),
        name="particle_step",
    )(*(pltpu.with_memory_space_constraint(x, pltpu.HBM) for x in given))
    density, accel, abund = pl.pallas_call(
        deliver,
        out_shape=(
            jax.ShapeDtypeStruct(tile, F32),
            jax.ShapeDtypeStruct(position.shape, F32),
            jax.ShapeDtypeStruct(species.shape, F32),
        ),
        in_specs=[vmem] * 3,
        out_specs=(hbm,) * 3,
        scratch_shapes=[pltpu.SemaphoreType.DMA((3,))],
        compiler_params=pltpu.CompilerParams(vmem_limit_bytes=1 << 20),
        name="deliver",
    )(density, accel, abund)
    return density.reshape(-1), accel, abund


def solution(mesh):
    flat = P(("dom", "sub"))
    wide = P(None, ("dom", "sub"))
    tall = P(("dom", "sub"), None)
    return jax.shard_map(
        on_device,
        mesh=mesh,
        in_specs=(wide, flat, flat, flat, wide, tall, tall, tall, P(), P(), flat, flat),
        out_specs=(flat, wide, wide),
        check_vma=False,
    )
```

```python
import functools

import jax
import jax.numpy as jnp
from jax import lax
from jax.experimental import pallas as pl
from jax.experimental.pallas import tpu as pltpu
from jax.sharding import PartitionSpec as P

BLOCK = 128
BLOCKS = 32
NBR = 4
SLOTS = 16
SPECIES = 12
S_LO = 4
SMAX = 32
HALF = BLOCKS * BLOCK // 2
FEAT = 48
GROUPS = 4
FIRST = 32
MESH = pl.DeviceIdType.MESH
F32 = jnp.float32
BF16 = jnp.bfloat16
HIGH = lax.Precision.HIGHEST

gamma_gas = 5.0 / 3.0
chem_tau = 0.5


def pieces(value):
    high = value.astype(BF16).astype(F32)
    rest = value - high
    middle = rest.astype(BF16).astype(F32)
    return high, middle, rest - middle


def halves(value):
    high = value.astype(BF16)
    return high, (value - high.astype(F32)).astype(BF16)


def mm(a, b):
    return jnp.dot(a, b, preferred_element_type=F32)


def source_features(fields):
    high, middle, low = pieces(fields)
    return jnp.concatenate([high, high, high, middle, middle, low], 0).T.astype(BF16)


def gradient_rows(fields, factor):
    row = lax.broadcasted_iota(jnp.int32, fields.shape, 0)
    both = jnp.where(row < 4, fields, pltpu.roll(fields, 4, 0))
    high, low = halves(both * jnp.where(row < 4, 1.0, factor))
    return jnp.concatenate([high, low], 0)


def distances(features, target, place):
    for k in range(0, len(features), 2):
        place[k // 2] = mm(jnp.concatenate(features[k : k + 2], 1), target)


def pair_terms(place, count, cubes, dens, row):
    total = None
    for k in range(count):
        for half in range(2):
            base = 1.0 / place[k, :, half * BLOCK : (half + 1) * BLOCK]
            squared = base * base
            at = (2 * k + half) * BLOCK
            cubes[at : at + BLOCK] = squared * base
            part = jnp.sum(squared.reshape(BLOCK // 8, 8, BLOCK), axis=0)
            total = part if total is None else total + part
    dens[pl.ds(row, 1)] = jnp.sum(total, axis=0, keepdims=True)


def pair_sums(rows, cubes):
    high, low = halves(cubes[...])
    lhs = jnp.concatenate(rows, 1)
    out = mm(lhs, high) + mm(lhs, low)
    return out[0:8] + out[8:16]


def spread(matrix):
    wide = 2 * SPECIES
    tall = jnp.concatenate([matrix, matrix], 0)
    full = jnp.concatenate([tall, tall], 1)
    same = (
        lax.broadcasted_iota(jnp.int32, (wide, wide), 0) // SPECIES
        == lax.broadcasted_iota(jnp.int32, (wide, wide), 1) // SPECIES
    )
    return jnp.where(same, full, 0.0)


def left_side(matrix):
    high, low = halves(matrix)
    blank = jnp.zeros((matrix.shape[0], 8), F32)
    high, low = high.astype(F32), low.astype(F32)
    return jnp.concatenate([high, blank, high, blank, low, blank], 1).astype(BF16)


def right_side(state):
    high, low = halves(jnp.concatenate([state, jnp.zeros((8, state.shape[1]), F32)], 0))
    return jnp.concatenate([high, low, high], 0)


def kernel(
    pos_in,
    width_in,
    mass_in,
    energy_in,
    species_in,
    neigh_in,
    exports_in,
    imports_in,
    jac_in,
    rates_in,
    steps_in,
    slot_in,
    density,
    accel,
    abund_all,
    pos,
    width,
    mass,
    energy,
    species,
    neigh,
    exports,
    imports,
    jac,
    rates,
    steps,
    slot,
    fields,
    targets,
    feats,
    far_feats,
    even,
    odd,
    stage,
    far_fields,
    factor,
    stage_factor,
    far_factor,
    rows,
    far_rows,
    near_cubes,
    far_cubes,
    near_dens,
    far_dens,
    near_acc,
    far_acc,
    root_mass,
    gain,
    limit,
    state,
    rate_in,
    load_sem,
    send_one,
    recv_one,
    send_two,
    recv_two,
):
    dom = lax.axis_index("dom")
    sub = lax.axis_index("sub")
    doms = lax.axis_size("dom")
    subs = lax.axis_size("sub")
    sides = [lax.rem(dom + doms - 1, doms), lax.rem(dom + 1, doms)]
    barrier = pltpu.get_barrier_semaphore()
    for side in sides:
        for q in range(subs):
            pl.semaphore_signal(barrier, inc=1, device_id=(side, q), device_id_type=MESH)

    pairs = {
        "pos": (pos_in, pos),
        "mass": (mass_in, mass),
        "imports": (imports_in, imports),
        "width": (width_in, width),
        "neigh": (neigh_in, neigh),
        "exports": (exports_in, exports),
        "jac": (jac_in, jac),
        "rates": (rates_in, rates),
        "energy": (energy_in, energy),
        "steps": (steps_in, steps),
        "slot": (slot_in, slot),
        "species": (species_in, species),
    }
    loads = {}
    for i, (name, (source, target)) in enumerate(pairs.items()):
        loads[name] = pltpu.make_async_copy(source, target, load_sem.at[i])
        loads[name].start()

    def exchange(sent, landed, send_sem, recv_sem):
        copies = []
        for e in range(2):
            for q in range(subs):
                copies.append(
                    pltpu.make_async_remote_copy(
                        src_ref=sent.at[e * subs + q],
                        dst_ref=landed.at[(1 - e) * subs + sub],
                        send_sem=send_sem.at[e * subs + q],
                        recv_sem=recv_sem.at[(1 - e) * subs + sub],
                        device_id=(sides[e], q),
                        device_id_type=MESH,
                    )
                )
        return copies

    def arrive(place, sent, landed, send_sem, recv_sem):
        pltpu.make_async_remote_copy(
            src_ref=sent.at[place],
            dst_ref=landed.at[place],
            send_sem=send_sem.at[place],
            recv_sem=recv_sem.at[place],
            device_id=(sides[0], 0),
            device_id_type=MESH,
        ).wait_recv()

    feats[...] = jnp.zeros_like(feats)
    targets[...] = jnp.zeros_like(targets)
    far_feats[...] = jnp.zeros_like(far_feats)
    loads["pos"].wait()
    loads["mass"].wait()
    root_mass[...] = 1.0 / jnp.sqrt(mass[...])

    def prepare(b, _):
        place = pos[:, pl.ds(pl.multiple_of(b * BLOCK, BLOCK), BLOCK)]
        weight = root_mass[pl.ds(b, 1)]
        fields[b, 0:3] = place * weight
        fields[b, 3:4] = weight
        fields[b, 4:5] = jnp.sum(place * place, axis=0, keepdims=True) * weight
        fields[b, 5:8] = jnp.zeros((3, BLOCK), F32)
        return 0

    lax.fori_loop(0, BLOCKS, prepare, 0, unroll=8)
    loads["imports"].wait()
    for r in range(SLOTS):
        for k in range(2):
            stage[r // 2, (r % 2) * 2 + k] = fields[imports[k, r]]
    loads["width"].wait()
    loads["neigh"].wait()
    loads["exports"].wait()
    loads["jac"].wait()
    loads["rates"].wait()
    pl.semaphore_wait(barrier, 2 * subs)
    first = exchange(stage, far_fields, send_one, recv_one)
    for copy in first:
        copy.start()

    def shape_block(b):
        place = pos[:, pl.ds(pl.multiple_of(b * BLOCK, BLOCK), BLOCK)]
        norm = jnp.sum(place * place, axis=0, keepdims=True)
        span = width[pl.ds(b, 1)]
        target = jnp.concatenate(
            [place * -2.0, span * span + norm, jnp.ones_like(norm), jnp.zeros((3, BLOCK), F32)], 0
        )
        high, middle, low = pieces(target)
        split = jnp.concatenate([high, middle, low, high, middle, high], 0).astype(BF16)
        targets[b, 0:FEAT, 0:BLOCK] = split
        targets[b, BLOCK : BLOCK + FEAT, BLOCK : 2 * BLOCK] = split
        feats[b, :, 0:FEAT] = source_features(fields[b])

    for b in range(FIRST):
        shape_block(b)
    jac_full = spread(jac[...])
    rate_full = spread(rates[...])
    both = jnp.dot(rates[...], jac[...], precision=HIGH, preferred_element_type=F32)
    left = left_side(jnp.concatenate([spread(both), jac_full], 0))
    left_first = left_side(rate_full)

    def fill(b, place):
        distances([feats[neigh[k, b]] for k in range(NBR)], targets[b], place)

    def drain(b, place):
        pair_terms(place, NBR // 2, near_cubes.at[b], near_dens, b)

    ring = [even.at[0], even.at[1], odd.at[0], odd.at[1]]
    fill(0, ring[0])
    fill(1, ring[1])
    for b in range(BLOCKS):
        if b + 2 < BLOCKS:
            fill(b + 2, ring[(b + 2) % 4])
        drain(b, ring[b % 4])
    for name in ("energy", "steps", "slot", "species"):
        loads[name].wait()

    def far_fill(i, place):
        q = lax.rem(sub + (0, 1, 3, 2)[i], subs)
        for e in range(2):
            arrive(e * subs + q, stage, far_fields, send_one, recv_one)
        for e in range(2):
            for k in range(4):
                far_feats[i % 2, e * 4 + k, :, 0:FEAT] = source_features(
                    far_fields[e * subs + q, k]
                )
            for x in range(2):
                parts = [far_feats[i % 2, e * 4 + 2 * x + k] for k in range(2)]
                target = targets[exports[x, e * subs + q]]
                distances(parts, target, place.at[e, pl.ds(x, 1)])

    def far_drain(i, place):
        q = lax.rem(sub + (0, 1, 3, 2)[i], subs)
        for e in range(2):
            for x in range(2):
                at = (e * subs + q) * 2 + x
                pair_terms(place.at[e, pl.ds(x, 1)], 1, far_cubes.at[at], far_dens, at)

    places = (odd, even)
    far_fill(0, places[0])
    for i in range(1, 4):
        far_fill(i, places[i % 2])
        far_drain(i - 1, places[(i - 1) % 2])
    far_drain(3, places[1])

    owner = lax.broadcasted_iota(jnp.int32, (BLOCKS, BLOCK), 0)
    total = near_dens[...]
    for r in range(SLOTS):
        total += jnp.where(owner == exports[r % 2, r // 2], far_dens[r : r + 1], 0.0)
    dens = total * width[...]
    density[...] = dens
    factor[...] = (gamma_gas - 1.0) * energy[...] / dens
    for r in range(SLOTS):
        for k in range(2):
            stage_factor[r // 2, pl.ds((r % 2) * 2 + k, 1)] = factor[pl.ds(imports[k, r], 1)]
    second = exchange(stage_factor, far_factor, send_two, recv_two)
    for copy in second:
        copy.start()
    gain_all = chem_tau * (dens / (dens + 1.0))
    most = jnp.where(slot[...] >= 0, steps[...], jnp.minimum(steps[...], S_LO)).astype(F32)
    for b in range(BLOCKS // 2):
        for h in range(2):
            block = b + h * (BLOCKS // 2)
            at = pl.ds(b * BLOCK, BLOCK)
            span = pl.ds(h * SPECIES, SPECIES)
            gain[span, at] = jnp.broadcast_to(gain_all[block : block + 1], (SPECIES, BLOCK))
            limit[span, at] = jnp.broadcast_to(most[block : block + 1], (SPECIES, BLOCK))
    state[0:SPECIES] = species[:, 0:HALF]
    state[SPECIES : 2 * SPECIES] = species[:, HALF : 2 * HALF]
    part = HALF // GROUPS
    for g in range(GROUPS):
        at = pl.ds(g * part, part)
        rate_in[:, at] = mm(left_first, right_side(state[:, at]))

    def rows_near(b, _):
        rows[b] = gradient_rows(fields[b], factor[pl.ds(b, 1)])
        return 0

    lax.fori_loop(0, BLOCKS, rows_near, 0, unroll=8)

    def chem_step(c):
        for g in range(GROUPS):
            at = pl.ds(g * part, part)
            abund = state[:, at]
            lift = gain[:, at]
            moved = (abund + lift) + lift * jnp.tanh(rate_in[:, at])
            out = mm(left, right_side(moved))
            rate_in[:, at] = out[: 2 * SPECIES]
            state[:, at] = jnp.where(limit[:, at] > c, out[2 * SPECIES :], abund)

    for c in range(SMAX // 2):
        chem_step(c)
        for b in (2 * c, 2 * c + 1):
            near_acc[b] = pair_sums([rows[neigh[k, b]] for k in range(NBR)], near_cubes.at[b])

    for c in range(16, 24):
        chem_step(c)
    for place in range(2 * subs):
        arrive(place, stage_factor, far_factor, send_two, recv_two)
    for j in range(2 * subs):
        for k in range(4):
            far_rows[j * 4 + k] = gradient_rows(far_fields[j, k], far_factor[j, k : k + 1])
    row = lax.broadcasted_iota(jnp.int32, (8, BLOCK), 0)
    lane = lax.broadcasted_iota(jnp.int32, (8, BLOCK), 1)
    named = jnp.zeros((8, BLOCK), jnp.int32)
    for r in range(SLOTS):
        named = jnp.where(lane // 8 == r, exports[r % 2, r // 2], named)
    named = jnp.where(lane % 8 == row, named, -1)
    for s in range(4):
        chem_step(24 + s)
        for n in range(4):
            r = s * 4 + n
            far_acc[r] = pair_sums([far_rows[r * 2 + k] for k in range(2)], far_cubes.at[r])
    pick = jnp.concatenate(
        [jnp.where(named == b, 1.0, 0.0) for b in range(BLOCKS)], 0
    ).astype(BF16)
    high, low = halves(far_acc[...].reshape(SLOTS * 8, BLOCK))
    far_all = mm(jnp.concatenate([pick, pick], 1), jnp.concatenate([high, low], 0))
    for s in range(4):
        chem_step(28 + s)
        for n in range(8):
            b = s * 8 + n
            acc = near_acc[b] + far_all[b * 8 : b * 8 + 8]
            acc = acc * jnp.where(row < 4, factor[b : b + 1], 1.0)
            acc = acc + pltpu.roll(acc, 4, 0)
            at = pl.ds(b * BLOCK, BLOCK)
            accel[:, at] = (4.0 * width[b : b + 1]) * (pos[:, at] * acc[3:4] - acc[0:3])
    abund_all[:, 0:HALF] = state[0:SPECIES]
    abund_all[:, HALF : 2 * HALF] = state[SPECIES : 2 * SPECIES]
    for copy in first + second:
        copy.wait_send()


def deliver(density, accel, abund, dens_out, accel_out, abund_out, sems):
    pairs = ((abund, abund_out), (accel, accel_out), (density, dens_out))
    copies = [pltpu.make_async_copy(a, b, sems.at[i]) for i, (a, b) in enumerate(pairs)]
    for copy in copies:
        copy.start()
    for copy in copies:
        copy.wait()


def on_device(
    position,
    smoothing,
    mass,
    energy,
    species,
    neighbours,
    exports,
    imports,
    jac_inverse,
    rates,
    chem_steps,
    dense_slot,
):
    tile = (BLOCKS, BLOCK)
    vmem = pl.BlockSpec(memory_space=pltpu.VMEM)
    hbm = pl.BlockSpec(memory_space=pltpu.HBM)
    far = 2 * SLOTS
    sides = SLOTS // 2
    chem = (2 * SPECIES, HALF)
    given = (
        position,
        smoothing.reshape(tile),
        mass.reshape(tile),
        energy.reshape(tile),
        species,
        neighbours.T,
        exports.T,
        imports.T,
        jac_inverse,
        rates,
        chem_steps.reshape(tile),
        dense_slot.reshape(tile),
    )
    spaces = [pltpu.VMEM] * 5 + [pltpu.SMEM] * 3 + [pltpu.VMEM] * 4
    density, accel, abund = pl.pallas_call(
        kernel,
        out_shape=(
            pltpu.VMEM(tile, F32),
            pltpu.VMEM(position.shape, F32),
            pltpu.VMEM(species.shape, F32),
        ),
        in_specs=[hbm] * len(given),
        out_specs=(vmem, vmem, vmem),
        scratch_shapes=[space(x.shape, x.dtype) for space, x in zip(spaces, given)]
        + [
            pltpu.VMEM((BLOCKS, 8, BLOCK), F32),
            pltpu.VMEM((BLOCKS, 2 * BLOCK, 2 * BLOCK), BF16),
            pltpu.VMEM((BLOCKS, BLOCK, BLOCK), BF16),
            pltpu.VMEM((2, 8, BLOCK, BLOCK), BF16),
            pltpu.VMEM((2, NBR // 2, BLOCK, 2 * BLOCK), F32),
            pltpu.VMEM((2, NBR // 2, BLOCK, 2 * BLOCK), F32),
            pltpu.VMEM((sides, 4, 8, BLOCK), F32),
            pltpu.VMEM((sides, 4, 8, BLOCK), F32),
            pltpu.VMEM(tile, F32),
            pltpu.VMEM((sides, 4, BLOCK), F32),
            pltpu.VMEM((sides, 4, BLOCK), F32),
            pltpu.VMEM((BLOCKS, 16, BLOCK), BF16),
            pltpu.VMEM((far, 16, BLOCK), BF16),
            pltpu.VMEM((BLOCKS, NBR * BLOCK, BLOCK), F32),
            pltpu.VMEM((SLOTS, 2 * BLOCK, BLOCK), F32),
            pltpu.VMEM(tile, F32),
            pltpu.VMEM((SLOTS, BLOCK), F32),
            pltpu.VMEM((BLOCKS, 8, BLOCK), F32),
            pltpu.VMEM((SLOTS, 8, BLOCK), F32),
            pltpu.VMEM(tile, F32),
            pltpu.VMEM(chem, F32),
            pltpu.VMEM(chem, F32),
            pltpu.VMEM(chem, F32),
            pltpu.VMEM(chem, F32),
            pltpu.SemaphoreType.DMA((len(given),)),
        ]
        + [pltpu.SemaphoreType.DMA((sides,))] * 4,
        compiler_params=pltpu.CompilerParams(
            collective_id=0, has_side_effects=True, vmem_limit_bytes=24 << 20
        ),
        name="particle_step",
    )(*(pltpu.with_memory_space_constraint(x, pltpu.HBM) for x in given))
    density, accel, abund = pl.pallas_call(
        deliver,
        out_shape=(
            jax.ShapeDtypeStruct(tile, F32),
            jax.ShapeDtypeStruct(position.shape, F32),
            jax.ShapeDtypeStruct(species.shape, F32),
        ),
        in_specs=[vmem] * 3,
        out_specs=(hbm,) * 3,
        scratch_shapes=[pltpu.SemaphoreType.DMA((3,))],
        compiler_params=pltpu.CompilerParams(vmem_limit_bytes=1 << 20),
        name="deliver",
    )(density, accel, abund)
    return density.reshape(-1), accel, abund


def solution(mesh):
    flat = P(("dom", "sub"))
    wide = P(None, ("dom", "sub"))
    tall = P(("dom", "sub"), None)
    return jax.shard_map(
        on_device,
        mesh=mesh,
        in_specs=(wide, flat, flat, flat, wide, tall, tall, tall, P(), P(), flat, flat),
        out_specs=(flat, wide, wide),
        check_vma=False,
    )
```

```python
import functools

import jax
import jax.numpy as jnp
from jax import lax
from jax.experimental import pallas as pl
from jax.experimental.pallas import tpu as pltpu
from jax.sharding import PartitionSpec as P

BLOCK = 128
BLOCKS = 32
NBR = 4
SLOTS = 16
SPECIES = 12
S_LO = 4
SMAX = 32
HALF = BLOCKS * BLOCK // 2
FEAT = 48
GROUPS = 4
FIRST = 32
MESH = pl.DeviceIdType.MESH
F32 = jnp.float32
BF16 = jnp.bfloat16
HIGH = lax.Precision.HIGHEST

gamma_gas = 5.0 / 3.0
chem_tau = 0.5


def pieces(value):
    high = value.astype(BF16).astype(F32)
    rest = value - high
    middle = rest.astype(BF16).astype(F32)
    return high, middle, rest - middle


def halves(value):
    high = value.astype(BF16)
    return high, (value - high.astype(F32)).astype(BF16)


def mm(a, b):
    return jnp.dot(a, b, preferred_element_type=F32)


def source_features(fields):
    high, middle, low = pieces(fields)
    return jnp.concatenate([high, high, high, middle, middle, low], 0).T.astype(BF16)


def gradient_rows(fields, factor):
    row = lax.broadcasted_iota(jnp.int32, fields.shape, 0)
    both = jnp.where(row < 4, fields, pltpu.roll(fields, 4, 0))
    high, low = halves(both * jnp.where(row < 4, 1.0, factor))
    return jnp.concatenate([high, low], 0)


def distances(features, target, place):
    for k in range(0, len(features), 2):
        place[k // 2] = mm(jnp.concatenate(features[k : k + 2], 1), target)


def pair_terms(place, count, cubes, dens, row):
    total = None
    for k in range(count):
        for half in range(2):
            base = 1.0 / place[k, :, half * BLOCK : (half + 1) * BLOCK]
            squared = base * base
            at = (2 * k + half) * BLOCK
            cubes[at : at + BLOCK] = squared * base
            part = jnp.sum(squared.reshape(BLOCK // 8, 8, BLOCK), axis=0)
            total = part if total is None else total + part
    dens[pl.ds(row, 1)] = jnp.sum(total, axis=0, keepdims=True)


def pair_sums(rows, cubes):
    high, low = halves(cubes[...])
    lhs = jnp.concatenate(rows, 1)
    out = mm(lhs, high) + mm(lhs, low)
    return out[0:8] + out[8:16]


def spread(matrix):
    wide = 2 * SPECIES
    tall = jnp.concatenate([matrix, matrix], 0)
    full = jnp.concatenate([tall, tall], 1)
    same = (
        lax.broadcasted_iota(jnp.int32, (wide, wide), 0) // SPECIES
        == lax.broadcasted_iota(jnp.int32, (wide, wide), 1) // SPECIES
    )
    return jnp.where(same, full, 0.0)


def left_side(matrix):
    high, low = halves(matrix)
    blank = jnp.zeros((matrix.shape[0], 8), F32)
    high, low = high.astype(F32), low.astype(F32)
    return jnp.concatenate([high, blank, high, blank, low, blank], 1).astype(BF16)


def right_side(state):
    high, low = halves(jnp.concatenate([state, jnp.zeros((8, state.shape[1]), F32)], 0))
    return jnp.concatenate([high, low, high], 0)


def kernel(
    pos_in,
    width_in,
    mass_in,
    energy_in,
    species_in,
    neigh_in,
    exports_in,
    imports_in,
    jac_in,
    rates_in,
    steps_in,
    slot_in,
    density,
    accel,
    abund_all,
    pos,
    width,
    mass,
    energy,
    species,
    neigh,
    exports,
    imports,
    jac,
    rates,
    steps,
    slot,
    fields,
    targets,
    feats,
    far_feats,
    even,
    odd,
    stage,
    far_fields,
    factor,
    stage_factor,
    far_factor,
    rows,
    far_rows,
    near_cubes,
    far_cubes,
    near_dens,
    far_dens,
    near_acc,
    far_acc,
    root_mass,
    gain,
    limit,
    state,
    rate_in,
    load_sem,
    send_one,
    recv_one,
    send_two,
    recv_two,
    ready,
):
    dom = lax.axis_index("dom")
    sub = lax.axis_index("sub")
    doms = lax.axis_size("dom")
    subs = lax.axis_size("sub")
    sides = [lax.rem(dom + doms - 1, doms), lax.rem(dom + 1, doms)]
    barrier = pltpu.get_barrier_semaphore()
    for q in range(subs):
        pl.semaphore_signal(barrier, inc=1, device_id=(sides[0], q), device_id_type=MESH)

    @pl.when(dom != doms - 1)
    def _():
        for q in range(subs):
            pl.semaphore_signal(barrier, inc=1, device_id=(sides[1], q), device_id_type=MESH)


    pairs = {
        "pos": (pos_in, pos),
        "mass": (mass_in, mass),
        "imports": (imports_in, imports),
        "width": (width_in, width),
        "neigh": (neigh_in, neigh),
        "exports": (exports_in, exports),
        "jac": (jac_in, jac),
        "rates": (rates_in, rates),
        "energy": (energy_in, energy),
        "steps": (steps_in, steps),
        "slot": (slot_in, slot),
        "species": (species_in, species),
    }
    loads = {}
    for i, (name, (source, target)) in enumerate(pairs.items()):
        loads[name] = pltpu.make_async_copy(source, target, load_sem.at[i])
        loads[name].start()

    def exchange(sent, landed, send_sem, recv_sem):
        copies = []
        for e in range(2):
            for q in range(subs):
                copies.append(
                    pltpu.make_async_remote_copy(
                        src_ref=sent.at[e * subs + q],
                        dst_ref=landed.at[(1 - e) * subs + sub],
                        send_sem=send_sem.at[e * subs + q],
                        recv_sem=recv_sem.at[(1 - e) * subs + sub],
                        device_id=(sides[e], q),
                        device_id_type=MESH,
                    )
                )
        return copies

    def arrive(place, sent, landed, send_sem, recv_sem):
        pltpu.make_async_remote_copy(
            src_ref=sent.at[place],
            dst_ref=landed.at[place],
            send_sem=send_sem.at[place],
            recv_sem=recv_sem.at[place],
            device_id=(sides[0], 0),
            device_id_type=MESH,
        ).wait_recv()

    feats[...] = jnp.zeros_like(feats)
    targets[...] = jnp.zeros_like(targets)
    far_feats[...] = jnp.zeros_like(far_feats)
    loads["pos"].wait()
    loads["mass"].wait()
    root_mass[...] = 1.0 / jnp.sqrt(mass[...])

    def prepare(b, _):
        place = pos[:, pl.ds(pl.multiple_of(b * BLOCK, BLOCK), BLOCK)]
        weight = root_mass[pl.ds(b, 1)]
        fields[b, 0:3] = place * weight
        fields[b, 3:4] = weight
        fields[b, 4:5] = jnp.sum(place * place, axis=0, keepdims=True) * weight
        fields[b, 5:8] = jnp.zeros((3, BLOCK), F32)
        return 0

    lax.fori_loop(0, BLOCKS, prepare, 0, unroll=8)
    loads["imports"].wait()
    for r in range(SLOTS):
        for k in range(2):
            stage[r // 2, (r % 2) * 2 + k] = fields[imports[k, r]]
    loads["width"].wait()
    loads["neigh"].wait()
    loads["exports"].wait()
    loads["jac"].wait()
    loads["rates"].wait()
    pl.semaphore_wait(barrier, jnp.where(dom == 0, subs, 2 * subs))

    @pl.when(dom == doms - 1)
    def _():
        for q in range(subs):
            pl.semaphore_signal(ready, inc=1, device_id=(sides[1], q), device_id_type=MESH)

    first = exchange(stage, far_fields, send_one, recv_one)
    for copy in first[subs:]:
        copy.start()

    @pl.when(dom != 0)
    def _():
        for copy in first[:subs]:
            copy.start()


    def shape_block(b):
        place = pos[:, pl.ds(pl.multiple_of(b * BLOCK, BLOCK), BLOCK)]
        norm = jnp.sum(place * place, axis=0, keepdims=True)
        span = width[pl.ds(b, 1)]
        target = jnp.concatenate(
            [place * -2.0, span * span + norm, jnp.ones_like(norm), jnp.zeros((3, BLOCK), F32)], 0
        )
        high, middle, low = pieces(target)
        split = jnp.concatenate([high, middle, low, high, middle, high], 0).astype(BF16)
        targets[b, 0:FEAT, 0:BLOCK] = split
        targets[b, BLOCK : BLOCK + FEAT, BLOCK : 2 * BLOCK] = split
        feats[b, :, 0:FEAT] = source_features(fields[b])

    for b in range(FIRST):
        shape_block(b)
    jac_full = spread(jac[...])
    rate_full = spread(rates[...])
    both = jnp.dot(rates[...], jac[...], precision=HIGH, preferred_element_type=F32)
    left = left_side(jnp.concatenate([spread(both), jac_full], 0))
    left_first = left_side(rate_full)

    def fill(b, place):
        distances([feats[neigh[k, b]] for k in range(NBR)], targets[b], place)

    def drain(b, place):
        pair_terms(place, NBR // 2, near_cubes.at[b], near_dens, b)

    ring = [even.at[0], even.at[1], odd.at[0], odd.at[1]]
    fill(0, ring[0])
    fill(1, ring[1])
    for b in range(BLOCKS):
        if b + 2 < BLOCKS:
            fill(b + 2, ring[(b + 2) % 4])
        drain(b, ring[b % 4])
    for name in ("energy", "steps", "slot", "species"):
        loads[name].wait()

    @pl.when(dom == 0)
    def _():
        pl.semaphore_wait(ready, subs)
        for copy in first[:subs]:
            copy.start()


    def far_fill(i, place):
        q = lax.rem(sub + (0, 1, 3, 2)[i], subs)
        for e in range(2):
            arrive(e * subs + q, stage, far_fields, send_one, recv_one)
        for e in range(2):
            for k in range(4):
                far_feats[i % 2, e * 4 + k, :, 0:FEAT] = source_features(
                    far_fields[e * subs + q, k]
                )
            for x in range(2):
                parts = [far_feats[i % 2, e * 4 + 2 * x + k] for k in range(2)]
                target = targets[exports[x, e * subs + q]]
                distances(parts, target, place.at[e, pl.ds(x, 1)])

    def far_drain(i, place):
        q = lax.rem(sub + (0, 1, 3, 2)[i], subs)
        for e in range(2):
            for x in range(2):
                at = (e * subs + q) * 2 + x
                pair_terms(place.at[e, pl.ds(x, 1)], 1, far_cubes.at[at], far_dens, at)

    places = (odd, even)
    far_fill(0, places[0])
    for i in range(1, 4):
        far_fill(i, places[i % 2])
        far_drain(i - 1, places[(i - 1) % 2])
    far_drain(3, places[1])

    owner = lax.broadcasted_iota(jnp.int32, (BLOCKS, BLOCK), 0)
    total = near_dens[...]
    for r in range(SLOTS):
        total += jnp.where(owner == exports[r % 2, r // 2], far_dens[r : r + 1], 0.0)
    dens = total * width[...]
    density[...] = dens
    factor[...] = (gamma_gas - 1.0) * energy[...] / dens
    for r in range(SLOTS):
        for k in range(2):
            stage_factor[r // 2, pl.ds((r % 2) * 2 + k, 1)] = factor[pl.ds(imports[k, r], 1)]
    second = exchange(stage_factor, far_factor, send_two, recv_two)
    for copy in second:
        copy.start()
    gain_all = chem_tau * (dens / (dens + 1.0))
    most = jnp.where(slot[...] >= 0, steps[...], jnp.minimum(steps[...], S_LO)).astype(F32)
    for b in range(BLOCKS // 2):
        for h in range(2):
            block = b + h * (BLOCKS // 2)
            at = pl.ds(b * BLOCK, BLOCK)
            span = pl.ds(h * SPECIES, SPECIES)
            gain[span, at] = jnp.broadcast_to(gain_all[block : block + 1], (SPECIES, BLOCK))
            limit[span, at] = jnp.broadcast_to(most[block : block + 1], (SPECIES, BLOCK))
    state[0:SPECIES] = species[:, 0:HALF]
    state[SPECIES : 2 * SPECIES] = species[:, HALF : 2 * HALF]
    part = HALF // GROUPS
    for g in range(GROUPS):
        at = pl.ds(g * part, part)
        rate_in[:, at] = mm(left_first, right_side(state[:, at]))

    def rows_near(b, _):
        rows[b] = gradient_rows(fields[b], factor[pl.ds(b, 1)])
        return 0

    lax.fori_loop(0, BLOCKS, rows_near, 0, unroll=8)

    def chem_step(c):
        for g in range(GROUPS):
            at = pl.ds(g * part, part)
            abund = state[:, at]
            lift = gain[:, at]
            moved = (abund + lift) + lift * jnp.tanh(rate_in[:, at])
            out = mm(left, right_side(moved))
            rate_in[:, at] = out[: 2 * SPECIES]
            state[:, at] = jnp.where(limit[:, at] > c, out[2 * SPECIES :], abund)

    for c in range(SMAX // 2):
        chem_step(c)
        for b in (2 * c, 2 * c + 1):
            near_acc[b] = pair_sums([rows[neigh[k, b]] for k in range(NBR)], near_cubes.at[b])

    for c in range(16, 24):
        chem_step(c)
    for place in range(2 * subs):
        arrive(place, stage_factor, far_factor, send_two, recv_two)
    for j in range(2 * subs):
        for k in range(4):
            far_rows[j * 4 + k] = gradient_rows(far_fields[j, k], far_factor[j, k : k + 1])
    row = lax.broadcasted_iota(jnp.int32, (8, BLOCK), 0)
    lane = lax.broadcasted_iota(jnp.int32, (8, BLOCK), 1)
    named = jnp.zeros((8, BLOCK), jnp.int32)
    for r in range(SLOTS):
        named = jnp.where(lane // 8 == r, exports[r % 2, r // 2], named)
    named = jnp.where(lane % 8 == row, named, -1)
    for s in range(4):
        chem_step(24 + s)
        for n in range(4):
            r = s * 4 + n
            far_acc[r] = pair_sums([far_rows[r * 2 + k] for k in range(2)], far_cubes.at[r])
    pick = jnp.concatenate(
        [jnp.where(named == b, 1.0, 0.0) for b in range(BLOCKS)], 0
    ).astype(BF16)
    high, low = halves(far_acc[...].reshape(SLOTS * 8, BLOCK))
    far_all = mm(jnp.concatenate([pick, pick], 1), jnp.concatenate([high, low], 0))
    for s in range(4):
        chem_step(28 + s)
        for n in range(8):
            b = s * 8 + n
            acc = near_acc[b] + far_all[b * 8 : b * 8 + 8]
            acc = acc * jnp.where(row < 4, factor[b : b + 1], 1.0)
            acc = acc + pltpu.roll(acc, 4, 0)
            at = pl.ds(b * BLOCK, BLOCK)
            accel[:, at] = (4.0 * width[b : b + 1]) * (pos[:, at] * acc[3:4] - acc[0:3])
    abund_all[:, 0:HALF] = state[0:SPECIES]
    abund_all[:, HALF : 2 * HALF] = state[SPECIES : 2 * SPECIES]
    for copy in first + second:
        copy.wait_send()


def deliver(density, accel, abund, dens_out, accel_out, abund_out, sems):
    pairs = ((abund, abund_out), (accel, accel_out), (density, dens_out))
    copies = [pltpu.make_async_copy(a, b, sems.at[i]) for i, (a, b) in enumerate(pairs)]
    for copy in copies:
        copy.start()
    for copy in copies:
        copy.wait()


def on_device(
    position,
    smoothing,
    mass,
    energy,
    species,
    neighbours,
    exports,
    imports,
    jac_inverse,
    rates,
    chem_steps,
    dense_slot,
):
    tile = (BLOCKS, BLOCK)
    vmem = pl.BlockSpec(memory_space=pltpu.VMEM)
    hbm = pl.BlockSpec(memory_space=pltpu.HBM)
    far = 2 * SLOTS
    sides = SLOTS // 2
    chem = (2 * SPECIES, HALF)
    given = (
        position,
        smoothing.reshape(tile),
        mass.reshape(tile),
        energy.reshape(tile),
        species,
        neighbours.T,
        exports.T,
        imports.T,
        jac_inverse,
        rates,
        chem_steps.reshape(tile),
        dense_slot.reshape(tile),
    )
    spaces = [pltpu.VMEM] * 5 + [pltpu.SMEM] * 3 + [pltpu.VMEM] * 4
    density, accel, abund = pl.pallas_call(
        kernel,
        out_shape=(
            pltpu.VMEM(tile, F32),
            pltpu.VMEM(position.shape, F32),
            pltpu.VMEM(species.shape, F32),
        ),
        in_specs=[hbm] * len(given),
        out_specs=(vmem, vmem, vmem),
        scratch_shapes=[space(x.shape, x.dtype) for space, x in zip(spaces, given)]
        + [
            pltpu.VMEM((BLOCKS, 8, BLOCK), F32),
            pltpu.VMEM((BLOCKS, 2 * BLOCK, 2 * BLOCK), BF16),
            pltpu.VMEM((BLOCKS, BLOCK, BLOCK), BF16),
            pltpu.VMEM((2, 8, BLOCK, BLOCK), BF16),
            pltpu.VMEM((2, NBR // 2, BLOCK, 2 * BLOCK), F32),
            pltpu.VMEM((2, NBR // 2, BLOCK, 2 * BLOCK), F32),
            pltpu.VMEM((sides, 4, 8, BLOCK), F32),
            pltpu.VMEM((sides, 4, 8, BLOCK), F32),
            pltpu.VMEM(tile, F32),
            pltpu.VMEM((sides, 4, BLOCK), F32),
            pltpu.VMEM((sides, 4, BLOCK), F32),
            pltpu.VMEM((BLOCKS, 16, BLOCK), BF16),
            pltpu.VMEM((far, 16, BLOCK), BF16),
            pltpu.VMEM((BLOCKS, NBR * BLOCK, BLOCK), F32),
            pltpu.VMEM((SLOTS, 2 * BLOCK, BLOCK), F32),
            pltpu.VMEM(tile, F32),
            pltpu.VMEM((SLOTS, BLOCK), F32),
            pltpu.VMEM((BLOCKS, 8, BLOCK), F32),
            pltpu.VMEM((SLOTS, 8, BLOCK), F32),
            pltpu.VMEM(tile, F32),
            pltpu.VMEM(chem, F32),
            pltpu.VMEM(chem, F32),
            pltpu.VMEM(chem, F32),
            pltpu.VMEM(chem, F32),
            pltpu.SemaphoreType.DMA((len(given),)),
        ]
        + [pltpu.SemaphoreType.DMA((sides,))] * 4
        + [pltpu.SemaphoreType.REGULAR],
        compiler_params=pltpu.CompilerParams(
            collective_id=0, has_side_effects=True, vmem_limit_bytes=24 << 20
        ),
        name="particle_step",
    )(*(pltpu.with_memory_space_constraint(x, pltpu.HBM) for x in given))
    density, accel, abund = pl.pallas_call(
        deliver,
        out_shape=(
            jax.ShapeDtypeStruct(tile, F32),
            jax.ShapeDtypeStruct(position.shape, F32),
            jax.ShapeDtypeStruct(species.shape, F32),
        ),
        in_specs=[vmem] * 3,
        out_specs=(hbm,) * 3,
        scratch_shapes=[pltpu.SemaphoreType.DMA((3,))],
        compiler_params=pltpu.CompilerParams(vmem_limit_bytes=1 << 20),
        name="deliver",
    )(density, accel, abund)
    return density.reshape(-1), accel, abund


def solution(mesh):
    flat = P(("dom", "sub"))
    wide = P(None, ("dom", "sub"))
    tall = P(("dom", "sub"), None)
    return jax.shard_map(
        on_device,
        mesh=mesh,
        in_specs=(wide, flat, flat, flat, wide, tall, tall, tall, P(), P(), flat, flat),
        out_specs=(flat, wide, wide),
        check_vma=False,
    )
```

```python
import functools

import jax
import jax.numpy as jnp
from jax import lax
from jax.experimental import pallas as pl
from jax.experimental.pallas import tpu as pltpu
from jax.sharding import PartitionSpec as P

BLOCK = 128
BLOCKS = 32
NBR = 4
SLOTS = 16
SPECIES = 12
S_LO = 4
SMAX = 32
HALF = BLOCKS * BLOCK // 2
FEAT = 48
GROUPS = 4
SPLIT = 24
FIRST = 32
MESH = pl.DeviceIdType.MESH
F32 = jnp.float32
BF16 = jnp.bfloat16
HIGH = lax.Precision.HIGHEST

gamma_gas = 5.0 / 3.0
chem_tau = 0.5


def pieces(value):
    high = value.astype(BF16).astype(F32)
    rest = value - high
    middle = rest.astype(BF16).astype(F32)
    return high, middle, rest - middle


def halves(value):
    high = value.astype(BF16)
    return high, (value - high.astype(F32)).astype(BF16)


def mm(a, b):
    return jnp.dot(a, b, preferred_element_type=F32)


def source_features(fields):
    high, middle, low = pieces(fields)
    return jnp.concatenate([high, high, high, middle, middle, low], 0).T.astype(BF16)


def weighted(place, weight):
    norm = jnp.sum(place * place, axis=0, keepdims=True)
    return jnp.concatenate(
        [place * weight, weight, norm * weight, jnp.zeros((3, BLOCK), F32)], 0
    )


def gradient_rows(fields, factor):
    row = lax.broadcasted_iota(jnp.int32, fields.shape, 0)
    both = jnp.where(row < 4, fields, pltpu.roll(fields, 4, 0))
    high, low = halves(both * jnp.where(row < 4, 1.0, factor))
    return jnp.concatenate([high, low], 0)


def distances(features, target, place):
    for k in range(0, len(features), 2):
        place[k // 2] = mm(jnp.concatenate(features[k : k + 2], 1), target)


def pair_terms(place, count, cubes, dens, row):
    total = None
    for k in range(count):
        for half in range(2):
            base = 1.0 / place[k, :, half * BLOCK : (half + 1) * BLOCK]
            squared = base * base
            at = (2 * k + half) * BLOCK
            cubes[at : at + BLOCK] = squared * base
            part = jnp.sum(squared.reshape(BLOCK // 8, 8, BLOCK), axis=0)
            total = part if total is None else total + part
    dens[pl.ds(row, 1)] = jnp.sum(total, axis=0, keepdims=True)


def pair_sums(rows, cubes):
    high, low = halves(cubes[...])
    lhs = jnp.concatenate(rows, 1)
    out = mm(lhs, high) + mm(lhs, low)
    return out[0:8] + out[8:16]


def spread(matrix):
    wide = 2 * SPECIES
    tall = jnp.concatenate([matrix, matrix], 0)
    full = jnp.concatenate([tall, tall], 1)
    same = (
        lax.broadcasted_iota(jnp.int32, (wide, wide), 0) // SPECIES
        == lax.broadcasted_iota(jnp.int32, (wide, wide), 1) // SPECIES
    )
    return jnp.where(same, full, 0.0)


def left_side(matrix):
    high, low = halves(matrix)
    blank = jnp.zeros((matrix.shape[0], 8), F32)
    high, low = high.astype(F32), low.astype(F32)
    return jnp.concatenate([high, blank, high, blank, low, blank], 1).astype(BF16)


def right_side(state):
    high, low = halves(jnp.concatenate([state, jnp.zeros((8, state.shape[1]), F32)], 0))
    return jnp.concatenate([high, low, high], 0)


def kernel(
    pos_in,
    width_in,
    mass_in,
    energy_in,
    species_in,
    neigh_in,
    exports_in,
    imports_in,
    jac_in,
    rates_in,
    steps_in,
    slot_in,
    density,
    accel,
    abund_all,
    pos,
    width,
    mass,
    energy,
    species,
    neigh,
    exports,
    imports,
    jac,
    rates,
    steps,
    slot,
    fields,
    targets,
    feats,
    far_feats,
    even,
    odd,
    far_ring,
    raw,
    stage,
    far_raw,
    far_fields,
    factor,
    stage_factor,
    far_factor,
    rows,
    far_rows,
    near_cubes,
    far_cubes,
    near_dens,
    far_dens,
    near_acc,
    far_acc,
    root_mass,
    gain,
    limit,
    state,
    rate_in,
    load_sem,
    send_one,
    recv_one,
    send_two,
    recv_two,
):
    dom = lax.axis_index("dom")
    sub = lax.axis_index("sub")
    doms = lax.axis_size("dom")
    subs = lax.axis_size("sub")
    sides = [lax.rem(dom + doms - 1, doms), lax.rem(dom + 1, doms)]
    barrier = pltpu.get_barrier_semaphore()
    for side in sides:
        for q in range(subs):
            pl.semaphore_signal(barrier, inc=1, device_id=(side, q), device_id_type=MESH)

    pairs = {
        "pos": (pos_in, pos),
        "mass": (mass_in, mass),
        "imports": (imports_in, imports),
        "width": (width_in, width),
        "neigh": (neigh_in, neigh),
        "exports": (exports_in, exports),
        "jac": (jac_in, jac),
        "rates": (rates_in, rates),
        "energy": (energy_in, energy),
        "steps": (steps_in, steps),
        "slot": (slot_in, slot),
        "species": (species_in, species),
    }
    loads = {}
    for i, (name, (source, target)) in enumerate(pairs.items()):
        loads[name] = pltpu.make_async_copy(source, target, load_sem.at[i])
        loads[name].start()

    def exchange(sent, landed, send_sem, recv_sem):
        copies = []
        for e in range(2):
            for q in range(subs):
                copies.append(
                    pltpu.make_async_remote_copy(
                        src_ref=sent.at[e * subs + q],
                        dst_ref=landed.at[(1 - e) * subs + sub],
                        send_sem=send_sem.at[e * subs + q],
                        recv_sem=recv_sem.at[(1 - e) * subs + sub],
                        device_id=(sides[e], q),
                        device_id_type=MESH,
                    )
                )
        return copies

    def arrive(place, sent, landed, send_sem, recv_sem):
        pltpu.make_async_remote_copy(
            src_ref=sent.at[place],
            dst_ref=landed.at[place],
            send_sem=send_sem.at[place],
            recv_sem=recv_sem.at[place],
            device_id=(sides[0], 0),
            device_id_type=MESH,
        ).wait_recv()

    feats[...] = jnp.zeros_like(feats)
    targets[...] = jnp.zeros_like(targets)
    far_feats[...] = jnp.zeros_like(far_feats)
    loads["pos"].wait()
    loads["mass"].wait()
    root_mass[...] = 1.0 / jnp.sqrt(mass[...])

    def prepare(b, _):
        place = pos[:, pl.ds(pl.multiple_of(b * BLOCK, BLOCK), BLOCK)]
        raw[b, 0:3] = place
        raw[b, 3:4] = root_mass[pl.ds(b, 1)]
        return 0

    lax.fori_loop(0, BLOCKS, prepare, 0, unroll=8)
    loads["imports"].wait()
    for r in range(SLOTS):
        for k in range(2):
            stage[r // 2, (r % 2) * 2 + k] = raw[imports[k, r]]
    loads["width"].wait()
    loads["neigh"].wait()
    loads["exports"].wait()
    loads["jac"].wait()
    loads["rates"].wait()
    pl.semaphore_wait(barrier, 2 * subs)
    first = exchange(stage, far_raw, send_one, recv_one)
    for copy in first:
        copy.start()

    def shape_block(b):
        place = pos[:, pl.ds(pl.multiple_of(b * BLOCK, BLOCK), BLOCK)]
        norm = jnp.sum(place * place, axis=0, keepdims=True)
        span = width[pl.ds(b, 1)]
        target = jnp.concatenate(
            [place * -2.0, span * span + norm, jnp.ones_like(norm), jnp.zeros((3, BLOCK), F32)], 0
        )
        high, middle, low = pieces(target)
        split = jnp.concatenate([high, middle, low, high, middle, high], 0).astype(BF16)
        targets[b, 0:FEAT, 0:BLOCK] = split
        targets[b, BLOCK : BLOCK + FEAT, BLOCK : 2 * BLOCK] = split
        full = weighted(place, root_mass[pl.ds(b, 1)])
        fields[b] = full
        feats[b, :, 0:FEAT] = source_features(full)

    for b in range(FIRST):
        shape_block(b)
    jac_full = spread(jac[...])
    rate_full = spread(rates[...])
    both = jnp.dot(rates[...], jac[...], precision=HIGH, preferred_element_type=F32)
    left = left_side(jnp.concatenate([spread(both), jac_full], 0))
    left_first = left_side(rate_full)

    def fill(b, place):
        distances([feats[neigh[k, b]] for k in range(NBR)], targets[b], place)

    def drain(b, place):
        pair_terms(place, NBR // 2, near_cubes.at[b], near_dens, b)

    ring = [even.at[0], even.at[1], odd.at[0], odd.at[1]]
    fill(0, ring[0])
    fill(1, ring[1])
    for b in range(BLOCKS):
        if b + 2 < BLOCKS:
            fill(b + 2, ring[(b + 2) % 4])
        drain(b, ring[b % 4])
    for name in ("energy", "steps", "slot", "species"):
        loads[name].wait()

    early = jnp.where(dom == 0, 1, 0)
    order = []
    for e in (early, 1 - early):
        for d in (0, 1, 3, 2):
            order.append(e * subs + lax.rem(sub + d, subs))

    def far_fill(i):
        place = order[i]
        for k in range(4):
            full = weighted(far_raw[place, k, 0:3], far_raw[place, k, 3:4])
            far_fields[place, k] = full
            far_feats[i * 4 + k, :, 0:FEAT] = source_features(full)
        for x in range(2):
            parts = [far_feats[i * 4 + 2 * x + k] for k in range(2)]
            distances(parts, targets[exports[x, place]], far_ring.at[pl.ds(2 * i + x, 1)])

    def far_drain(i):
        for x in range(2):
            at = order[i] * 2 + x
            pair_terms(far_ring.at[pl.ds(2 * i + x, 1)], 1, far_cubes.at[at], far_dens, at)

    before = ()
    for group in ((0, 1, 2, 3), (4, 5), (6,), (7,)):
        for i in group:
            arrive(order[i], stage, far_raw, send_one, recv_one)
        for i in group:
            far_fill(i)
        for i in before:
            far_drain(i)
        before = group
    for i in before:
        far_drain(i)

    owner = lax.broadcasted_iota(jnp.int32, (BLOCKS, BLOCK), 0)
    total = near_dens[...]
    for r in range(SLOTS):
        total += jnp.where(owner == exports[r % 2, r // 2], far_dens[r : r + 1], 0.0)
    dens = total * width[...]
    density[...] = dens
    factor[...] = (gamma_gas - 1.0) * energy[...] / dens
    for r in range(SLOTS):
        for k in range(2):
            stage_factor[r // 2, pl.ds((r % 2) * 2 + k, 1)] = factor[pl.ds(imports[k, r], 1)]
    second = exchange(stage_factor, far_factor, send_two, recv_two)
    for copy in second:
        copy.start()
    gain_all = chem_tau * (dens / (dens + 1.0))
    most = jnp.where(slot[...] >= 0, steps[...], jnp.minimum(steps[...], S_LO)).astype(F32)
    for b in range(BLOCKS // 2):
        for h in range(2):
            block = b + h * (BLOCKS // 2)
            at = pl.ds(b * BLOCK, BLOCK)
            span = pl.ds(h * SPECIES, SPECIES)
            gain[span, at] = jnp.broadcast_to(gain_all[block : block + 1], (SPECIES, BLOCK))
            limit[span, at] = jnp.broadcast_to(most[block : block + 1], (SPECIES, BLOCK))
    state[0:SPECIES] = species[:, 0:HALF]
    state[SPECIES : 2 * SPECIES] = species[:, HALF : 2 * HALF]
    part = HALF // GROUPS
    for g in range(GROUPS):
        at = pl.ds(g * part, part)
        rate_in[:, at] = mm(left_first, right_side(state[:, at]))

    def rows_near(b, _):
        rows[b] = gradient_rows(fields[b], factor[pl.ds(b, 1)])
        return 0

    lax.fori_loop(0, BLOCKS, rows_near, 0, unroll=8)

    def chem_step(c):
        for g in range(GROUPS):
            at = pl.ds(g * part, part)
            abund = state[:, at]
            lift = gain[:, at]
            moved = (abund + lift) + lift * jnp.tanh(rate_in[:, at])
            out = mm(left, right_side(moved))
            rate_in[:, at] = out[: 2 * SPECIES]
            state[:, at] = jnp.where(limit[:, at] > c, out[2 * SPECIES :], abund)

    for c in range(SMAX // 2):
        chem_step(c)
        for b in (2 * c, 2 * c + 1):
            near_acc[b] = pair_sums([rows[neigh[k, b]] for k in range(NBR)], near_cubes.at[b])

    row = lax.broadcasted_iota(jnp.int32, (8, BLOCK), 0)
    lane = lax.broadcasted_iota(jnp.int32, (8, BLOCK), 1)
    named = jnp.zeros((8, BLOCK), jnp.int32)
    for r in range(SLOTS):
        named = jnp.where(lane // 8 == r, exports[r % 2, r // 2], named)
    named = jnp.where(lane % 8 == row, named, -1)
    pick = jnp.concatenate(
        [jnp.where(named == b, 1.0, 0.0) for b in range(BLOCKS)], 0
    ).astype(BF16)
    for c in range(16, SPLIT):
        chem_step(c)

    def rows_far(group):
        for i in group:
            arrive(order[i], stage_factor, far_factor, send_two, recv_two)
        for i in group:
            place = order[i]
            for k in range(4):
                far_rows[i * 4 + k] = gradient_rows(
                    far_fields[place, k], far_factor[place, pl.ds(k, 1)]
                )

    def sums_far(i, x):
        at = order[i] * 2 + x
        parts = [far_rows[i * 4 + 2 * x + k] for k in range(2)]
        far_acc[at] = pair_sums(parts, far_cubes.at[at])

    rows_far((0, 1, 2, 3))
    slots = [(i, x) for i in range(4) for x in range(2)]
    for c in range(SPLIT, SMAX):
        chem_step(c)
        n = 8 // (SMAX - SPLIT)
        for i, x in slots[(c - SPLIT) * n : (c - SPLIT + 1) * n]:
            sums_far(i, x)
    rows_far((4, 5, 6, 7))
    for i in range(4, 8):
        for x in range(2):
            sums_far(i, x)
    high, low = halves(far_acc[...].reshape(SLOTS * 8, BLOCK))
    far_all = mm(jnp.concatenate([pick, pick], 1), jnp.concatenate([high, low], 0))
    for b in range(BLOCKS):
        acc = near_acc[b] + far_all[b * 8 : b * 8 + 8]
        acc = acc * jnp.where(row < 4, factor[b : b + 1], 1.0)
        acc = acc + pltpu.roll(acc, 4, 0)
        at = pl.ds(b * BLOCK, BLOCK)
        accel[:, at] = (4.0 * width[b : b + 1]) * (pos[:, at] * acc[3:4] - acc[0:3])
    abund_all[:, 0:HALF] = state[0:SPECIES]
    abund_all[:, HALF : 2 * HALF] = state[SPECIES : 2 * SPECIES]
    for copy in first + second:
        copy.wait_send()


def deliver(density, accel, abund, dens_out, accel_out, abund_out, sems):
    pairs = ((abund, abund_out), (accel, accel_out), (density, dens_out))
    copies = [pltpu.make_async_copy(a, b, sems.at[i]) for i, (a, b) in enumerate(pairs)]
    for copy in copies:
        copy.start()
    for copy in copies:
        copy.wait()


def on_device(
    position,
    smoothing,
    mass,
    energy,
    species,
    neighbours,
    exports,
    imports,
    jac_inverse,
    rates,
    chem_steps,
    dense_slot,
):
    tile = (BLOCKS, BLOCK)
    vmem = pl.BlockSpec(memory_space=pltpu.VMEM)
    hbm = pl.BlockSpec(memory_space=pltpu.HBM)
    far = 2 * SLOTS
    sides = SLOTS // 2
    chem = (2 * SPECIES, HALF)
    given = (
        position,
        smoothing.reshape(tile),
        mass.reshape(tile),
        energy.reshape(tile),
        species,
        neighbours.T,
        exports.T,
        imports.T,
        jac_inverse,
        rates,
        chem_steps.reshape(tile),
        dense_slot.reshape(tile),
    )
    spaces = [pltpu.VMEM] * 5 + [pltpu.SMEM] * 3 + [pltpu.VMEM] * 4
    density, accel, abund = pl.pallas_call(
        kernel,
        out_shape=(
            pltpu.VMEM(tile, F32),
            pltpu.VMEM(position.shape, F32),
            pltpu.VMEM(species.shape, F32),
        ),
        in_specs=[hbm] * len(given),
        out_specs=(vmem, vmem, vmem),
        scratch_shapes=[space(x.shape, x.dtype) for space, x in zip(spaces, given)]
        + [
            pltpu.VMEM((BLOCKS, 8, BLOCK), F32),
            pltpu.VMEM((BLOCKS, 2 * BLOCK, 2 * BLOCK), BF16),
            pltpu.VMEM((BLOCKS, BLOCK, BLOCK), BF16),
            pltpu.VMEM((far, BLOCK, BLOCK), BF16),
            pltpu.VMEM((2, NBR // 2, BLOCK, 2 * BLOCK), F32),
            pltpu.VMEM((2, NBR // 2, BLOCK, 2 * BLOCK), F32),
            pltpu.VMEM((SLOTS, BLOCK, 2 * BLOCK), F32),
            pltpu.VMEM((BLOCKS, 4, BLOCK), F32),
            pltpu.VMEM((sides, 4, 4, BLOCK), F32),
            pltpu.VMEM((sides, 4, 4, BLOCK), F32),
            pltpu.VMEM((sides, 4, 8, BLOCK), F32),
            pltpu.VMEM(tile, F32),
            pltpu.VMEM((sides, 4, BLOCK), F32),
            pltpu.VMEM((sides, 4, BLOCK), F32),
            pltpu.VMEM((BLOCKS, 16, BLOCK), BF16),
            pltpu.VMEM((far, 16, BLOCK), BF16),
            pltpu.VMEM((BLOCKS, NBR * BLOCK, BLOCK), F32),
            pltpu.VMEM((SLOTS, 2 * BLOCK, BLOCK), F32),
            pltpu.VMEM(tile, F32),
            pltpu.VMEM((SLOTS, BLOCK), F32),
            pltpu.VMEM((BLOCKS, 8, BLOCK), F32),
            pltpu.VMEM((SLOTS, 8, BLOCK), F32),
            pltpu.VMEM(tile, F32),
            pltpu.VMEM(chem, F32),
            pltpu.VMEM(chem, F32),
            pltpu.VMEM(chem, F32),
            pltpu.VMEM(chem, F32),
            pltpu.SemaphoreType.DMA((len(given),)),
        ]
        + [pltpu.SemaphoreType.DMA((sides,))] * 4,
        compiler_params=pltpu.CompilerParams(
            collective_id=0, has_side_effects=True, vmem_limit_bytes=24 << 20
        ),
        name="particle_step",
    )(*(pltpu.with_memory_space_constraint(x, pltpu.HBM) for x in given))
    density, accel, abund = pl.pallas_call(
        deliver,
        out_shape=(
            jax.ShapeDtypeStruct(tile, F32),
            jax.ShapeDtypeStruct(position.shape, F32),
            jax.ShapeDtypeStruct(species.shape, F32),
        ),
        in_specs=[vmem] * 3,
        out_specs=(hbm,) * 3,
        scratch_shapes=[pltpu.SemaphoreType.DMA((3,))],
        compiler_params=pltpu.CompilerParams(vmem_limit_bytes=1 << 20),
        name="deliver",
    )(density, accel, abund)
    return density.reshape(-1), accel, abund


def solution(mesh):
    flat = P(("dom", "sub"))
    wide = P(None, ("dom", "sub"))
    tall = P(("dom", "sub"), None)
    return jax.shard_map(
        on_device,
        mesh=mesh,
        in_specs=(wide, flat, flat, flat, wide, tall, tall, tall, P(), P(), flat, flat),
        out_specs=(flat, wide, wide),
        check_vma=False,
    )
```

```python
import functools

import jax
import jax.numpy as jnp
from jax import lax
from jax.experimental import pallas as pl
from jax.experimental.pallas import tpu as pltpu
from jax.sharding import PartitionSpec as P

BLOCK = 128
BLOCKS = 32
NBR = 4
SLOTS = 16
SPECIES = 12
S_LO = 4
SMAX = 32
HALF = BLOCKS * BLOCK // 2
FEAT = 48
GROUPS = 4
SPLIT = 24
FIRST = 32
MESH = pl.DeviceIdType.MESH
F32 = jnp.float32
BF16 = jnp.bfloat16
HIGH = lax.Precision.HIGHEST

gamma_gas = 5.0 / 3.0
chem_tau = 0.5


def pieces(value):
    high = value.astype(BF16).astype(F32)
    rest = value - high
    middle = rest.astype(BF16).astype(F32)
    return high, middle, rest - middle


def halves(value):
    high = value.astype(BF16)
    return high, (value - high.astype(F32)).astype(BF16)


def mm(a, b):
    return jnp.dot(a, b, preferred_element_type=F32)


def source_features(fields):
    high, middle, low = pieces(fields)
    return jnp.concatenate([high, high, high, middle, middle, low], 0).T.astype(BF16)


def weighted(place, weight):
    norm = jnp.sum(place * place, axis=0, keepdims=True)
    return jnp.concatenate(
        [place * weight, weight, norm * weight, jnp.zeros((3, BLOCK), F32)], 0
    )


def gradient_rows(fields, factor):
    row = lax.broadcasted_iota(jnp.int32, fields.shape, 0)
    both = jnp.where(row < 4, fields, pltpu.roll(fields, 4, 0))
    high, low = halves(both * jnp.where(row < 4, 1.0, factor))
    return jnp.concatenate([high, low], 0)


def distances(features, target, place):
    for k in range(0, len(features), 2):
        place[k // 2] = mm(jnp.concatenate(features[k : k + 2], 1), target)


def pair_terms(place, count, cubes, dens, row):
    total = None
    for k in range(count):
        for half in range(2):
            base = 1.0 / place[k, :, half * BLOCK : (half + 1) * BLOCK]
            squared = base * base
            at = (2 * k + half) * BLOCK
            cubes[at : at + BLOCK] = squared * base
            part = jnp.sum(squared.reshape(BLOCK // 8, 8, BLOCK), axis=0)
            total = part if total is None else total + part
    dens[pl.ds(row, 1)] = jnp.sum(total, axis=0, keepdims=True)


def pair_sums(rows, cubes):
    high, low = halves(cubes[...])
    lhs = jnp.concatenate(rows, 1)
    out = mm(lhs, high) + mm(lhs, low)
    return out[0:8] + out[8:16]


def spread(matrix):
    wide = 2 * SPECIES
    tall = jnp.concatenate([matrix, matrix], 0)
    full = jnp.concatenate([tall, tall], 1)
    same = (
        lax.broadcasted_iota(jnp.int32, (wide, wide), 0) // SPECIES
        == lax.broadcasted_iota(jnp.int32, (wide, wide), 1) // SPECIES
    )
    return jnp.where(same, full, 0.0)


def left_side(matrix):
    high, low = halves(matrix)
    blank = jnp.zeros((matrix.shape[0], 8), F32)
    high, low = high.astype(F32), low.astype(F32)
    return jnp.concatenate([high, blank, high, blank, low, blank], 1).astype(BF16)


def right_side(state):
    high, low = halves(jnp.concatenate([state, jnp.zeros((8, state.shape[1]), F32)], 0))
    return jnp.concatenate([high, low, high], 0)


def kernel(
    pos_in,
    width_in,
    mass_in,
    energy_in,
    species_in,
    neigh_in,
    exports_in,
    imports_in,
    jac_in,
    rates_in,
    steps_in,
    slot_in,
    density,
    accel,
    abund_all,
    pos,
    width,
    mass,
    energy,
    species,
    neigh,
    exports,
    imports,
    jac,
    rates,
    steps,
    slot,
    fields,
    targets,
    feats,
    far_feats,
    even,
    odd,
    far_ring,
    raw,
    stage,
    far_raw,
    far_fields,
    factor,
    stage_factor,
    far_factor,
    rows,
    far_rows,
    near_cubes,
    far_cubes,
    near_dens,
    far_dens,
    near_acc,
    far_acc,
    root_mass,
    gain,
    limit,
    state,
    rate_in,
    load_sem,
    send_one,
    recv_one,
    send_two,
    recv_two,
):
    dom = lax.axis_index("dom")
    sub = lax.axis_index("sub")
    doms = lax.axis_size("dom")
    subs = lax.axis_size("sub")
    sides = [lax.rem(dom + doms - 1, doms), lax.rem(dom + 1, doms)]
    barrier = pltpu.get_barrier_semaphore()
    for side in sides:
        for q in range(subs):
            pl.semaphore_signal(barrier, inc=1, device_id=(side, q), device_id_type=MESH)

    pairs = {
        "pos": (pos_in, pos),
        "mass": (mass_in, mass),
        "imports": (imports_in, imports),
        "width": (width_in, width),
        "neigh": (neigh_in, neigh),
        "exports": (exports_in, exports),
        "jac": (jac_in, jac),
        "rates": (rates_in, rates),
        "energy": (energy_in, energy),
        "steps": (steps_in, steps),
        "slot": (slot_in, slot),
        "species": (species_in, species),
    }
    loads = {}
    for i, (name, (source, target)) in enumerate(pairs.items()):
        loads[name] = pltpu.make_async_copy(source, target, load_sem.at[i])
        loads[name].start()

    def exchange(sent, landed, send_sem, recv_sem):
        copies = []
        for e in range(2):
            for q in range(subs):
                copies.append(
                    pltpu.make_async_remote_copy(
                        src_ref=sent.at[e * subs + q],
                        dst_ref=landed.at[(1 - e) * subs + sub],
                        send_sem=send_sem.at[e * subs + q],
                        recv_sem=recv_sem.at[(1 - e) * subs + sub],
                        device_id=(sides[e], q),
                        device_id_type=MESH,
                    )
                )
        return copies

    def arrive(place, sent, landed, send_sem, recv_sem):
        pltpu.make_async_remote_copy(
            src_ref=sent.at[place],
            dst_ref=landed.at[place],
            send_sem=send_sem.at[place],
            recv_sem=recv_sem.at[place],
            device_id=(sides[0], 0),
            device_id_type=MESH,
        ).wait_recv()

    feats[...] = jnp.zeros_like(feats)
    targets[...] = jnp.zeros_like(targets)
    far_feats[...] = jnp.zeros_like(far_feats)
    loads["pos"].wait()
    loads["mass"].wait()
    root_mass[...] = 1.0 / jnp.sqrt(mass[...])

    def prepare(b, _):
        place = pos[:, pl.ds(pl.multiple_of(b * BLOCK, BLOCK), BLOCK)]
        raw[b, 0:3] = place
        raw[b, 3:4] = root_mass[pl.ds(b, 1)]
        return 0

    lax.fori_loop(0, BLOCKS, prepare, 0, unroll=8)
    loads["imports"].wait()
    for r in range(SLOTS):
        for k in range(2):
            stage[r // 2, (r % 2) * 2 + k] = raw[imports[k, r]]
    loads["width"].wait()
    loads["neigh"].wait()
    loads["exports"].wait()
    loads["jac"].wait()
    loads["rates"].wait()
    pl.semaphore_wait(barrier, 2 * subs)
    first = exchange(stage, far_raw, send_one, recv_one)
    for copy in first:
        copy.start()

    def shape_block(b):
        place = pos[:, pl.ds(pl.multiple_of(b * BLOCK, BLOCK), BLOCK)]
        norm = jnp.sum(place * place, axis=0, keepdims=True)
        span = width[pl.ds(b, 1)]
        target = jnp.concatenate(
            [place * -2.0, span * span + norm, jnp.ones_like(norm), jnp.zeros((3, BLOCK), F32)], 0
        )
        high, middle, low = pieces(target)
        split = jnp.concatenate([high, middle, low, high, middle, high], 0).astype(BF16)
        targets[b, 0:FEAT, 0:BLOCK] = split
        targets[b, BLOCK : BLOCK + FEAT, BLOCK : 2 * BLOCK] = split
        full = weighted(place, root_mass[pl.ds(b, 1)])
        fields[b] = full
        feats[b, :, 0:FEAT] = source_features(full)

    for b in range(FIRST):
        shape_block(b)
    jac_full = spread(jac[...])
    rate_full = spread(rates[...])
    both = jnp.dot(rates[...], jac[...], precision=HIGH, preferred_element_type=F32)
    left = left_side(jnp.concatenate([spread(both), jac_full], 0))
    left_first = left_side(rate_full)

    def fill(b, place):
        distances([feats[neigh[k, b]] for k in range(NBR)], targets[b], place)

    def drain(b, place):
        pair_terms(place, NBR // 2, near_cubes.at[b], near_dens, b)

    ring = [even.at[0], even.at[1], odd.at[0], odd.at[1]]
    fill(0, ring[0])
    fill(1, ring[1])
    for b in range(BLOCKS):
        if b + 2 < BLOCKS:
            fill(b + 2, ring[(b + 2) % 4])
        drain(b, ring[b % 4])
    for name in ("energy", "steps", "slot", "species"):
        loads[name].wait()

    early = jnp.where(dom < doms // 2, 1, 0)
    order = []
    for e in (early, 1 - early):
        for d in (0, 1, 3, 2):
            order.append(e * subs + lax.rem(sub + d, subs))

    def far_fill(i):
        place = order[i]
        for k in range(4):
            full = weighted(far_raw[place, k, 0:3], far_raw[place, k, 3:4])
            far_fields[place, k] = full
            far_feats[i * 4 + k, :, 0:FEAT] = source_features(full)
        for x in range(2):
            parts = [far_feats[i * 4 + 2 * x + k] for k in range(2)]
            distances(parts, targets[exports[x, place]], far_ring.at[pl.ds(2 * i + x, 1)])

    def far_drain(i):
        for x in range(2):
            at = 2 * i + x
            pair_terms(far_ring.at[pl.ds(at, 1)], 1, far_cubes.at[at], far_dens, at)

    before = ()
    for group in ((0, 1, 2, 3), (4, 5), (6,), (7,)):
        for i in group:
            arrive(order[i], stage, far_raw, send_one, recv_one)
        for i in group:
            far_fill(i)
        for i in before:
            far_drain(i)
        before = group
    for i in before:
        far_drain(i)

    owner = lax.broadcasted_iota(jnp.int32, (BLOCKS, BLOCK), 0)
    total = near_dens[...]
    for r in range(SLOTS):
        total += jnp.where(owner == exports[r % 2, order[r // 2]], far_dens[r : r + 1], 0.0)
    dens = total * width[...]
    density[...] = dens
    factor[...] = (gamma_gas - 1.0) * energy[...] / dens
    for r in range(SLOTS):
        for k in range(2):
            stage_factor[r // 2, pl.ds((r % 2) * 2 + k, 1)] = factor[pl.ds(imports[k, r], 1)]
    second = exchange(stage_factor, far_factor, send_two, recv_two)
    for copy in second[subs:] + second[:subs]:
        copy.start()
    gain_all = chem_tau * (dens / (dens + 1.0))
    most = jnp.where(slot[...] >= 0, steps[...], jnp.minimum(steps[...], S_LO)).astype(F32)
    for b in range(BLOCKS // 2):
        for h in range(2):
            block = b + h * (BLOCKS // 2)
            at = pl.ds(b * BLOCK, BLOCK)
            span = pl.ds(h * SPECIES, SPECIES)
            gain[span, at] = jnp.broadcast_to(gain_all[block : block + 1], (SPECIES, BLOCK))
            limit[span, at] = jnp.broadcast_to(most[block : block + 1], (SPECIES, BLOCK))
    state[0:SPECIES] = species[:, 0:HALF]
    state[SPECIES : 2 * SPECIES] = species[:, HALF : 2 * HALF]
    part = HALF // GROUPS
    for g in range(GROUPS):
        at = pl.ds(g * part, part)
        rate_in[:, at] = mm(left_first, right_side(state[:, at]))

    def rows_near(b, _):
        rows[b] = gradient_rows(fields[b], factor[pl.ds(b, 1)])
        return 0

    lax.fori_loop(0, BLOCKS, rows_near, 0, unroll=8)

    def chem_step(c):
        for g in range(GROUPS):
            at = pl.ds(g * part, part)
            abund = state[:, at]
            lift = gain[:, at]
            moved = (abund + lift) + lift * jnp.tanh(rate_in[:, at])
            out = mm(left, right_side(moved))
            rate_in[:, at] = out[: 2 * SPECIES]
            state[:, at] = jnp.where(limit[:, at] > c, out[2 * SPECIES :], abund)

    for c in range(SMAX // 2):
        chem_step(c)
        for b in (2 * c, 2 * c + 1):
            near_acc[b] = pair_sums([rows[neigh[k, b]] for k in range(NBR)], near_cubes.at[b])

    row = lax.broadcasted_iota(jnp.int32, (8, BLOCK), 0)
    lane = lax.broadcasted_iota(jnp.int32, (8, BLOCK), 1)
    named = jnp.zeros((8, BLOCK), jnp.int32)
    for r in range(SLOTS):
        named = jnp.where(lane // 8 == r, exports[r % 2, order[r // 2]], named)
    named = jnp.where(lane % 8 == row, named, -1)
    pick = jnp.concatenate(
        [jnp.where(named == b, 1.0, 0.0) for b in range(BLOCKS)], 0
    ).astype(BF16)
    for c in range(16, SPLIT):
        chem_step(c)

    def rows_far(group):
        for i in group:
            arrive(order[i], stage_factor, far_factor, send_two, recv_two)
        for i in group:
            place = order[i]
            for k in range(4):
                far_rows[i * 4 + k] = gradient_rows(
                    far_fields[place, k], far_factor[place, pl.ds(k, 1)]
                )

    def sums_far(i, x):
        at = 2 * i + x
        parts = [far_rows[i * 4 + 2 * x + k] for k in range(2)]
        far_acc[at] = pair_sums(parts, far_cubes.at[at])

    rows_far((0, 1, 2, 3))
    slots = [(i, x) for i in range(4) for x in range(2)]
    for c in range(SPLIT, SMAX):
        chem_step(c)
        n = 8 // (SMAX - SPLIT)
        for i, x in slots[(c - SPLIT) * n : (c - SPLIT + 1) * n]:
            sums_far(i, x)
    for group in ((4, 5), (6,), (7,)):
        rows_far(group)
        for i in group:
            for x in range(2):
                sums_far(i, x)
    high, low = halves(far_acc[...].reshape(SLOTS * 8, BLOCK))
    far_all = mm(jnp.concatenate([pick, pick], 1), jnp.concatenate([high, low], 0))
    for b in range(BLOCKS):
        acc = near_acc[b] + far_all[b * 8 : b * 8 + 8]
        acc = acc * jnp.where(row < 4, factor[b : b + 1], 1.0)
        acc = acc + pltpu.roll(acc, 4, 0)
        at = pl.ds(b * BLOCK, BLOCK)
        accel[:, at] = (4.0 * width[b : b + 1]) * (pos[:, at] * acc[3:4] - acc[0:3])
    abund_all[:, 0:HALF] = state[0:SPECIES]
    abund_all[:, HALF : 2 * HALF] = state[SPECIES : 2 * SPECIES]
    for copy in first + second:
        copy.wait_send()


def deliver(density, accel, abund, dens_out, accel_out, abund_out, sems):
    pairs = ((abund, abund_out), (accel, accel_out), (density, dens_out))
    copies = [pltpu.make_async_copy(a, b, sems.at[i]) for i, (a, b) in enumerate(pairs)]
    for copy in copies:
        copy.start()
    for copy in copies:
        copy.wait()


def on_device(
    position,
    smoothing,
    mass,
    energy,
    species,
    neighbours,
    exports,
    imports,
    jac_inverse,
    rates,
    chem_steps,
    dense_slot,
):
    tile = (BLOCKS, BLOCK)
    vmem = pl.BlockSpec(memory_space=pltpu.VMEM)
    hbm = pl.BlockSpec(memory_space=pltpu.HBM)
    far = 2 * SLOTS
    sides = SLOTS // 2
    chem = (2 * SPECIES, HALF)
    given = (
        position,
        smoothing.reshape(tile),
        mass.reshape(tile),
        energy.reshape(tile),
        species,
        neighbours.T,
        exports.T,
        imports.T,
        jac_inverse,
        rates,
        chem_steps.reshape(tile),
        dense_slot.reshape(tile),
    )
    spaces = [pltpu.VMEM] * 5 + [pltpu.SMEM] * 3 + [pltpu.VMEM] * 4
    density, accel, abund = pl.pallas_call(
        kernel,
        out_shape=(
            pltpu.VMEM(tile, F32),
            pltpu.VMEM(position.shape, F32),
            pltpu.VMEM(species.shape, F32),
        ),
        in_specs=[hbm] * len(given),
        out_specs=(vmem, vmem, vmem),
        scratch_shapes=[space(x.shape, x.dtype) for space, x in zip(spaces, given)]
        + [
            pltpu.VMEM((BLOCKS, 8, BLOCK), F32),
            pltpu.VMEM((BLOCKS, 2 * BLOCK, 2 * BLOCK), BF16),
            pltpu.VMEM((BLOCKS, BLOCK, BLOCK), BF16),
            pltpu.VMEM((far, BLOCK, BLOCK), BF16),
            pltpu.VMEM((2, NBR // 2, BLOCK, 2 * BLOCK), F32),
            pltpu.VMEM((2, NBR // 2, BLOCK, 2 * BLOCK), F32),
            pltpu.VMEM((SLOTS, BLOCK, 2 * BLOCK), F32),
            pltpu.VMEM((BLOCKS, 4, BLOCK), F32),
            pltpu.VMEM((sides, 4, 4, BLOCK), F32),
            pltpu.VMEM((sides, 4, 4, BLOCK), F32),
            pltpu.VMEM((sides, 4, 8, BLOCK), F32),
            pltpu.VMEM(tile, F32),
            pltpu.VMEM((sides, 4, BLOCK), F32),
            pltpu.VMEM((sides, 4, BLOCK), F32),
            pltpu.VMEM((BLOCKS, 16, BLOCK), BF16),
            pltpu.VMEM((far, 16, BLOCK), BF16),
            pltpu.VMEM((BLOCKS, NBR * BLOCK, BLOCK), F32),
            pltpu.VMEM((SLOTS, 2 * BLOCK, BLOCK), F32),
            pltpu.VMEM(tile, F32),
            pltpu.VMEM((SLOTS, BLOCK), F32),
            pltpu.VMEM((BLOCKS, 8, BLOCK), F32),
            pltpu.VMEM((SLOTS, 8, BLOCK), F32),
            pltpu.VMEM(tile, F32),
            pltpu.VMEM(chem, F32),
            pltpu.VMEM(chem, F32),
            pltpu.VMEM(chem, F32),
            pltpu.VMEM(chem, F32),
            pltpu.SemaphoreType.DMA((len(given),)),
        ]
        + [pltpu.SemaphoreType.DMA((sides,))] * 4,
        compiler_params=pltpu.CompilerParams(
            collective_id=0, has_side_effects=True, vmem_limit_bytes=24 << 20
        ),
        name="particle_step",
    )(*(pltpu.with_memory_space_constraint(x, pltpu.HBM) for x in given))
    density, accel, abund = pl.pallas_call(
        deliver,
        out_shape=(
            jax.ShapeDtypeStruct(tile, F32),
            jax.ShapeDtypeStruct(position.shape, F32),
            jax.ShapeDtypeStruct(species.shape, F32),
        ),
        in_specs=[vmem] * 3,
        out_specs=(hbm,) * 3,
        scratch_shapes=[pltpu.SemaphoreType.DMA((3,))],
        compiler_params=pltpu.CompilerParams(vmem_limit_bytes=1 << 20),
        name="deliver",
    )(density, accel, abund)
    return density.reshape(-1), accel, abund


def solution(mesh):
    flat = P(("dom", "sub"))
    wide = P(None, ("dom", "sub"))
    tall = P(("dom", "sub"), None)
    return jax.shard_map(
        on_device,
        mesh=mesh,
        in_specs=(wide, flat, flat, flat, wide, tall, tall, tall, P(), P(), flat, flat),
        out_specs=(flat, wide, wide),
        check_vma=False,
    )
```

```python
import functools

import jax
import jax.numpy as jnp
from jax import lax
from jax.experimental import pallas as pl
from jax.experimental.pallas import tpu as pltpu
from jax.sharding import PartitionSpec as P

BLOCK = 128
BLOCKS = 32
NBR = 4
SLOTS = 16
SPECIES = 12
S_LO = 4
SMAX = 32
HALF = BLOCKS * BLOCK // 2
FEAT = 48
GROUPS = 4
SPLIT = 24
FIRST = 32
MESH = pl.DeviceIdType.MESH
F32 = jnp.float32
BF16 = jnp.bfloat16
HIGH = lax.Precision.HIGHEST

gamma_gas = 5.0 / 3.0
chem_tau = 0.5


def pieces(value):
    high = value.astype(BF16).astype(F32)
    rest = value - high
    middle = rest.astype(BF16).astype(F32)
    return high, middle, rest - middle


def halves(value):
    high = value.astype(BF16)
    return high, (value - high.astype(F32)).astype(BF16)


def mm(a, b):
    return jnp.dot(a, b, preferred_element_type=F32)


def source_features(fields):
    high, middle, low = pieces(fields)
    return jnp.concatenate([high, high, high, middle, middle, low], 0).T.astype(BF16)


def weighted(place, weight):
    norm = jnp.sum(place * place, axis=0, keepdims=True)
    return jnp.concatenate(
        [place * weight, weight, norm * weight, jnp.zeros((3, BLOCK), F32)], 0
    )


def gradient_rows(fields, factor):
    row = lax.broadcasted_iota(jnp.int32, fields.shape, 0)
    both = jnp.where(row < 4, fields, pltpu.roll(fields, 4, 0))
    high, low = halves(both * jnp.where(row < 4, 1.0, factor))
    return jnp.concatenate([high, low], 0)


def distances(features, target, place):
    for k in range(0, len(features), 2):
        place[k // 2] = mm(jnp.concatenate(features[k : k + 2], 1), target)


def pair_terms(place, count, cubes, dens, row):
    total = None
    for k in range(count):
        for half in range(2):
            base = 1.0 / place[k, :, half * BLOCK : (half + 1) * BLOCK]
            squared = base * base
            at = (2 * k + half) * BLOCK
            cubes[at : at + BLOCK] = squared * base
            part = jnp.sum(squared.reshape(BLOCK // 8, 8, BLOCK), axis=0)
            total = part if total is None else total + part
    dens[pl.ds(row, 1)] = jnp.sum(total, axis=0, keepdims=True)


def pair_sums(rows, cubes):
    high, low = halves(cubes[...])
    lhs = jnp.concatenate(rows, 1)
    out = mm(lhs, high) + mm(lhs, low)
    return out[0:8] + out[8:16]


def spread(matrix):
    wide = 2 * SPECIES
    tall = jnp.concatenate([matrix, matrix], 0)
    full = jnp.concatenate([tall, tall], 1)
    same = (
        lax.broadcasted_iota(jnp.int32, (wide, wide), 0) // SPECIES
        == lax.broadcasted_iota(jnp.int32, (wide, wide), 1) // SPECIES
    )
    return jnp.where(same, full, 0.0)


def left_side(matrix):
    high, low = halves(matrix)
    blank = jnp.zeros((matrix.shape[0], 8), F32)
    high, low = high.astype(F32), low.astype(F32)
    return jnp.concatenate([high, blank, high, blank, low, blank], 1).astype(BF16)


def right_side(state):
    high, low = halves(jnp.concatenate([state, jnp.zeros((8, state.shape[1]), F32)], 0))
    return jnp.concatenate([high, low, high], 0)


def kernel(
    pos_in,
    width_in,
    mass_in,
    energy_in,
    species_in,
    neigh_in,
    exports_in,
    imports_in,
    jac_in,
    rates_in,
    steps_in,
    slot_in,
    density,
    accel,
    abund_all,
    pos,
    width,
    mass,
    energy,
    species,
    neigh,
    exports,
    imports,
    jac,
    rates,
    steps,
    slot,
    fields,
    targets,
    feats,
    far_feats,
    even,
    odd,
    far_ring,
    raw,
    stage,
    far_raw,
    far_fields,
    factor,
    stage_factor,
    far_factor,
    rows,
    far_rows,
    near_cubes,
    far_cubes,
    near_dens,
    far_dens,
    near_acc,
    far_acc,
    root_mass,
    gain,
    limit,
    state,
    rate_in,
    load_sem,
    send_one,
    recv_one,
    send_two,
    recv_two,
    relay,
    send_mate,
    recv_mate,
    send_wrap,
    recv_wrap,
    ready,
):
    dom = lax.axis_index("dom")
    sub = lax.axis_index("sub")
    doms = lax.axis_size("dom")
    subs = lax.axis_size("sub")
    sides = [lax.rem(dom + doms - 1, doms), lax.rem(dom + 1, doms)]
    barrier = pltpu.get_barrier_semaphore()
    last = doms - 1
    for q in range(subs):
        pl.semaphore_signal(barrier, inc=1, device_id=(sides[0], q), device_id_type=MESH)

    @pl.when(dom < last - 1)
    def _():
        for q in range(subs):
            pl.semaphore_signal(barrier, inc=1, device_id=(sides[1], q), device_id_type=MESH)

    mates = [lax.rem(sub + k, subs) for k in range(1, subs)]

    @pl.when(dom == 0)
    def _():
        for q in mates:
            pl.semaphore_signal(barrier, inc=1, device_id=(dom, q), device_id_type=MESH)

    @pl.when(dom == last)
    def _():
        pl.semaphore_wait(barrier, subs)
        pl.semaphore_signal(ready, inc=1, device_id=(sides[1], sub), device_id_type=MESH)


    pairs = {
        "pos": (pos_in, pos),
        "mass": (mass_in, mass),
        "imports": (imports_in, imports),
        "width": (width_in, width),
        "neigh": (neigh_in, neigh),
        "exports": (exports_in, exports),
        "jac": (jac_in, jac),
        "rates": (rates_in, rates),
        "energy": (energy_in, energy),
        "steps": (steps_in, steps),
        "slot": (slot_in, slot),
        "species": (species_in, species),
    }
    loads = {}
    for i, (name, (source, target)) in enumerate(pairs.items()):
        loads[name] = pltpu.make_async_copy(source, target, load_sem.at[i])
        loads[name].start()

    def exchange(sent, landed, send_sem, recv_sem):
        copies = []
        for e in range(2):
            for q in range(subs):
                copies.append(
                    pltpu.make_async_remote_copy(
                        src_ref=sent.at[e * subs + q],
                        dst_ref=landed.at[(1 - e) * subs + sub],
                        send_sem=send_sem.at[e * subs + q],
                        recv_sem=recv_sem.at[(1 - e) * subs + sub],
                        device_id=(sides[e], q),
                        device_id_type=MESH,
                    )
                )
        return copies

    def arrive(place, sent, landed, send_sem, recv_sem):
        pltpu.make_async_remote_copy(
            src_ref=sent.at[place],
            dst_ref=landed.at[place],
            send_sem=send_sem.at[place],
            recv_sem=recv_sem.at[place],
            device_id=(sides[0], 0),
            device_id_type=MESH,
        ).wait_recv()

    feats[...] = jnp.zeros_like(feats)
    targets[...] = jnp.zeros_like(targets)
    far_feats[...] = jnp.zeros_like(far_feats)
    loads["pos"].wait()
    loads["mass"].wait()
    root_mass[...] = 1.0 / jnp.sqrt(mass[...])

    def prepare(b, _):
        place = pos[:, pl.ds(pl.multiple_of(b * BLOCK, BLOCK), BLOCK)]
        raw[b, 0:3] = place
        raw[b, 3:4] = root_mass[pl.ds(b, 1)]
        return 0

    lax.fori_loop(0, BLOCKS, prepare, 0, unroll=8)
    loads["imports"].wait()
    for r in range(SLOTS):
        for k in range(2):
            stage[r // 2, (r % 2) * 2 + k] = raw[imports[k, r]]
    loads["width"].wait()
    loads["neigh"].wait()
    loads["exports"].wait()
    loads["jac"].wait()
    loads["rates"].wait()
    first = exchange(stage, far_raw, send_one, recv_one)
    relayed = [
        pltpu.make_async_remote_copy(
            src_ref=stage.at[q],
            dst_ref=relay.at[sub],
            send_sem=send_mate.at[k],
            recv_sem=recv_mate.at[k],
            device_id=(dom, q),
            device_id_type=MESH,
        )
        for k, q in enumerate(mates)
    ]
    wrapped = pltpu.make_async_remote_copy(
        src_ref=relay,
        dst_ref=far_raw.at[pl.ds(subs, subs)],
        send_sem=send_wrap,
        recv_sem=recv_wrap,
        device_id=(sides[0], sub),
        device_id_type=MESH,
    )

    @pl.when(dom != last)
    def _():
        pl.semaphore_wait(barrier, jnp.where(dom == 0, 2 * subs - 1, 2 * subs))

    @pl.when(dom == last - 1)
    def _():
        for q in range(subs):
            pl.semaphore_signal(ready, inc=1, device_id=(sides[1], q), device_id_type=MESH)

    for copy in first[subs:]:
        copy.start()

    @pl.when((dom != 0) & (dom != last))
    def _():
        for copy in first[:subs]:
            copy.start()

    @pl.when(dom == 0)
    def _():
        for copy in relayed:
            copy.start()
        relay[sub] = stage[sub]


    def shape_block(b):
        place = pos[:, pl.ds(pl.multiple_of(b * BLOCK, BLOCK), BLOCK)]
        norm = jnp.sum(place * place, axis=0, keepdims=True)
        span = width[pl.ds(b, 1)]
        target = jnp.concatenate(
            [place * -2.0, span * span + norm, jnp.ones_like(norm), jnp.zeros((3, BLOCK), F32)], 0
        )
        high, middle, low = pieces(target)
        split = jnp.concatenate([high, middle, low, high, middle, high], 0).astype(BF16)
        targets[b, 0:FEAT, 0:BLOCK] = split
        targets[b, BLOCK : BLOCK + FEAT, BLOCK : 2 * BLOCK] = split
        full = weighted(place, root_mass[pl.ds(b, 1)])
        fields[b] = full
        feats[b, :, 0:FEAT] = source_features(full)

    for b in range(FIRST):
        shape_block(b)
    jac_full = spread(jac[...])
    rate_full = spread(rates[...])
    both = jnp.dot(rates[...], jac[...], precision=HIGH, preferred_element_type=F32)
    left = left_side(jnp.concatenate([spread(both), jac_full], 0))
    left_first = left_side(rate_full)

    def fill(b, place):
        distances([feats[neigh[k, b]] for k in range(NBR)], targets[b], place)

    def drain(b, place):
        pair_terms(place, NBR // 2, near_cubes.at[b], near_dens, b)

    ring = [even.at[0], even.at[1], odd.at[0], odd.at[1]]
    fill(0, ring[0])
    fill(1, ring[1])
    for b in range(BLOCKS):
        if b + 2 < BLOCKS:
            fill(b + 2, ring[(b + 2) % 4])
        drain(b, ring[b % 4])
    for name in ("energy", "steps", "slot", "species"):
        loads[name].wait()

    @pl.when(dom == 0)
    def _():
        for k in range(subs - 1):
            pltpu.make_async_remote_copy(
                src_ref=stage.at[0],
                dst_ref=relay.at[lax.rem(sub + subs - 1 - k, subs)],
                send_sem=send_mate.at[k],
                recv_sem=recv_mate.at[k],
                device_id=(dom, mates[k]),
                device_id_type=MESH,
            ).wait_recv()
        pl.semaphore_wait(ready, 1)
        wrapped.start()

    @pl.when(dom == last)
    def _():
        pl.semaphore_wait(ready, subs)
        for copy in first[:subs]:
            copy.start()


    early = jnp.where(dom < doms // 2, 1, 0)
    order = []
    for e in (early, 1 - early):
        for d in (0, 1, 3, 2):
            order.append(e * subs + lax.rem(sub + d, subs))

    def far_fill(i):
        place = order[i]
        for k in range(4):
            full = weighted(far_raw[place, k, 0:3], far_raw[place, k, 3:4])
            far_fields[place, k] = full
            far_feats[i * 4 + k, :, 0:FEAT] = source_features(full)
        for x in range(2):
            parts = [far_feats[i * 4 + 2 * x + k] for k in range(2)]
            distances(parts, targets[exports[x, place]], far_ring.at[pl.ds(2 * i + x, 1)])

    def far_drain(i):
        for x in range(2):
            at = 2 * i + x
            pair_terms(far_ring.at[pl.ds(at, 1)], 1, far_cubes.at[at], far_dens, at)

    before = ()
    for group in ((0, 1, 2, 3), (4, 5), (6,), (7,)):
        if group[0] < subs:
            for i in group:
                arrive(order[i], stage, far_raw, send_one, recv_one)
        else:

            @pl.when(dom != last)
            def _():
                for i in group:
                    arrive(order[i], stage, far_raw, send_one, recv_one)

            if group[0] == subs:

                @pl.when(dom == last)
                def _():
                    wrapped.wait_recv()

        for i in group:
            far_fill(i)
        for i in before:
            far_drain(i)
        before = group
    for i in before:
        far_drain(i)

    owner = lax.broadcasted_iota(jnp.int32, (BLOCKS, BLOCK), 0)
    total = near_dens[...]
    for r in range(SLOTS):
        total += jnp.where(owner == exports[r % 2, order[r // 2]], far_dens[r : r + 1], 0.0)
    dens = total * width[...]
    density[...] = dens
    factor[...] = (gamma_gas - 1.0) * energy[...] / dens
    for r in range(SLOTS):
        for k in range(2):
            stage_factor[r // 2, pl.ds((r % 2) * 2 + k, 1)] = factor[pl.ds(imports[k, r], 1)]
    second = exchange(stage_factor, far_factor, send_two, recv_two)
    for copy in second[subs:] + second[:subs]:
        copy.start()
    gain_all = chem_tau * (dens / (dens + 1.0))
    most = jnp.where(slot[...] >= 0, steps[...], jnp.minimum(steps[...], S_LO)).astype(F32)
    for b in range(BLOCKS // 2):
        for h in range(2):
            block = b + h * (BLOCKS // 2)
            at = pl.ds(b * BLOCK, BLOCK)
            span = pl.ds(h * SPECIES, SPECIES)
            gain[span, at] = jnp.broadcast_to(gain_all[block : block + 1], (SPECIES, BLOCK))
            limit[span, at] = jnp.broadcast_to(most[block : block + 1], (SPECIES, BLOCK))
    state[0:SPECIES] = species[:, 0:HALF]
    state[SPECIES : 2 * SPECIES] = species[:, HALF : 2 * HALF]
    part = HALF // GROUPS
    for g in range(GROUPS):
        at = pl.ds(g * part, part)
        rate_in[:, at] = mm(left_first, right_side(state[:, at]))

    def rows_near(b, _):
        rows[b] = gradient_rows(fields[b], factor[pl.ds(b, 1)])
        return 0

    lax.fori_loop(0, BLOCKS, rows_near, 0, unroll=8)

    def chem_step(c):
        for g in range(GROUPS):
            at = pl.ds(g * part, part)
            abund = state[:, at]
            lift = gain[:, at]
            moved = (abund + lift) + lift * jnp.tanh(rate_in[:, at])
            out = mm(left, right_side(moved))
            rate_in[:, at] = out[: 2 * SPECIES]
            state[:, at] = jnp.where(limit[:, at] > c, out[2 * SPECIES :], abund)

    for c in range(SMAX // 2):
        chem_step(c)
        for b in (2 * c, 2 * c + 1):
            near_acc[b] = pair_sums([rows[neigh[k, b]] for k in range(NBR)], near_cubes.at[b])

    row = lax.broadcasted_iota(jnp.int32, (8, BLOCK), 0)
    lane = lax.broadcasted_iota(jnp.int32, (8, BLOCK), 1)
    named = jnp.zeros((8, BLOCK), jnp.int32)
    for r in range(SLOTS):
        named = jnp.where(lane // 8 == r, exports[r % 2, order[r // 2]], named)
    named = jnp.where(lane % 8 == row, named, -1)
    pick = jnp.concatenate(
        [jnp.where(named == b, 1.0, 0.0) for b in range(BLOCKS)], 0
    ).astype(BF16)
    for c in range(16, SPLIT):
        chem_step(c)

    def rows_far(group):
        for i in group:
            arrive(order[i], stage_factor, far_factor, send_two, recv_two)
        for i in group:
            place = order[i]
            for k in range(4):
                far_rows[i * 4 + k] = gradient_rows(
                    far_fields[place, k], far_factor[place, pl.ds(k, 1)]
                )

    def sums_far(i, x):
        at = 2 * i + x
        parts = [far_rows[i * 4 + 2 * x + k] for k in range(2)]
        far_acc[at] = pair_sums(parts, far_cubes.at[at])

    rows_far((0, 1, 2, 3))
    slots = [(i, x) for i in range(4) for x in range(2)]
    for c in range(SPLIT, SMAX):
        chem_step(c)
        n = 8 // (SMAX - SPLIT)
        for i, x in slots[(c - SPLIT) * n : (c - SPLIT + 1) * n]:
            sums_far(i, x)
    for group in ((4, 5), (6,), (7,)):
        rows_far(group)
        for i in group:
            for x in range(2):
                sums_far(i, x)
    high, low = halves(far_acc[...].reshape(SLOTS * 8, BLOCK))
    far_all = mm(jnp.concatenate([pick, pick], 1), jnp.concatenate([high, low], 0))
    for b in range(BLOCKS):
        acc = near_acc[b] + far_all[b * 8 : b * 8 + 8]
        acc = acc * jnp.where(row < 4, factor[b : b + 1], 1.0)
        acc = acc + pltpu.roll(acc, 4, 0)
        at = pl.ds(b * BLOCK, BLOCK)
        accel[:, at] = (4.0 * width[b : b + 1]) * (pos[:, at] * acc[3:4] - acc[0:3])
    abund_all[:, 0:HALF] = state[0:SPECIES]
    abund_all[:, HALF : 2 * HALF] = state[SPECIES : 2 * SPECIES]
    for copy in first[subs:] + second:
        copy.wait_send()

    @pl.when(dom != 0)
    def _():
        for copy in first[:subs]:
            copy.wait_send()

    @pl.when(dom == 0)
    def _():
        for copy in relayed + [wrapped]:
            copy.wait_send()


def deliver(density, accel, abund, dens_out, accel_out, abund_out, sems):
    pairs = ((abund, abund_out), (accel, accel_out), (density, dens_out))
    copies = [pltpu.make_async_copy(a, b, sems.at[i]) for i, (a, b) in enumerate(pairs)]
    for copy in copies:
        copy.start()
    for copy in copies:
        copy.wait()


def on_device(
    position,
    smoothing,
    mass,
    energy,
    species,
    neighbours,
    exports,
    imports,
    jac_inverse,
    rates,
    chem_steps,
    dense_slot,
):
    tile = (BLOCKS, BLOCK)
    vmem = pl.BlockSpec(memory_space=pltpu.VMEM)
    hbm = pl.BlockSpec(memory_space=pltpu.HBM)
    far = 2 * SLOTS
    sides = SLOTS // 2
    chem = (2 * SPECIES, HALF)
    given = (
        position,
        smoothing.reshape(tile),
        mass.reshape(tile),
        energy.reshape(tile),
        species,
        neighbours.T,
        exports.T,
        imports.T,
        jac_inverse,
        rates,
        chem_steps.reshape(tile),
        dense_slot.reshape(tile),
    )
    spaces = [pltpu.VMEM] * 5 + [pltpu.SMEM] * 3 + [pltpu.VMEM] * 4
    density, accel, abund = pl.pallas_call(
        kernel,
        out_shape=(
            pltpu.VMEM(tile, F32),
            pltpu.VMEM(position.shape, F32),
            pltpu.VMEM(species.shape, F32),
        ),
        in_specs=[hbm] * len(given),
        out_specs=(vmem, vmem, vmem),
        scratch_shapes=[space(x.shape, x.dtype) for space, x in zip(spaces, given)]
        + [
            pltpu.VMEM((BLOCKS, 8, BLOCK), F32),
            pltpu.VMEM((BLOCKS, 2 * BLOCK, 2 * BLOCK), BF16),
            pltpu.VMEM((BLOCKS, BLOCK, BLOCK), BF16),
            pltpu.VMEM((far, BLOCK, BLOCK), BF16),
            pltpu.VMEM((2, NBR // 2, BLOCK, 2 * BLOCK), F32),
            pltpu.VMEM((2, NBR // 2, BLOCK, 2 * BLOCK), F32),
            pltpu.VMEM((SLOTS, BLOCK, 2 * BLOCK), F32),
            pltpu.VMEM((BLOCKS, 4, BLOCK), F32),
            pltpu.VMEM((sides, 4, 4, BLOCK), F32),
            pltpu.VMEM((sides, 4, 4, BLOCK), F32),
            pltpu.VMEM((sides, 4, 8, BLOCK), F32),
            pltpu.VMEM(tile, F32),
            pltpu.VMEM((sides, 4, BLOCK), F32),
            pltpu.VMEM((sides, 4, BLOCK), F32),
            pltpu.VMEM((BLOCKS, 16, BLOCK), BF16),
            pltpu.VMEM((far, 16, BLOCK), BF16),
            pltpu.VMEM((BLOCKS, NBR * BLOCK, BLOCK), F32),
            pltpu.VMEM((SLOTS, 2 * BLOCK, BLOCK), F32),
            pltpu.VMEM(tile, F32),
            pltpu.VMEM((SLOTS, BLOCK), F32),
            pltpu.VMEM((BLOCKS, 8, BLOCK), F32),
            pltpu.VMEM((SLOTS, 8, BLOCK), F32),
            pltpu.VMEM(tile, F32),
            pltpu.VMEM(chem, F32),
            pltpu.VMEM(chem, F32),
            pltpu.VMEM(chem, F32),
            pltpu.VMEM(chem, F32),
            pltpu.SemaphoreType.DMA((len(given),)),
        ]
        + [pltpu.SemaphoreType.DMA((sides,))] * 4
        + [
            pltpu.VMEM((4, 4, 4, BLOCK), F32),
            pltpu.SemaphoreType.DMA((3,)),
            pltpu.SemaphoreType.DMA((3,)),
            pltpu.SemaphoreType.DMA,
            pltpu.SemaphoreType.DMA,
            pltpu.SemaphoreType.REGULAR,
        ],
        compiler_params=pltpu.CompilerParams(
            collective_id=0, has_side_effects=True, vmem_limit_bytes=24 << 20
        ),
        name="particle_step",
    )(*(pltpu.with_memory_space_constraint(x, pltpu.HBM) for x in given))
    density, accel, abund = pl.pallas_call(
        deliver,
        out_shape=(
            jax.ShapeDtypeStruct(tile, F32),
            jax.ShapeDtypeStruct(position.shape, F32),
            jax.ShapeDtypeStruct(species.shape, F32),
        ),
        in_specs=[vmem] * 3,
        out_specs=(hbm,) * 3,
        scratch_shapes=[pltpu.SemaphoreType.DMA((3,))],
        compiler_params=pltpu.CompilerParams(vmem_limit_bytes=1 << 20),
        name="deliver",
    )(density, accel, abund)
    return density.reshape(-1), accel, abund


def solution(mesh):
    flat = P(("dom", "sub"))
    wide = P(None, ("dom", "sub"))
    tall = P(("dom", "sub"), None)
    return jax.shard_map(
        on_device,
        mesh=mesh,
        in_specs=(wide, flat, flat, flat, wide, tall, tall, tall, P(), P(), flat, flat),
        out_specs=(flat, wide, wide),
        check_vma=False,
    )
```

```python
import functools

import jax
import jax.numpy as jnp
from jax import lax
from jax.experimental import pallas as pl
from jax.experimental.pallas import tpu as pltpu
from jax.sharding import PartitionSpec as P

BLOCK = 128
BLOCKS = 32
NBR = 4
SLOTS = 16
SPECIES = 12
S_LO = 4
SMAX = 32
HALF = BLOCKS * BLOCK // 2
FEAT = 48
GROUPS = 4
SPLIT = 24
FIRST = 32
MESH = pl.DeviceIdType.MESH
F32 = jnp.float32
BF16 = jnp.bfloat16
HIGH = lax.Precision.HIGHEST

gamma_gas = 5.0 / 3.0
chem_tau = 0.5


def pieces(value):
    high = value.astype(BF16).astype(F32)
    rest = value - high
    middle = rest.astype(BF16).astype(F32)
    return high, middle, rest - middle


def halves(value):
    high = value.astype(BF16)
    return high, (value - high.astype(F32)).astype(BF16)


def mm(a, b):
    return jnp.dot(a, b, preferred_element_type=F32)


def source_features(fields):
    high, middle, low = pieces(fields)
    return jnp.concatenate([high, high, high, middle, middle, low], 0).T.astype(BF16)


def weighted(place, weight):
    norm = jnp.sum(place * place, axis=0, keepdims=True)
    return jnp.concatenate(
        [place * weight, weight, norm * weight, jnp.zeros((3, BLOCK), F32)], 0
    )


def gradient_rows(fields, factor):
    row = lax.broadcasted_iota(jnp.int32, fields.shape, 0)
    both = jnp.where(row < 4, fields, pltpu.roll(fields, 4, 0))
    high, low = halves(both * jnp.where(row < 4, 1.0, factor))
    return jnp.concatenate([high, low], 0)


def distances(features, target, place):
    for k in range(0, len(features), 2):
        place[k // 2] = mm(jnp.concatenate(features[k : k + 2], 1), target)


def pair_terms(place, count, cubes, dens, row):
    total = None
    for k in range(count):
        for half in range(2):
            base = 1.0 / place[k, :, half * BLOCK : (half + 1) * BLOCK]
            squared = base * base
            at = (2 * k + half) * BLOCK
            cubes[at : at + BLOCK] = squared * base
            part = jnp.sum(squared.reshape(BLOCK // 8, 8, BLOCK), axis=0)
            total = part if total is None else total + part
    dens[pl.ds(row, 1)] = jnp.sum(total, axis=0, keepdims=True)


def pair_sums(rows, cubes):
    high, low = halves(cubes[...])
    lhs = jnp.concatenate(rows, 1)
    out = mm(lhs, high) + mm(lhs, low)
    return out[0:8] + out[8:16]


def spread(matrix):
    wide = 2 * SPECIES
    tall = jnp.concatenate([matrix, matrix], 0)
    full = jnp.concatenate([tall, tall], 1)
    same = (
        lax.broadcasted_iota(jnp.int32, (wide, wide), 0) // SPECIES
        == lax.broadcasted_iota(jnp.int32, (wide, wide), 1) // SPECIES
    )
    return jnp.where(same, full, 0.0)


def left_side(matrix):
    high, low = halves(matrix)
    blank = jnp.zeros((matrix.shape[0], 8), F32)
    high, low = high.astype(F32), low.astype(F32)
    return jnp.concatenate([high, blank, high, blank, low, blank], 1).astype(BF16)


def right_side(state):
    high, low = halves(jnp.concatenate([state, jnp.zeros((8, state.shape[1]), F32)], 0))
    return jnp.concatenate([high, low, high], 0)


def kernel(
    pos_in,
    width_in,
    mass_in,
    energy_in,
    species_in,
    neigh_in,
    exports_in,
    imports_in,
    jac_in,
    rates_in,
    steps_in,
    slot_in,
    density,
    accel,
    abund_all,
    pos,
    width,
    mass,
    energy,
    species,
    neigh,
    exports,
    imports,
    jac,
    rates,
    steps,
    slot,
    fields,
    targets,
    feats,
    far_feats,
    even,
    odd,
    far_ring,
    raw,
    stage,
    far_raw,
    far_fields,
    factor,
    stage_factor,
    far_factor,
    rows,
    far_rows,
    near_cubes,
    far_cubes,
    near_dens,
    far_dens,
    near_acc,
    far_acc,
    root_mass,
    gain,
    limit,
    state,
    rate_in,
    load_sem,
    send_one,
    recv_one,
    send_two,
    recv_two,
    relay,
    send_mate,
    recv_mate,
    send_wrap,
    recv_wrap,
    ready,
):
    dom = lax.axis_index("dom")
    sub = lax.axis_index("sub")
    doms = lax.axis_size("dom")
    subs = lax.axis_size("sub")
    sides = [lax.rem(dom + doms - 1, doms), lax.rem(dom + 1, doms)]
    barrier = pltpu.get_barrier_semaphore()
    last = doms - 1
    for q in range(subs):
        pl.semaphore_signal(barrier, inc=1, device_id=(sides[0], q), device_id_type=MESH)

    @pl.when(dom < last - 1)
    def _():
        for q in range(subs):
            pl.semaphore_signal(barrier, inc=1, device_id=(sides[1], q), device_id_type=MESH)

    mates = [lax.rem(sub + k, subs) for k in range(1, subs)]

    @pl.when(dom == 0)
    def _():
        for q in mates:
            pl.semaphore_signal(barrier, inc=1, device_id=(dom, q), device_id_type=MESH)

    @pl.when(dom == last)
    def _():
        pl.semaphore_wait(barrier, subs)
        pl.semaphore_signal(ready, inc=1, device_id=(sides[1], sub), device_id_type=MESH)


    pairs = {
        "pos": (pos_in, pos),
        "mass": (mass_in, mass),
        "imports": (imports_in, imports),
        "width": (width_in, width),
        "neigh": (neigh_in, neigh),
        "exports": (exports_in, exports),
        "jac": (jac_in, jac),
        "rates": (rates_in, rates),
        "energy": (energy_in, energy),
        "steps": (steps_in, steps),
        "slot": (slot_in, slot),
        "species": (species_in, species),
    }
    loads = {}
    for i, (name, (source, target)) in enumerate(pairs.items()):
        loads[name] = pltpu.make_async_copy(source, target, load_sem.at[i])
        loads[name].start()

    def exchange(sent, landed, send_sem, recv_sem):
        copies = []
        for e in range(2):
            for q in range(subs):
                copies.append(
                    pltpu.make_async_remote_copy(
                        src_ref=sent.at[e * subs + q],
                        dst_ref=landed.at[(1 - e) * subs + sub],
                        send_sem=send_sem.at[e * subs + q],
                        recv_sem=recv_sem.at[(1 - e) * subs + sub],
                        device_id=(sides[e], q),
                        device_id_type=MESH,
                    )
                )
        return copies

    def arrive(place, sent, landed, send_sem, recv_sem):
        pltpu.make_async_remote_copy(
            src_ref=sent.at[place],
            dst_ref=landed.at[place],
            send_sem=send_sem.at[place],
            recv_sem=recv_sem.at[place],
            device_id=(sides[0], 0),
            device_id_type=MESH,
        ).wait_recv()

    feats[...] = jnp.zeros_like(feats)
    targets[...] = jnp.zeros_like(targets)
    far_feats[...] = jnp.zeros_like(far_feats)
    loads["pos"].wait()
    loads["mass"].wait()
    root_mass[...] = 1.0 / jnp.sqrt(mass[...])

    def prepare(b, _):
        place = pos[:, pl.ds(pl.multiple_of(b * BLOCK, BLOCK), BLOCK)]
        raw[b, 0:3] = place
        raw[b, 3:4] = root_mass[pl.ds(b, 1)]
        return 0

    lax.fori_loop(0, BLOCKS, prepare, 0, unroll=8)
    loads["imports"].wait()
    for r in range(SLOTS):
        for k in range(2):
            stage[r // 2, (r % 2) * 2 + k] = raw[imports[k, r]]
    loads["width"].wait()
    loads["neigh"].wait()
    loads["exports"].wait()
    loads["jac"].wait()
    loads["rates"].wait()
    first = exchange(stage, far_raw, send_one, recv_one)
    relayed = [
        pltpu.make_async_remote_copy(
            src_ref=stage.at[q],
            dst_ref=relay.at[sub],
            send_sem=send_mate.at[k],
            recv_sem=recv_mate.at[k],
            device_id=(dom, q),
            device_id_type=MESH,
        )
        for k, q in enumerate(mates)
    ]
    wrapped = pltpu.make_async_remote_copy(
        src_ref=relay,
        dst_ref=far_raw.at[pl.ds(subs, subs)],
        send_sem=send_wrap,
        recv_sem=recv_wrap,
        device_id=(sides[0], sub),
        device_id_type=MESH,
    )

    @pl.when(dom != last)
    def _():
        pl.semaphore_wait(barrier, jnp.where(dom == 0, 2 * subs - 1, 2 * subs))

    @pl.when(dom == last - 1)
    def _():
        for q in range(subs):
            pl.semaphore_signal(ready, inc=1, device_id=(sides[1], q), device_id_type=MESH)

    for copy in first[subs:]:
        copy.start()

    @pl.when((dom != 0) & (dom != last))
    def _():
        for copy in first[:subs]:
            copy.start()

    @pl.when(dom == 0)
    def _():
        for copy in relayed:
            copy.start()
        relay[sub] = stage[sub]


    def shape_block(b):
        place = pos[:, pl.ds(pl.multiple_of(b * BLOCK, BLOCK), BLOCK)]
        norm = jnp.sum(place * place, axis=0, keepdims=True)
        span = width[pl.ds(b, 1)]
        target = jnp.concatenate(
            [place * -2.0, span * span + norm, jnp.ones_like(norm), jnp.zeros((3, BLOCK), F32)], 0
        )
        high, middle, low = pieces(target)
        split = jnp.concatenate([high, middle, low, high, middle, high], 0).astype(BF16)
        targets[b, 0:FEAT, 0:BLOCK] = split
        targets[b, BLOCK : BLOCK + FEAT, BLOCK : 2 * BLOCK] = split
        full = weighted(place, root_mass[pl.ds(b, 1)])
        fields[b] = full
        feats[b, :, 0:FEAT] = source_features(full)

    for b in range(FIRST):
        shape_block(b)
    jac_full = spread(jac[...])
    rate_full = spread(rates[...])
    both = jnp.dot(rates[...], jac[...], precision=HIGH, preferred_element_type=F32)
    left = left_side(jnp.concatenate([spread(both), jac_full], 0))
    left_first = left_side(rate_full)

    def fill(b, place):
        distances([feats[neigh[k, b]] for k in range(NBR)], targets[b], place)

    def drain(b, place):
        pair_terms(place, NBR // 2, near_cubes.at[b], near_dens, b)

    ring = [even.at[0], even.at[1], odd.at[0], odd.at[1]]
    fill(0, ring[0])
    fill(1, ring[1])
    for b in range(BLOCKS):
        if b + 2 < BLOCKS:
            fill(b + 2, ring[(b + 2) % 4])
        drain(b, ring[b % 4])
    for name in ("energy", "steps", "slot", "species"):
        loads[name].wait()

    @pl.when(dom == 0)
    def _():
        for k in range(subs - 1):
            pltpu.make_async_remote_copy(
                src_ref=stage.at[0],
                dst_ref=relay.at[lax.rem(sub + subs - 1 - k, subs)],
                send_sem=send_mate.at[k],
                recv_sem=recv_mate.at[k],
                device_id=(dom, mates[k]),
                device_id_type=MESH,
            ).wait_recv()
        pl.semaphore_wait(ready, 1)
        wrapped.start()

    @pl.when(dom == last)
    def _():
        pl.semaphore_wait(ready, subs)
        for copy in first[:subs]:
            copy.start()


    early = jnp.where(dom == 1, 1, 1 - lax.rem(dom, 2))
    order = []
    for e in (early, 1 - early):
        for d in (0, 1, 3, 2):
            order.append(e * subs + lax.rem(sub + d, subs))

    def far_fill(i):
        place = order[i]
        for k in range(4):
            full = weighted(far_raw[place, k, 0:3], far_raw[place, k, 3:4])
            far_fields[place, k] = full
            far_feats[i * 4 + k, :, 0:FEAT] = source_features(full)
        for x in range(2):
            parts = [far_feats[i * 4 + 2 * x + k] for k in range(2)]
            distances(parts, targets[exports[x, place]], far_ring.at[pl.ds(2 * i + x, 1)])

    def far_drain(i):
        for x in range(2):
            at = 2 * i + x
            pair_terms(far_ring.at[pl.ds(at, 1)], 1, far_cubes.at[at], far_dens, at)

    before = ()
    for group in ((0, 1, 2, 3), (4, 5), (6,), (7,)):
        if group[0] < subs:
            for i in group:
                arrive(order[i], stage, far_raw, send_one, recv_one)
        else:

            @pl.when(dom != last)
            def _():
                for i in group:
                    arrive(order[i], stage, far_raw, send_one, recv_one)

            if group[0] == subs:

                @pl.when(dom == last)
                def _():
                    wrapped.wait_recv()

        for i in group:
            far_fill(i)
        for i in before:
            far_drain(i)
        before = group
    for i in before:
        far_drain(i)

    owner = lax.broadcasted_iota(jnp.int32, (BLOCKS, BLOCK), 0)
    total = near_dens[...]
    for r in range(SLOTS):
        total += jnp.where(owner == exports[r % 2, order[r // 2]], far_dens[r : r + 1], 0.0)
    dens = total * width[...]
    density[...] = dens
    factor[...] = (gamma_gas - 1.0) * energy[...] / dens
    for r in range(SLOTS):
        for k in range(2):
            stage_factor[r // 2, pl.ds((r % 2) * 2 + k, 1)] = factor[pl.ds(imports[k, r], 1)]
    second = exchange(stage_factor, far_factor, send_two, recv_two)
    for copy in second[subs:] + second[:subs]:
        copy.start()
    gain_all = chem_tau * (dens / (dens + 1.0))
    most = jnp.where(slot[...] >= 0, steps[...], jnp.minimum(steps[...], S_LO)).astype(F32)
    for b in range(BLOCKS // 2):
        for h in range(2):
            block = b + h * (BLOCKS // 2)
            at = pl.ds(b * BLOCK, BLOCK)
            span = pl.ds(h * SPECIES, SPECIES)
            gain[span, at] = jnp.broadcast_to(gain_all[block : block + 1], (SPECIES, BLOCK))
            limit[span, at] = jnp.broadcast_to(most[block : block + 1], (SPECIES, BLOCK))
    state[0:SPECIES] = species[:, 0:HALF]
    state[SPECIES : 2 * SPECIES] = species[:, HALF : 2 * HALF]
    part = HALF // GROUPS
    for g in range(GROUPS):
        at = pl.ds(g * part, part)
        rate_in[:, at] = mm(left_first, right_side(state[:, at]))

    def rows_near(b, _):
        rows[b] = gradient_rows(fields[b], factor[pl.ds(b, 1)])
        return 0

    lax.fori_loop(0, BLOCKS, rows_near, 0, unroll=8)

    def chem_step(c):
        for g in range(GROUPS):
            at = pl.ds(g * part, part)
            abund = state[:, at]
            lift = gain[:, at]
            moved = (abund + lift) + lift * jnp.tanh(rate_in[:, at])
            out = mm(left, right_side(moved))
            rate_in[:, at] = out[: 2 * SPECIES]
            state[:, at] = jnp.where(limit[:, at] > c, out[2 * SPECIES :], abund)

    for c in range(SMAX // 2):
        chem_step(c)
        for b in (2 * c, 2 * c + 1):
            near_acc[b] = pair_sums([rows[neigh[k, b]] for k in range(NBR)], near_cubes.at[b])

    row = lax.broadcasted_iota(jnp.int32, (8, BLOCK), 0)
    lane = lax.broadcasted_iota(jnp.int32, (8, BLOCK), 1)
    named = jnp.zeros((8, BLOCK), jnp.int32)
    for r in range(SLOTS):
        named = jnp.where(lane // 8 == r, exports[r % 2, order[r // 2]], named)
    named = jnp.where(lane % 8 == row, named, -1)
    pick = jnp.concatenate(
        [jnp.where(named == b, 1.0, 0.0) for b in range(BLOCKS)], 0
    ).astype(BF16)
    for c in range(16, SPLIT):
        chem_step(c)

    def rows_far(group):
        for i in group:
            arrive(order[i], stage_factor, far_factor, send_two, recv_two)
        for i in group:
            place = order[i]
            for k in range(4):
                far_rows[i * 4 + k] = gradient_rows(
                    far_fields[place, k], far_factor[place, pl.ds(k, 1)]
                )

    def sums_far(i, x):
        at = 2 * i + x
        parts = [far_rows[i * 4 + 2 * x + k] for k in range(2)]
        far_acc[at] = pair_sums(parts, far_cubes.at[at])

    rows_far((0, 1, 2, 3))
    slots = [(i, x) for i in range(4) for x in range(2)]
    for c in range(SPLIT, SMAX):
        chem_step(c)
        n = 8 // (SMAX - SPLIT)
        for i, x in slots[(c - SPLIT) * n : (c - SPLIT + 1) * n]:
            sums_far(i, x)
    for group in ((4, 5), (6,), (7,)):
        rows_far(group)
        for i in group:
            for x in range(2):
                sums_far(i, x)
    high, low = halves(far_acc[...].reshape(SLOTS * 8, BLOCK))
    far_all = mm(jnp.concatenate([pick, pick], 1), jnp.concatenate([high, low], 0))
    for b in range(BLOCKS):
        acc = near_acc[b] + far_all[b * 8 : b * 8 + 8]
        acc = acc * jnp.where(row < 4, factor[b : b + 1], 1.0)
        acc = acc + pltpu.roll(acc, 4, 0)
        at = pl.ds(b * BLOCK, BLOCK)
        accel[:, at] = (4.0 * width[b : b + 1]) * (pos[:, at] * acc[3:4] - acc[0:3])
    abund_all[:, 0:HALF] = state[0:SPECIES]
    abund_all[:, HALF : 2 * HALF] = state[SPECIES : 2 * SPECIES]
    for copy in first[subs:] + second:
        copy.wait_send()

    @pl.when(dom != 0)
    def _():
        for copy in first[:subs]:
            copy.wait_send()

    @pl.when(dom == 0)
    def _():
        for copy in relayed + [wrapped]:
            copy.wait_send()


def deliver(density, accel, abund, dens_out, accel_out, abund_out, sems):
    pairs = ((abund, abund_out), (accel, accel_out), (density, dens_out))
    copies = [pltpu.make_async_copy(a, b, sems.at[i]) for i, (a, b) in enumerate(pairs)]
    for copy in copies:
        copy.start()
    for copy in copies:
        copy.wait()


def on_device(
    position,
    smoothing,
    mass,
    energy,
    species,
    neighbours,
    exports,
    imports,
    jac_inverse,
    rates,
    chem_steps,
    dense_slot,
):
    tile = (BLOCKS, BLOCK)
    vmem = pl.BlockSpec(memory_space=pltpu.VMEM)
    hbm = pl.BlockSpec(memory_space=pltpu.HBM)
    far = 2 * SLOTS
    sides = SLOTS // 2
    chem = (2 * SPECIES, HALF)
    given = (
        position,
        smoothing.reshape(tile),
        mass.reshape(tile),
        energy.reshape(tile),
        species,
        neighbours.T,
        exports.T,
        imports.T,
        jac_inverse,
        rates,
        chem_steps.reshape(tile),
        dense_slot.reshape(tile),
    )
    spaces = [pltpu.VMEM] * 5 + [pltpu.SMEM] * 3 + [pltpu.VMEM] * 4
    density, accel, abund = pl.pallas_call(
        kernel,
        out_shape=(
            pltpu.VMEM(tile, F32),
            pltpu.VMEM(position.shape, F32),
            pltpu.VMEM(species.shape, F32),
        ),
        in_specs=[hbm] * len(given),
        out_specs=(vmem, vmem, vmem),
        scratch_shapes=[space(x.shape, x.dtype) for space, x in zip(spaces, given)]
        + [
            pltpu.VMEM((BLOCKS, 8, BLOCK), F32),
            pltpu.VMEM((BLOCKS, 2 * BLOCK, 2 * BLOCK), BF16),
            pltpu.VMEM((BLOCKS, BLOCK, BLOCK), BF16),
            pltpu.VMEM((far, BLOCK, BLOCK), BF16),
            pltpu.VMEM((2, NBR // 2, BLOCK, 2 * BLOCK), F32),
            pltpu.VMEM((2, NBR // 2, BLOCK, 2 * BLOCK), F32),
            pltpu.VMEM((SLOTS, BLOCK, 2 * BLOCK), F32),
            pltpu.VMEM((BLOCKS, 4, BLOCK), F32),
            pltpu.VMEM((sides, 4, 4, BLOCK), F32),
            pltpu.VMEM((sides, 4, 4, BLOCK), F32),
            pltpu.VMEM((sides, 4, 8, BLOCK), F32),
            pltpu.VMEM(tile, F32),
            pltpu.VMEM((sides, 4, BLOCK), F32),
            pltpu.VMEM((sides, 4, BLOCK), F32),
            pltpu.VMEM((BLOCKS, 16, BLOCK), BF16),
            pltpu.VMEM((far, 16, BLOCK), BF16),
            pltpu.VMEM((BLOCKS, NBR * BLOCK, BLOCK), F32),
            pltpu.VMEM((SLOTS, 2 * BLOCK, BLOCK), F32),
            pltpu.VMEM(tile, F32),
            pltpu.VMEM((SLOTS, BLOCK), F32),
            pltpu.VMEM((BLOCKS, 8, BLOCK), F32),
            pltpu.VMEM((SLOTS, 8, BLOCK), F32),
            pltpu.VMEM(tile, F32),
            pltpu.VMEM(chem, F32),
            pltpu.VMEM(chem, F32),
            pltpu.VMEM(chem, F32),
            pltpu.VMEM(chem, F32),
            pltpu.SemaphoreType.DMA((len(given),)),
        ]
        + [pltpu.SemaphoreType.DMA((sides,))] * 4
        + [
            pltpu.VMEM((4, 4, 4, BLOCK), F32),
            pltpu.SemaphoreType.DMA((3,)),
            pltpu.SemaphoreType.DMA((3,)),
            pltpu.SemaphoreType.DMA,
            pltpu.SemaphoreType.DMA,
            pltpu.SemaphoreType.REGULAR,
        ],
        compiler_params=pltpu.CompilerParams(
            collective_id=0, has_side_effects=True, vmem_limit_bytes=24 << 20
        ),
        name="particle_step",
    )(*(pltpu.with_memory_space_constraint(x, pltpu.HBM) for x in given))
    density, accel, abund = pl.pallas_call(
        deliver,
        out_shape=(
            jax.ShapeDtypeStruct(tile, F32),
            jax.ShapeDtypeStruct(position.shape, F32),
            jax.ShapeDtypeStruct(species.shape, F32),
        ),
        in_specs=[vmem] * 3,
        out_specs=(hbm,) * 3,
        scratch_shapes=[pltpu.SemaphoreType.DMA((3,))],
        compiler_params=pltpu.CompilerParams(vmem_limit_bytes=1 << 20),
        name="deliver",
    )(density, accel, abund)
    return density.reshape(-1), accel, abund


def solution(mesh):
    flat = P(("dom", "sub"))
    wide = P(None, ("dom", "sub"))
    tall = P(("dom", "sub"), None)
    return jax.shard_map(
        on_device,
        mesh=mesh,
        in_specs=(wide, flat, flat, flat, wide, tall, tall, tall, P(), P(), flat, flat),
        out_specs=(flat, wide, wide),
        check_vma=False,
    )
```

```python
import functools

import jax
import jax.numpy as jnp
from jax import lax
from jax.experimental import pallas as pl
from jax.experimental.pallas import tpu as pltpu
from jax.sharding import PartitionSpec as P

BLOCK = 128
BLOCKS = 32
NBR = 4
SLOTS = 16
SPECIES = 12
S_LO = 4
SMAX = 32
HALF = BLOCKS * BLOCK // 2
FEAT = 48
GROUPS = 4
SPLIT = 24
FIRST = 32
MESH = pl.DeviceIdType.MESH
F32 = jnp.float32
BF16 = jnp.bfloat16
HIGH = lax.Precision.HIGHEST

gamma_gas = 5.0 / 3.0
chem_tau = 0.5


def pieces(value):
    high = value.astype(BF16).astype(F32)
    rest = value - high
    middle = rest.astype(BF16).astype(F32)
    return high, middle, rest - middle


def halves(value):
    high = value.astype(BF16)
    return high, (value - high.astype(F32)).astype(BF16)


def mm(a, b):
    return jnp.dot(a, b, preferred_element_type=F32)


def source_features(fields):
    high, middle, low = pieces(fields)
    return jnp.concatenate([high, high, high, middle, middle, low], 0).T.astype(BF16)


def weighted(place, weight):
    norm = jnp.sum(place * place, axis=0, keepdims=True)
    return jnp.concatenate(
        [place * weight, weight, norm * weight, jnp.zeros((3, BLOCK), F32)], 0
    )


def gradient_rows(fields, factor):
    row = lax.broadcasted_iota(jnp.int32, fields.shape, 0)
    both = jnp.where(row < 4, fields, pltpu.roll(fields, 4, 0))
    high, low = halves(both * jnp.where(row < 4, 1.0, factor))
    return jnp.concatenate([high, low], 0)


def distances(features, target, place):
    for k in range(0, len(features), 2):
        place[k // 2] = mm(jnp.concatenate(features[k : k + 2], 1), target)


def pair_terms(place, count, cubes, dens, row):
    total = None
    for k in range(count):
        for half in range(2):
            base = 1.0 / place[k, :, half * BLOCK : (half + 1) * BLOCK]
            squared = base * base
            at = (2 * k + half) * BLOCK
            cubes[at : at + BLOCK] = squared * base
            part = jnp.sum(squared.reshape(BLOCK // 8, 8, BLOCK), axis=0)
            total = part if total is None else total + part
    dens[pl.ds(row, 1)] = jnp.sum(total, axis=0, keepdims=True)


def pair_sums(rows, cubes):
    high, low = halves(cubes[...])
    lhs = jnp.concatenate(rows, 1)
    out = mm(lhs, high) + mm(lhs, low)
    return out[0:8] + out[8:16]


def spread(matrix):
    wide = 2 * SPECIES
    tall = jnp.concatenate([matrix, matrix], 0)
    full = jnp.concatenate([tall, tall], 1)
    same = (
        lax.broadcasted_iota(jnp.int32, (wide, wide), 0) // SPECIES
        == lax.broadcasted_iota(jnp.int32, (wide, wide), 1) // SPECIES
    )
    return jnp.where(same, full, 0.0)


def left_side(matrix):
    high, low = halves(matrix)
    blank = jnp.zeros((matrix.shape[0], 8), F32)
    high, low = high.astype(F32), low.astype(F32)
    return jnp.concatenate([high, blank, high, blank, low, blank], 1).astype(BF16)


def right_side(state):
    high, low = halves(jnp.concatenate([state, jnp.zeros((8, state.shape[1]), F32)], 0))
    return jnp.concatenate([high, low, high], 0)


def kernel(
    pos_in,
    width_in,
    mass_in,
    energy_in,
    species_in,
    neigh_in,
    exports_in,
    imports_in,
    jac_in,
    rates_in,
    steps_in,
    slot_in,
    density,
    accel,
    abund_all,
    pos,
    width,
    mass,
    energy,
    species,
    neigh,
    exports,
    imports,
    jac,
    rates,
    steps,
    slot,
    fields,
    targets,
    feats,
    far_feats,
    even,
    odd,
    far_ring,
    raw,
    stage,
    far_raw,
    far_fields,
    factor,
    stage_factor,
    far_factor,
    rows,
    far_rows,
    near_cubes,
    far_cubes,
    near_dens,
    far_dens,
    near_acc,
    far_acc,
    root_mass,
    gain,
    limit,
    state,
    rate_in,
    load_sem,
    send_one,
    recv_one,
    send_two,
    recv_two,
    relay,
    send_mate,
    recv_mate,
    send_wrap,
    recv_wrap,
    ready,
):
    dom = lax.axis_index("dom")
    sub = lax.axis_index("sub")
    doms = lax.axis_size("dom")
    subs = lax.axis_size("sub")
    sides = [lax.rem(dom + doms - 1, doms), lax.rem(dom + 1, doms)]
    barrier = pltpu.get_barrier_semaphore()
    last = doms - 1
    for q in range(subs):
        pl.semaphore_signal(barrier, inc=1, device_id=(sides[0], q), device_id_type=MESH)

    @pl.when(dom < last - 1)
    def _():
        for q in range(subs):
            pl.semaphore_signal(barrier, inc=1, device_id=(sides[1], q), device_id_type=MESH)

    mates = [lax.rem(sub + k, subs) for k in range(1, subs)]

    @pl.when(dom == 0)
    def _():
        for q in mates:
            pl.semaphore_signal(barrier, inc=1, device_id=(dom, q), device_id_type=MESH)

    @pl.when(dom == last)
    def _():
        pl.semaphore_wait(barrier, subs)
        pl.semaphore_signal(ready, inc=1, device_id=(sides[1], sub), device_id_type=MESH)


    pairs = {
        "pos": (pos_in, pos),
        "mass": (mass_in, mass),
        "imports": (imports_in, imports),
        "width": (width_in, width),
        "neigh": (neigh_in, neigh),
        "exports": (exports_in, exports),
        "jac": (jac_in, jac),
        "rates": (rates_in, rates),
        "energy": (energy_in, energy),
        "steps": (steps_in, steps),
        "slot": (slot_in, slot),
        "species": (species_in, species),
    }
    loads = {}
    for i, (name, (source, target)) in enumerate(pairs.items()):
        loads[name] = pltpu.make_async_copy(source, target, load_sem.at[i])
        loads[name].start()

    def exchange(sent, landed, send_sem, recv_sem):
        copies = []
        for e in range(2):
            for q in range(subs):
                copies.append(
                    pltpu.make_async_remote_copy(
                        src_ref=sent.at[e * subs + q],
                        dst_ref=landed.at[(1 - e) * subs + sub],
                        send_sem=send_sem.at[e * subs + q],
                        recv_sem=recv_sem.at[(1 - e) * subs + sub],
                        device_id=(sides[e], q),
                        device_id_type=MESH,
                    )
                )
        return copies

    def arrive(place, sent, landed, send_sem, recv_sem):
        pltpu.make_async_remote_copy(
            src_ref=sent.at[place],
            dst_ref=landed.at[place],
            send_sem=send_sem.at[place],
            recv_sem=recv_sem.at[place],
            device_id=(sides[0], 0),
            device_id_type=MESH,
        ).wait_recv()

    feats[...] = jnp.zeros_like(feats)
    targets[...] = jnp.zeros_like(targets)
    far_feats[...] = jnp.zeros_like(far_feats)
    loads["pos"].wait()
    loads["mass"].wait()
    root_mass[...] = 1.0 / jnp.sqrt(mass[...])

    def prepare(b, _):
        place = pos[:, pl.ds(pl.multiple_of(b * BLOCK, BLOCK), BLOCK)]
        raw[b, 0:3] = place
        raw[b, 3:4] = root_mass[pl.ds(b, 1)]
        return 0

    lax.fori_loop(0, BLOCKS, prepare, 0, unroll=8)
    loads["imports"].wait()
    for r in range(SLOTS):
        for k in range(2):
            stage[r // 2, (r % 2) * 2 + k] = raw[imports[k, r]]
    first = exchange(stage, far_raw, send_one, recv_one)
    relayed = [
        pltpu.make_async_remote_copy(
            src_ref=stage.at[q],
            dst_ref=relay.at[sub],
            send_sem=send_mate.at[k],
            recv_sem=recv_mate.at[k],
            device_id=(dom, q),
            device_id_type=MESH,
        )
        for k, q in enumerate(mates)
    ]
    wrapped = pltpu.make_async_remote_copy(
        src_ref=relay,
        dst_ref=far_raw.at[pl.ds(subs, subs)],
        send_sem=send_wrap,
        recv_sem=recv_wrap,
        device_id=(sides[0], sub),
        device_id_type=MESH,
    )

    @pl.when(dom != last)
    def _():
        pl.semaphore_wait(barrier, jnp.where(dom == 0, 2 * subs - 1, 2 * subs))

    @pl.when(dom == last - 1)
    def _():
        for q in range(subs):
            pl.semaphore_signal(ready, inc=1, device_id=(sides[1], q), device_id_type=MESH)

    for copy in first[subs:]:
        copy.start()

    @pl.when((dom != 0) & (dom != last))
    def _():
        for copy in first[:subs]:
            copy.start()

    @pl.when(dom == 0)
    def _():
        for copy in relayed:
            copy.start()
        relay[sub] = stage[sub]


    loads["width"].wait()
    loads["neigh"].wait()
    loads["exports"].wait()
    loads["jac"].wait()
    loads["rates"].wait()

    def shape_block(b):
        place = pos[:, pl.ds(pl.multiple_of(b * BLOCK, BLOCK), BLOCK)]
        norm = jnp.sum(place * place, axis=0, keepdims=True)
        span = width[pl.ds(b, 1)]
        target = jnp.concatenate(
            [place * -2.0, span * span + norm, jnp.ones_like(norm), jnp.zeros((3, BLOCK), F32)], 0
        )
        high, middle, low = pieces(target)
        split = jnp.concatenate([high, middle, low, high, middle, high], 0).astype(BF16)
        targets[b, 0:FEAT, 0:BLOCK] = split
        targets[b, BLOCK : BLOCK + FEAT, BLOCK : 2 * BLOCK] = split
        full = weighted(place, root_mass[pl.ds(b, 1)])
        fields[b] = full
        feats[b, :, 0:FEAT] = source_features(full)

    for b in range(FIRST):
        shape_block(b)
    jac_full = spread(jac[...])
    rate_full = spread(rates[...])
    both = jnp.dot(rates[...], jac[...], precision=HIGH, preferred_element_type=F32)
    left = left_side(jnp.concatenate([spread(both), jac_full], 0))
    left_first = left_side(rate_full)

    def fill(b, place):
        distances([feats[neigh[k, b]] for k in range(NBR)], targets[b], place)

    def drain(b, place):
        pair_terms(place, NBR // 2, near_cubes.at[b], near_dens, b)

    ring = [even.at[0], even.at[1], odd.at[0], odd.at[1]]
    fill(0, ring[0])
    fill(1, ring[1])
    for b in range(BLOCKS):
        if b + 2 < BLOCKS:
            fill(b + 2, ring[(b + 2) % 4])
        drain(b, ring[b % 4])
    for name in ("energy", "steps", "slot", "species"):
        loads[name].wait()

    @pl.when(dom == 0)
    def _():
        for k in range(subs - 1):
            pltpu.make_async_remote_copy(
                src_ref=stage.at[0],
                dst_ref=relay.at[lax.rem(sub + subs - 1 - k, subs)],
                send_sem=send_mate.at[k],
                recv_sem=recv_mate.at[k],
                device_id=(dom, mates[k]),
                device_id_type=MESH,
            ).wait_recv()
        pl.semaphore_wait(ready, 1)
        wrapped.start()

    @pl.when(dom == last)
    def _():
        pl.semaphore_wait(ready, subs)
        for copy in first[:subs]:
            copy.start()


    early = jnp.where(dom == 1, 1, 1 - lax.rem(dom, 2))
    order = []
    for e in (early, 1 - early):
        for d in (0, 1, 3, 2):
            order.append(e * subs + lax.rem(sub + d, subs))

    def far_fill(i):
        place = order[i]
        for k in range(4):
            full = weighted(far_raw[place, k, 0:3], far_raw[place, k, 3:4])
            far_fields[place, k] = full
            far_feats[i * 4 + k, :, 0:FEAT] = source_features(full)
        for x in range(2):
            parts = [far_feats[i * 4 + 2 * x + k] for k in range(2)]
            distances(parts, targets[exports[x, place]], far_ring.at[pl.ds(2 * i + x, 1)])

    def far_drain(i):
        for x in range(2):
            at = 2 * i + x
            pair_terms(far_ring.at[pl.ds(at, 1)], 1, far_cubes.at[at], far_dens, at)

    before = ()
    for group in ((0, 1, 2, 3), (4, 5), (6,), (7,)):
        if group[0] < subs:
            for i in group:
                arrive(order[i], stage, far_raw, send_one, recv_one)
        else:

            @pl.when(dom != last)
            def _():
                for i in group:
                    arrive(order[i], stage, far_raw, send_one, recv_one)

            if group[0] == subs:

                @pl.when(dom == last)
                def _():
                    wrapped.wait_recv()

        for i in group:
            far_fill(i)
        for i in before:
            far_drain(i)
        before = group
    for i in before:
        far_drain(i)

    owner = lax.broadcasted_iota(jnp.int32, (BLOCKS, BLOCK), 0)
    total = near_dens[...]
    for r in range(SLOTS):
        total += jnp.where(owner == exports[r % 2, order[r // 2]], far_dens[r : r + 1], 0.0)
    dens = total * width[...]
    density[...] = dens
    factor[...] = (gamma_gas - 1.0) * energy[...] / dens
    for r in range(SLOTS):
        for k in range(2):
            stage_factor[r // 2, pl.ds((r % 2) * 2 + k, 1)] = factor[pl.ds(imports[k, r], 1)]
    second = exchange(stage_factor, far_factor, send_two, recv_two)
    for copy in second[subs:] + second[:subs]:
        copy.start()
    gain_all = chem_tau * (dens / (dens + 1.0))
    most = jnp.where(slot[...] >= 0, steps[...], jnp.minimum(steps[...], S_LO)).astype(F32)
    for b in range(BLOCKS // 2):
        for h in range(2):
            block = b + h * (BLOCKS // 2)
            at = pl.ds(b * BLOCK, BLOCK)
            span = pl.ds(h * SPECIES, SPECIES)
            gain[span, at] = jnp.broadcast_to(gain_all[block : block + 1], (SPECIES, BLOCK))
            limit[span, at] = jnp.broadcast_to(most[block : block + 1], (SPECIES, BLOCK))
    state[0:SPECIES] = species[:, 0:HALF]
    state[SPECIES : 2 * SPECIES] = species[:, HALF : 2 * HALF]
    part = HALF // GROUPS
    for g in range(GROUPS):
        at = pl.ds(g * part, part)
        rate_in[:, at] = mm(left_first, right_side(state[:, at]))

    def rows_near(b, _):
        rows[b] = gradient_rows(fields[b], factor[pl.ds(b, 1)])
        return 0

    lax.fori_loop(0, BLOCKS, rows_near, 0, unroll=8)

    def chem_step(c):
        for g in range(GROUPS):
            at = pl.ds(g * part, part)
            abund = state[:, at]
            lift = gain[:, at]
            moved = (abund + lift) + lift * jnp.tanh(rate_in[:, at])
            out = mm(left, right_side(moved))
            rate_in[:, at] = out[: 2 * SPECIES]
            state[:, at] = jnp.where(limit[:, at] > c, out[2 * SPECIES :], abund)

    for c in range(SMAX // 2):
        chem_step(c)
        for b in (2 * c, 2 * c + 1):
            near_acc[b] = pair_sums([rows[neigh[k, b]] for k in range(NBR)], near_cubes.at[b])

    row = lax.broadcasted_iota(jnp.int32, (8, BLOCK), 0)
    lane = lax.broadcasted_iota(jnp.int32, (8, BLOCK), 1)
    named = jnp.zeros((8, BLOCK), jnp.int32)
    for r in range(SLOTS):
        named = jnp.where(lane // 8 == r, exports[r % 2, order[r // 2]], named)
    named = jnp.where(lane % 8 == row, named, -1)
    pick = jnp.concatenate(
        [jnp.where(named == b, 1.0, 0.0) for b in range(BLOCKS)], 0
    ).astype(BF16)
    for c in range(16, SPLIT):
        chem_step(c)

    def rows_far(group):
        for i in group:
            arrive(order[i], stage_factor, far_factor, send_two, recv_two)
        for i in group:
            place = order[i]
            for k in range(4):
                far_rows[i * 4 + k] = gradient_rows(
                    far_fields[place, k], far_factor[place, pl.ds(k, 1)]
                )

    def sums_far(i, x):
        at = 2 * i + x
        parts = [far_rows[i * 4 + 2 * x + k] for k in range(2)]
        far_acc[at] = pair_sums(parts, far_cubes.at[at])

    rows_far((0, 1, 2, 3))
    slots = [(i, x) for i in range(4) for x in range(2)]
    for c in range(SPLIT, SMAX):
        chem_step(c)
        n = 8 // (SMAX - SPLIT)
        for i, x in slots[(c - SPLIT) * n : (c - SPLIT + 1) * n]:
            sums_far(i, x)
    abund_all[:, 0:HALF] = state[0:SPECIES]
    abund_all[:, HALF : 2 * HALF] = state[SPECIES : 2 * SPECIES]
    for group in ((4, 5), (6, 7)):
        rows_far(group)
        for i in group:
            for x in range(2):
                sums_far(i, x)
    high, low = halves(far_acc[...].reshape(SLOTS * 8, BLOCK))
    far_all = mm(jnp.concatenate([pick, pick], 1), jnp.concatenate([high, low], 0))
    for b in range(BLOCKS):
        acc = near_acc[b] + far_all[b * 8 : b * 8 + 8]
        acc = acc * jnp.where(row < 4, factor[b : b + 1], 1.0)
        acc = acc + pltpu.roll(acc, 4, 0)
        at = pl.ds(b * BLOCK, BLOCK)
        accel[:, at] = (4.0 * width[b : b + 1]) * (pos[:, at] * acc[3:4] - acc[0:3])
    for copy in first[subs:] + second:
        copy.wait_send()

    @pl.when(dom != 0)
    def _():
        for copy in first[:subs]:
            copy.wait_send()

    @pl.when(dom == 0)
    def _():
        for copy in relayed + [wrapped]:
            copy.wait_send()


def deliver(density, accel, abund, dens_out, accel_out, abund_out, sems):
    pairs = ((abund, abund_out), (accel, accel_out), (density, dens_out))
    copies = [pltpu.make_async_copy(a, b, sems.at[i]) for i, (a, b) in enumerate(pairs)]
    for copy in copies:
        copy.start()
    for copy in copies:
        copy.wait()


def on_device(
    position,
    smoothing,
    mass,
    energy,
    species,
    neighbours,
    exports,
    imports,
    jac_inverse,
    rates,
    chem_steps,
    dense_slot,
):
    tile = (BLOCKS, BLOCK)
    vmem = pl.BlockSpec(memory_space=pltpu.VMEM)
    hbm = pl.BlockSpec(memory_space=pltpu.HBM)
    far = 2 * SLOTS
    sides = SLOTS // 2
    chem = (2 * SPECIES, HALF)
    given = (
        position,
        smoothing.reshape(tile),
        mass.reshape(tile),
        energy.reshape(tile),
        species,
        neighbours.T,
        exports.T,
        imports.T,
        jac_inverse,
        rates,
        chem_steps.reshape(tile),
        dense_slot.reshape(tile),
    )
    spaces = [pltpu.VMEM] * 5 + [pltpu.SMEM] * 3 + [pltpu.VMEM] * 4
    density, accel, abund = pl.pallas_call(
        kernel,
        out_shape=(
            pltpu.VMEM(tile, F32),
            pltpu.VMEM(position.shape, F32),
            pltpu.VMEM(species.shape, F32),
        ),
        in_specs=[hbm] * len(given),
        out_specs=(vmem, vmem, vmem),
        scratch_shapes=[space(x.shape, x.dtype) for space, x in zip(spaces, given)]
        + [
            pltpu.VMEM((BLOCKS, 8, BLOCK), F32),
            pltpu.VMEM((BLOCKS, 2 * BLOCK, 2 * BLOCK), BF16),
            pltpu.VMEM((BLOCKS, BLOCK, BLOCK), BF16),
            pltpu.VMEM((far, BLOCK, BLOCK), BF16),
            pltpu.VMEM((2, NBR // 2, BLOCK, 2 * BLOCK), F32),
            pltpu.VMEM((2, NBR // 2, BLOCK, 2 * BLOCK), F32),
            pltpu.VMEM((SLOTS, BLOCK, 2 * BLOCK), F32),
            pltpu.VMEM((BLOCKS, 4, BLOCK), F32),
            pltpu.VMEM((sides, 4, 4, BLOCK), F32),
            pltpu.VMEM((sides, 4, 4, BLOCK), F32),
            pltpu.VMEM((sides, 4, 8, BLOCK), F32),
            pltpu.VMEM(tile, F32),
            pltpu.VMEM((sides, 4, BLOCK), F32),
            pltpu.VMEM((sides, 4, BLOCK), F32),
            pltpu.VMEM((BLOCKS, 16, BLOCK), BF16),
            pltpu.VMEM((far, 16, BLOCK), BF16),
            pltpu.VMEM((BLOCKS, NBR * BLOCK, BLOCK), F32),
            pltpu.VMEM((SLOTS, 2 * BLOCK, BLOCK), F32),
            pltpu.VMEM(tile, F32),
            pltpu.VMEM((SLOTS, BLOCK), F32),
            pltpu.VMEM((BLOCKS, 8, BLOCK), F32),
            pltpu.VMEM((SLOTS, 8, BLOCK), F32),
            pltpu.VMEM(tile, F32),
            pltpu.VMEM(chem, F32),
            pltpu.VMEM(chem, F32),
            pltpu.VMEM(chem, F32),
            pltpu.VMEM(chem, F32),
            pltpu.SemaphoreType.DMA((len(given),)),
        ]
        + [pltpu.SemaphoreType.DMA((sides,))] * 4
        + [
            pltpu.VMEM((4, 4, 4, BLOCK), F32),
            pltpu.SemaphoreType.DMA((3,)),
            pltpu.SemaphoreType.DMA((3,)),
            pltpu.SemaphoreType.DMA,
            pltpu.SemaphoreType.DMA,
            pltpu.SemaphoreType.REGULAR,
        ],
        compiler_params=pltpu.CompilerParams(
            collective_id=0, has_side_effects=True, vmem_limit_bytes=24 << 20
        ),
        name="particle_step",
    )(*(pltpu.with_memory_space_constraint(x, pltpu.HBM) for x in given))
    density, accel, abund = pl.pallas_call(
        deliver,
        out_shape=(
            jax.ShapeDtypeStruct(tile, F32),
            jax.ShapeDtypeStruct(position.shape, F32),
            jax.ShapeDtypeStruct(species.shape, F32),
        ),
        in_specs=[vmem] * 3,
        out_specs=(hbm,) * 3,
        scratch_shapes=[pltpu.SemaphoreType.DMA((3,))],
        compiler_params=pltpu.CompilerParams(vmem_limit_bytes=1 << 20),
        name="deliver",
    )(density, accel, abund)
    return density.reshape(-1), accel, abund


def solution(mesh):
    flat = P(("dom", "sub"))
    wide = P(None, ("dom", "sub"))
    tall = P(("dom", "sub"), None)
    return jax.shard_map(
        on_device,
        mesh=mesh,
        in_specs=(wide, flat, flat, flat, wide, tall, tall, tall, P(), P(), flat, flat),
        out_specs=(flat, wide, wide),
        check_vma=False,
    )
```

```python
import functools

import jax
import jax.numpy as jnp
from jax import lax
from jax.experimental import pallas as pl
from jax.experimental.pallas import tpu as pltpu
from jax.sharding import PartitionSpec as P

BLOCK = 128
BLOCKS = 32
NBR = 4
SLOTS = 16
SPECIES = 12
S_LO = 4
SMAX = 32
HALF = BLOCKS * BLOCK // 2
FEAT = 48
GROUPS = 2
SPLIT = 24
FIRST = 32
MESH = pl.DeviceIdType.MESH
F32 = jnp.float32
BF16 = jnp.bfloat16
HIGH = lax.Precision.HIGHEST

gamma_gas = 5.0 / 3.0
chem_tau = 0.5


def pieces(value):
    high = value.astype(BF16).astype(F32)
    rest = value - high
    middle = rest.astype(BF16).astype(F32)
    return high, middle, rest - middle


def halves(value):
    high = value.astype(BF16)
    return high, (value - high.astype(F32)).astype(BF16)


def mm(a, b):
    return jnp.dot(a, b, preferred_element_type=F32)


def source_features(fields):
    high, middle, low = pieces(fields)
    return jnp.concatenate([high, high, high, middle, middle, low], 0).T.astype(BF16)


def weighted(place, weight):
    norm = jnp.sum(place * place, axis=0, keepdims=True)
    return jnp.concatenate(
        [place * weight, weight, norm * weight, jnp.zeros((3, BLOCK), F32)], 0
    )


def gradient_rows(fields, factor):
    row = lax.broadcasted_iota(jnp.int32, fields.shape, 0)
    both = jnp.where(row < 4, fields, pltpu.roll(fields, 4, 0))
    high, low = halves(both * jnp.where(row < 4, 1.0, factor))
    return jnp.concatenate([high, low], 0)


def distances(features, target, place):
    for k in range(0, len(features), 2):
        place[k // 2] = mm(jnp.concatenate(features[k : k + 2], 1), target)


def pair_terms(place, count, cubes, dens, row):
    total = None
    for k in range(count):
        for half in range(2):
            base = 1.0 / place[k, :, half * BLOCK : (half + 1) * BLOCK]
            squared = base * base
            at = (2 * k + half) * BLOCK
            cubes[at : at + BLOCK] = squared * base
            part = jnp.sum(squared.reshape(BLOCK // 8, 8, BLOCK), axis=0)
            total = part if total is None else total + part
    dens[pl.ds(row, 1)] = jnp.sum(total, axis=0, keepdims=True)


def pair_sums(rows, cubes):
    high, low = halves(cubes[...])
    lhs = jnp.concatenate(rows, 1)
    out = mm(lhs, high) + mm(lhs, low)
    return out[0:8] + out[8:16]


def spread(matrix):
    wide = 2 * SPECIES
    tall = jnp.concatenate([matrix, matrix], 0)
    full = jnp.concatenate([tall, tall], 1)
    same = (
        lax.broadcasted_iota(jnp.int32, (wide, wide), 0) // SPECIES
        == lax.broadcasted_iota(jnp.int32, (wide, wide), 1) // SPECIES
    )
    return jnp.where(same, full, 0.0)


def left_side(matrix):
    high, low = halves(matrix)
    blank = jnp.zeros((matrix.shape[0], 8), F32)
    high, low = high.astype(F32), low.astype(F32)
    return jnp.concatenate([high, blank, high, blank, low, blank], 1).astype(BF16)


def right_side(state):
    high, low = halves(jnp.concatenate([state, jnp.zeros((8, state.shape[1]), F32)], 0))
    return jnp.concatenate([high, low, high], 0)


def kernel(
    pos_in,
    width_in,
    mass_in,
    energy_in,
    species_in,
    neigh_in,
    exports_in,
    imports_in,
    jac_in,
    rates_in,
    steps_in,
    slot_in,
    density,
    accel,
    abund_all,
    pos,
    width,
    mass,
    energy,
    species,
    neigh,
    exports,
    imports,
    jac,
    rates,
    steps,
    slot,
    fields,
    targets,
    feats,
    far_feats,
    even,
    odd,
    far_ring,
    raw,
    stage,
    far_raw,
    far_fields,
    factor,
    stage_factor,
    far_factor,
    rows,
    far_rows,
    near_cubes,
    far_cubes,
    near_dens,
    far_dens,
    near_acc,
    far_acc,
    root_mass,
    gain,
    limit,
    state,
    rate_in,
    load_sem,
    send_one,
    recv_one,
    send_two,
    recv_two,
    relay,
    send_mate,
    recv_mate,
    send_wrap,
    recv_wrap,
    ready,
):
    dom = lax.axis_index("dom")
    sub = lax.axis_index("sub")
    doms = lax.axis_size("dom")
    subs = lax.axis_size("sub")
    sides = [lax.rem(dom + doms - 1, doms), lax.rem(dom + 1, doms)]
    barrier = pltpu.get_barrier_semaphore()
    last = doms - 1
    for q in range(subs):
        pl.semaphore_signal(barrier, inc=1, device_id=(sides[0], q), device_id_type=MESH)

    @pl.when(dom < last - 1)
    def _():
        for q in range(subs):
            pl.semaphore_signal(barrier, inc=1, device_id=(sides[1], q), device_id_type=MESH)

    mates = [lax.rem(sub + k, subs) for k in range(1, subs)]

    @pl.when(dom == 0)
    def _():
        for q in mates:
            pl.semaphore_signal(barrier, inc=1, device_id=(dom, q), device_id_type=MESH)

    @pl.when(dom == last)
    def _():
        pl.semaphore_wait(barrier, subs)
        pl.semaphore_signal(ready, inc=1, device_id=(sides[1], sub), device_id_type=MESH)


    pairs = {
        "pos": (pos_in, pos),
        "mass": (mass_in, mass),
        "imports": (imports_in, imports),
        "width": (width_in, width),
        "neigh": (neigh_in, neigh),
        "exports": (exports_in, exports),
        "jac": (jac_in, jac),
        "rates": (rates_in, rates),
        "energy": (energy_in, energy),
        "steps": (steps_in, steps),
        "slot": (slot_in, slot),
        "species": (species_in, species),
    }
    loads = {}
    for i, (name, (source, target)) in enumerate(pairs.items()):
        loads[name] = pltpu.make_async_copy(source, target, load_sem.at[i])
        loads[name].start()

    def exchange(sent, landed, send_sem, recv_sem):
        copies = []
        for e in range(2):
            for q in range(subs):
                copies.append(
                    pltpu.make_async_remote_copy(
                        src_ref=sent.at[e * subs + q],
                        dst_ref=landed.at[(1 - e) * subs + sub],
                        send_sem=send_sem.at[e * subs + q],
                        recv_sem=recv_sem.at[(1 - e) * subs + sub],
                        device_id=(sides[e], q),
                        device_id_type=MESH,
                    )
                )
        return copies

    def arrive(place, sent, landed, send_sem, recv_sem):
        pltpu.make_async_remote_copy(
            src_ref=sent.at[place],
            dst_ref=landed.at[place],
            send_sem=send_sem.at[place],
            recv_sem=recv_sem.at[place],
            device_id=(sides[0], 0),
            device_id_type=MESH,
        ).wait_recv()

    feats[...] = jnp.zeros_like(feats)
    targets[...] = jnp.zeros_like(targets)
    far_feats[...] = jnp.zeros_like(far_feats)
    loads["pos"].wait()
    loads["mass"].wait()
    root_mass[...] = 1.0 / jnp.sqrt(mass[...])

    def prepare(b, _):
        place = pos[:, pl.ds(pl.multiple_of(b * BLOCK, BLOCK), BLOCK)]
        raw[b, 0:3] = place
        raw[b, 3:4] = root_mass[pl.ds(b, 1)]
        return 0

    lax.fori_loop(0, BLOCKS, prepare, 0, unroll=8)
    loads["imports"].wait()
    for r in range(SLOTS):
        for k in range(2):
            stage[r // 2, (r % 2) * 2 + k] = raw[imports[k, r]]
    loads["width"].wait()
    loads["neigh"].wait()
    loads["exports"].wait()
    loads["jac"].wait()
    loads["rates"].wait()
    first = exchange(stage, far_raw, send_one, recv_one)
    relayed = [
        pltpu.make_async_remote_copy(
            src_ref=stage.at[q],
            dst_ref=relay.at[sub],
            send_sem=send_mate.at[k],
            recv_sem=recv_mate.at[k],
            device_id=(dom, q),
            device_id_type=MESH,
        )
        for k, q in enumerate(mates)
    ]
    wrapped = pltpu.make_async_remote_copy(
        src_ref=relay,
        dst_ref=far_raw.at[pl.ds(subs, subs)],
        send_sem=send_wrap,
        recv_sem=recv_wrap,
        device_id=(sides[0], sub),
        device_id_type=MESH,
    )

    @pl.when(dom != last)
    def _():
        pl.semaphore_wait(barrier, jnp.where(dom == 0, 2 * subs - 1, 2 * subs))

    @pl.when(dom == last - 1)
    def _():
        for q in range(subs):
            pl.semaphore_signal(ready, inc=1, device_id=(sides[1], q), device_id_type=MESH)

    for copy in first[subs:]:
        copy.start()

    @pl.when((dom != 0) & (dom != last))
    def _():
        for copy in first[:subs]:
            copy.start()

    @pl.when(dom == 0)
    def _():
        for copy in relayed:
            copy.start()
        relay[sub] = stage[sub]


    def shape_block(b):
        place = pos[:, pl.ds(pl.multiple_of(b * BLOCK, BLOCK), BLOCK)]
        norm = jnp.sum(place * place, axis=0, keepdims=True)
        span = width[pl.ds(b, 1)]
        target = jnp.concatenate(
            [place * -2.0, span * span + norm, jnp.ones_like(norm), jnp.zeros((3, BLOCK), F32)], 0
        )
        high, middle, low = pieces(target)
        split = jnp.concatenate([high, middle, low, high, middle, high], 0).astype(BF16)
        targets[b, 0:FEAT, 0:BLOCK] = split
        targets[b, BLOCK : BLOCK + FEAT, BLOCK : 2 * BLOCK] = split
        full = weighted(place, root_mass[pl.ds(b, 1)])
        fields[b] = full
        feats[b, :, 0:FEAT] = source_features(full)

    for b in range(FIRST):
        shape_block(b)
    jac_full = spread(jac[...])
    rate_full = spread(rates[...])
    both = jnp.dot(rates[...], jac[...], precision=HIGH, preferred_element_type=F32)
    left = left_side(jnp.concatenate([spread(both), jac_full], 0))
    left_first = left_side(rate_full)

    def fill(b, place):
        distances([feats[neigh[k, b]] for k in range(NBR)], targets[b], place)

    def drain(b, place):
        pair_terms(place, NBR // 2, near_cubes.at[b], near_dens, b)

    ring = [even.at[0], even.at[1], odd.at[0], odd.at[1]]
    fill(0, ring[0])
    fill(1, ring[1])
    for b in range(BLOCKS):
        if b + 2 < BLOCKS:
            fill(b + 2, ring[(b + 2) % 4])
        drain(b, ring[b % 4])
    for name in ("energy", "steps", "slot", "species"):
        loads[name].wait()

    @pl.when(dom == 0)
    def _():
        for k in range(subs - 1):
            pltpu.make_async_remote_copy(
                src_ref=stage.at[0],
                dst_ref=relay.at[lax.rem(sub + subs - 1 - k, subs)],
                send_sem=send_mate.at[k],
                recv_sem=recv_mate.at[k],
                device_id=(dom, mates[k]),
                device_id_type=MESH,
            ).wait_recv()
        pl.semaphore_wait(ready, 1)
        wrapped.start()

    @pl.when(dom == last)
    def _():
        pl.semaphore_wait(ready, subs)
        for copy in first[:subs]:
            copy.start()


    early = jnp.where(dom < doms // 2, 1, 0)
    order = []
    for e in (early, 1 - early):
        for d in (0, 1, 3, 2):
            order.append(e * subs + lax.rem(sub + d, subs))

    def far_fill(i):
        place = order[i]
        for k in range(4):
            full = weighted(far_raw[place, k, 0:3], far_raw[place, k, 3:4])
            far_fields[place, k] = full
            far_feats[i * 4 + k, :, 0:FEAT] = source_features(full)
        for x in range(2):
            parts = [far_feats[i * 4 + 2 * x + k] for k in range(2)]
            distances(parts, targets[exports[x, place]], far_ring.at[pl.ds(2 * i + x, 1)])

    def far_drain(i):
        for x in range(2):
            at = 2 * i + x
            pair_terms(far_ring.at[pl.ds(at, 1)], 1, far_cubes.at[at], far_dens, at)

    before = ()
    for group in ((0, 1, 2, 3), (4, 5), (6,), (7,)):
        if group[0] < subs:
            for i in group:
                arrive(order[i], stage, far_raw, send_one, recv_one)
        else:

            @pl.when(dom != last)
            def _():
                for i in group:
                    arrive(order[i], stage, far_raw, send_one, recv_one)

            if group[0] == subs:

                @pl.when(dom == last)
                def _():
                    wrapped.wait_recv()

        for i in group:
            far_fill(i)
        for i in before:
            far_drain(i)
        before = group
    for i in before:
        far_drain(i)

    owner = lax.broadcasted_iota(jnp.int32, (BLOCKS, BLOCK), 0)
    total = near_dens[...]
    for r in range(SLOTS):
        total += jnp.where(owner == exports[r % 2, order[r // 2]], far_dens[r : r + 1], 0.0)
    dens = total * width[...]
    density[...] = dens
    factor[...] = (gamma_gas - 1.0) * energy[...] / dens
    for r in range(SLOTS):
        for k in range(2):
            stage_factor[r // 2, pl.ds((r % 2) * 2 + k, 1)] = factor[pl.ds(imports[k, r], 1)]
    second = exchange(stage_factor, far_factor, send_two, recv_two)
    for copy in second[subs:] + second[:subs]:
        copy.start()
    gain_all = chem_tau * (dens / (dens + 1.0))
    most = jnp.where(slot[...] >= 0, steps[...], jnp.minimum(steps[...], S_LO)).astype(F32)
    for b in range(BLOCKS // 2):
        for h in range(2):
            block = b + h * (BLOCKS // 2)
            at = pl.ds(b * BLOCK, BLOCK)
            span = pl.ds(h * SPECIES, SPECIES)
            gain[span, at] = jnp.broadcast_to(gain_all[block : block + 1], (SPECIES, BLOCK))
            limit[span, at] = jnp.broadcast_to(most[block : block + 1], (SPECIES, BLOCK))
    state[0:SPECIES] = species[:, 0:HALF]
    state[SPECIES : 2 * SPECIES] = species[:, HALF : 2 * HALF]
    part = HALF // GROUPS
    for g in range(GROUPS):
        at = pl.ds(g * part, part)
        rate_in[:, at] = mm(left_first, right_side(state[:, at]))

    def rows_near(b, _):
        rows[b] = gradient_rows(fields[b], factor[pl.ds(b, 1)])
        return 0

    lax.fori_loop(0, BLOCKS, rows_near, 0, unroll=8)

    def chem_step(c):
        for g in range(GROUPS):
            at = pl.ds(g * part, part)
            abund = state[:, at]
            lift = gain[:, at]
            moved = (abund + lift) + lift * jnp.tanh(rate_in[:, at])
            out = mm(left, right_side(moved))
            rate_in[:, at] = out[: 2 * SPECIES]
            state[:, at] = jnp.where(limit[:, at] > c, out[2 * SPECIES :], abund)

    for c in range(SMAX // 2):
        chem_step(c)
        for b in (2 * c, 2 * c + 1):
            near_acc[b] = pair_sums([rows[neigh[k, b]] for k in range(NBR)], near_cubes.at[b])

    row = lax.broadcasted_iota(jnp.int32, (8, BLOCK), 0)
    lane = lax.broadcasted_iota(jnp.int32, (8, BLOCK), 1)
    named = jnp.zeros((8, BLOCK), jnp.int32)
    for r in range(SLOTS):
        named = jnp.where(lane // 8 == r, exports[r % 2, order[r // 2]], named)
    named = jnp.where(lane % 8 == row, named, -1)
    pick = jnp.concatenate(
        [jnp.where(named == b, 1.0, 0.0) for b in range(BLOCKS)], 0
    ).astype(BF16)
    for c in range(16, SPLIT):
        chem_step(c)

    def rows_far(group):
        for i in group:
            arrive(order[i], stage_factor, far_factor, send_two, recv_two)
        for i in group:
            place = order[i]
            for k in range(4):
                far_rows[i * 4 + k] = gradient_rows(
                    far_fields[place, k], far_factor[place, pl.ds(k, 1)]
                )

    def sums_far(i, x):
        at = 2 * i + x
        parts = [far_rows[i * 4 + 2 * x + k] for k in range(2)]
        far_acc[at] = pair_sums(parts, far_cubes.at[at])

    rows_far((0, 1, 2, 3))
    slots = [(i, x) for i in range(4) for x in range(2)]
    for c in range(SPLIT, SMAX):
        chem_step(c)
        n = 8 // (SMAX - SPLIT)
        for i, x in slots[(c - SPLIT) * n : (c - SPLIT + 1) * n]:
            sums_far(i, x)
    for group in ((4, 5), (6,), (7,)):
        rows_far(group)
        for i in group:
            for x in range(2):
                sums_far(i, x)
    high, low = halves(far_acc[...].reshape(SLOTS * 8, BLOCK))
    far_all = mm(jnp.concatenate([pick, pick], 1), jnp.concatenate([high, low], 0))
    for b in range(BLOCKS):
        acc = near_acc[b] + far_all[b * 8 : b * 8 + 8]
        acc = acc * jnp.where(row < 4, factor[b : b + 1], 1.0)
        acc = acc + pltpu.roll(acc, 4, 0)
        at = pl.ds(b * BLOCK, BLOCK)
        accel[:, at] = (4.0 * width[b : b + 1]) * (pos[:, at] * acc[3:4] - acc[0:3])
    abund_all[:, 0:HALF] = state[0:SPECIES]
    abund_all[:, HALF : 2 * HALF] = state[SPECIES : 2 * SPECIES]
    for copy in first[subs:] + second:
        copy.wait_send()

    @pl.when(dom != 0)
    def _():
        for copy in first[:subs]:
            copy.wait_send()

    @pl.when(dom == 0)
    def _():
        for copy in relayed + [wrapped]:
            copy.wait_send()


def deliver(density, accel, abund, dens_out, accel_out, abund_out, sems):
    pairs = ((abund, abund_out), (accel, accel_out), (density, dens_out))
    copies = [pltpu.make_async_copy(a, b, sems.at[i]) for i, (a, b) in enumerate(pairs)]
    for copy in copies:
        copy.start()
    for copy in copies:
        copy.wait()


def on_device(
    position,
    smoothing,
    mass,
    energy,
    species,
    neighbours,
    exports,
    imports,
    jac_inverse,
    rates,
    chem_steps,
    dense_slot,
):
    tile = (BLOCKS, BLOCK)
    vmem = pl.BlockSpec(memory_space=pltpu.VMEM)
    hbm = pl.BlockSpec(memory_space=pltpu.HBM)
    far = 2 * SLOTS
    sides = SLOTS // 2
    chem = (2 * SPECIES, HALF)
    given = (
        position,
        smoothing.reshape(tile),
        mass.reshape(tile),
        energy.reshape(tile),
        species,
        neighbours.T,
        exports.T,
        imports.T,
        jac_inverse,
        rates,
        chem_steps.reshape(tile),
        dense_slot.reshape(tile),
    )
    spaces = [pltpu.VMEM] * 5 + [pltpu.SMEM] * 3 + [pltpu.VMEM] * 4
    density, accel, abund = pl.pallas_call(
        kernel,
        out_shape=(
            pltpu.VMEM(tile, F32),
            pltpu.VMEM(position.shape, F32),
            pltpu.VMEM(species.shape, F32),
        ),
        in_specs=[hbm] * len(given),
        out_specs=(vmem, vmem, vmem),
        scratch_shapes=[space(x.shape, x.dtype) for space, x in zip(spaces, given)]
        + [
            pltpu.VMEM((BLOCKS, 8, BLOCK), F32),
            pltpu.VMEM((BLOCKS, 2 * BLOCK, 2 * BLOCK), BF16),
            pltpu.VMEM((BLOCKS, BLOCK, BLOCK), BF16),
            pltpu.VMEM((far, BLOCK, BLOCK), BF16),
            pltpu.VMEM((2, NBR // 2, BLOCK, 2 * BLOCK), F32),
            pltpu.VMEM((2, NBR // 2, BLOCK, 2 * BLOCK), F32),
            pltpu.VMEM((SLOTS, BLOCK, 2 * BLOCK), F32),
            pltpu.VMEM((BLOCKS, 4, BLOCK), F32),
            pltpu.VMEM((sides, 4, 4, BLOCK), F32),
            pltpu.VMEM((sides, 4, 4, BLOCK), F32),
            pltpu.VMEM((sides, 4, 8, BLOCK), F32),
            pltpu.VMEM(tile, F32),
            pltpu.VMEM((sides, 4, BLOCK), F32),
            pltpu.VMEM((sides, 4, BLOCK), F32),
            pltpu.VMEM((BLOCKS, 16, BLOCK), BF16),
            pltpu.VMEM((far, 16, BLOCK), BF16),
            pltpu.VMEM((BLOCKS, NBR * BLOCK, BLOCK), F32),
            pltpu.VMEM((SLOTS, 2 * BLOCK, BLOCK), F32),
            pltpu.VMEM(tile, F32),
            pltpu.VMEM((SLOTS, BLOCK), F32),
            pltpu.VMEM((BLOCKS, 8, BLOCK), F32),
            pltpu.VMEM((SLOTS, 8, BLOCK), F32),
            pltpu.VMEM(tile, F32),
            pltpu.VMEM(chem, F32),
            pltpu.VMEM(chem, F32),
            pltpu.VMEM(chem, F32),
            pltpu.VMEM(chem, F32),
            pltpu.SemaphoreType.DMA((len(given),)),
        ]
        + [pltpu.SemaphoreType.DMA((sides,))] * 4
        + [
            pltpu.VMEM((4, 4, 4, BLOCK), F32),
            pltpu.SemaphoreType.DMA((3,)),
            pltpu.SemaphoreType.DMA((3,)),
            pltpu.SemaphoreType.DMA,
            pltpu.SemaphoreType.DMA,
            pltpu.SemaphoreType.REGULAR,
        ],
        compiler_params=pltpu.CompilerParams(
            collective_id=0, has_side_effects=True, vmem_limit_bytes=24 << 20
        ),
        name="particle_step",
    )(*(pltpu.with_memory_space_constraint(x, pltpu.HBM) for x in given))
    density, accel, abund = pl.pallas_call(
        deliver,
        out_shape=(
            jax.ShapeDtypeStruct(tile, F32),
            jax.ShapeDtypeStruct(position.shape, F32),
            jax.ShapeDtypeStruct(species.shape, F32),
        ),
        in_specs=[vmem] * 3,
        out_specs=(hbm,) * 3,
        scratch_shapes=[pltpu.SemaphoreType.DMA((3,))],
        compiler_params=pltpu.CompilerParams(vmem_limit_bytes=1 << 20),
        name="deliver",
    )(density, accel, abund)
    return density.reshape(-1), accel, abund


def solution(mesh):
    flat = P(("dom", "sub"))
    wide = P(None, ("dom", "sub"))
    tall = P(("dom", "sub"), None)
    return jax.shard_map(
        on_device,
        mesh=mesh,
        in_specs=(wide, flat, flat, flat, wide, tall, tall, tall, P(), P(), flat, flat),
        out_specs=(flat, wide, wide),
        check_vma=False,
    )
```
